32 devices in a mesh: bag: 8 (over z, x), head: 4 (over y, core).
Axes of the slice: x: 2, y: 2, z: 4, core: 2. Of those that a mesh axis runs over, the one named last changes fastest.
Arguments:
- latents: bfloat16 [8, 8, 16, 16, 512], P('bag', 'head'), may hold values from -6 to 6
- frame_counts: int32 [8], P('bag'), may hold values from 4 to 8
- routes: int32 [4096, 1], P('bag'), may hold values from 0 to 7; in each aligned block of 128 rows (0 to 127, 128 to 255, ...) at most 24 rows name the same one
- samples: int32 [4096], P('bag'), may hold values from 0 to 3, as said below
- conv_weight: bfloat16 [27, 512, 128], replicated, may hold values from -0.0546875 to 0.0546875
- embed_weight: bfloat16 [512, 2048], replicated, may hold values from -0.25 to 0.25
- qkv_weight: bfloat16 [3, 2048, 2048], P(None, None, 'head')
Outputs:
- attended: bfloat16 [4096, 2048], P(('bag', 'head'))
The draws below stay inside these ranges and needn't reach their ends.
Inputs may be any that keep to these rules, and one draw needn't show every extreme that they name: `routes`: in each aligned block of 128 rows (the tokens of one device) no bag is named by more than 24 rows, a bound that some block reaches. `samples`: all tokens of one clip carry the same sample id, and every id occurs in some clip.
All inputs are finite; a program needn't handle non-finite values.
Results may differ from the reference program's by a relative error of at most 0.013.
Values may be sent and summed in bfloat16 or wider, within the bound.
No kernel may reach another device: no remote copies, remote signals or barrier semaphores. Data moves between devices by JAX's collectives and lax.ppermute only.
A program may use at most 128 MiB of HBM per device.

```python
import math
import jax
import jax.numpy as jnp
import numpy as np
from jax import lax

CIN = 512
COUT = 128
HEADS = 32
HDIM = 64
D = 2048
PF = 512
SAMPLES = 4
HT = 16
WT = 16
FRAMES = 8
CLIPS = 8
TOK_DEV = 128
TOKENS = 4096
CAP = 24
SLOTS = 768
N_BAG = 8


def draw_samples(key, part):
    clip_ids = jax.random.permutation(jax.random.fold_in(key, 11), CLIPS) % SAMPLES
    return jnp.repeat(clip_ids.astype(jnp.int32), TOKENS // CLIPS, total_repeat_length=TOKENS)


def draw_qkv_weight(key, part):
    base = jax.random.normal(key, (3, D, D), jnp.float32) * D ** (-0.5)
    return base.astype(jnp.bfloat16)


def plant(entries, own_key, least, largest):
    spot = [jax.random.randint(jax.random.fold_in(own_key, axis), (), 0, length) for axis, length in enumerate(entries.shape)]
    main_axis = entries.shape.index(max(entries.shape))
    neighbour = spot[:main_axis] + [(spot[main_axis] + 1) % entries.shape[main_axis]] + spot[main_axis + 1:]
    return entries.at[tuple(spot)].set(least).at[tuple(neighbour)].set(largest)


def shard_levels(own_key, dims, split, least, largest):
    factor_of, own = 1.0, jax.random.fold_in(own_key, 6)
    for axis_at, shards_of in split:
        steps = jnp.exp(jax.random.uniform(jax.random.fold_in(own, axis_at), (shards_of,), jnp.float32, least / len(split), largest / len(split)))
        factor_of = factor_of * jnp.repeat(steps, dims[axis_at] // shards_of).reshape([-1 if axis == axis_at else 1 for axis in range(len(dims))])
    return factor_of


def deal_out(own_key, own, number, rows, number_of, top, bound, slope):
    order = jax.random.permutation(own_key, number_of)
    packed, common = portions_of(number_of, rows * top, bound, slope, True), portions_of(number_of, rows * top, bound, slope, False)
    places = jnp.arange(number_of)

    def named(lengths, turn):
        used = int((lengths > 0).sum())
        fixed = max(1, used // 4)
        moved = fixed + (places - fixed + turn * (used - fixed)) % max(1, number_of - fixed)
        return jnp.zeros((number_of,), jnp.int32).at[order[jnp.where(places < fixed, places, moved)]].set(jnp.asarray(lengths, jnp.int32))

    lengths = jnp.where(number % 4 == 0, named(packed, number // 4), named(common, number - number // 4 - 1))
    mixed = jax.random.permutation(jax.random.fold_in(own, 3), number_of)
    donor, taker = mixed[0:number_of // 2 * 2:2], mixed[1:number_of // 2 * 2:2]
    room = jnp.minimum(lengths[donor] - 1, bound - lengths[taker]) // 2
    room = jnp.where((donor == order[0]) | (taker == order[0]) | (lengths[taker] == 0), 0, jnp.maximum(room, 0))
    moved = jax.random.randint(jax.random.fold_in(own, 4), (number_of // 2,), 0, 1 << 20) % (room + 1)
    lengths = lengths.at[donor].add(-moved).at[taker].add(moved)
    items = jnp.searchsorted(jnp.cumsum(lengths), jnp.arange(rows * top), side="right").astype(jnp.int32)
    table = items.reshape(top, rows).T
    table = table[jax.random.permutation(jax.random.fold_in(own, 1), rows)]
    turn = jax.random.randint(jax.random.fold_in(own, 2), (rows, 1), 0, top)
    return jnp.take_along_axis(table, (jnp.arange(top)[None, :] + turn) % top, axis=1)


def portions_of(number_of, total, reach, lean, full):
    portions = [(1 << 20) // math.isqrt(grade ** lean) + 1 for grade in range(1, number_of + 1)]
    largest = reach if full else min(reach, max(-(-total // number_of), total * portions[0] // sum(portions)))
    least = 1 if total - largest >= number_of - 1 else 0
    counts, surplus = [largest] + [least] * (number_of - 1), total - largest - least * (number_of - 1)
    while surplus > 0:
        free = [i for i in range(1, number_of) if counts[i] < largest] or [i for i in range(1, number_of) if counts[i] < reach]
        pool, left = sum([portions[i] for i in free]), surplus
        for i in free:
            extra = min(reach - counts[i], max(1, left * portions[i] // pool), surplus)
            counts[i] = counts[i] + extra
            surplus = surplus - extra
    return np.array(counts)


def bell_draw(own_key, extent, deviation, reach, shards=(), held_as=jnp.bfloat16):
    drawn = jax.random.normal(own_key, extent, jnp.float32) * deviation
    if len(shards) > 0:
        drawn = shard_levels(own_key, extent, shards, -0.22, 0.18) * drawn
    return jnp.clip(drawn, min=-reach, max=reach).astype(held_as)


def setup_inputs(seed: int = 0) -> dict:
    streams_of = jax.random.split(jax.random.key(seed), 8)
    latents = bell_draw(streams_of[0], (CLIPS, FRAMES, HT, WT, CIN), 1.0, 6.0, ((0, 8), (1, 4)))
    frame_counts = plant(jax.random.randint(streams_of[1], (CLIPS,), FRAMES // 2, FRAMES + 1), jax.random.fold_in(streams_of[1], 1), FRAMES // 2, FRAMES).astype(jnp.int32)
    routes_keys = jax.random.split(jax.random.fold_in(streams_of[2], 1), TOKENS // TOK_DEV)
    routes_turns = jax.random.permutation(jax.random.fold_in(streams_of[2], 3), TOKENS // TOK_DEV)
    routes = jax.vmap(lambda own, number: deal_out(jax.random.fold_in(streams_of[2], 2), own, number, TOK_DEV, N_BAG, 1, CAP, 2))(routes_keys, routes_turns).reshape((TOKENS, 1))
    samples = draw_samples(jax.random.fold_in(streams_of[7], 71), 0)
    conv_weight = bell_draw(streams_of[4], (27, CIN, COUT), (27 * CIN) ** -0.5, 0.0546875)
    embed_weight = bell_draw(streams_of[5], (PF, D), PF ** -0.5, 0.25)
    qkv_weight = draw_qkv_weight(jax.random.fold_in(streams_of[7], 71), 0)
    return dict(latents=latents, frame_counts=frame_counts, routes=routes, samples=samples, conv_weight=conv_weight, embed_weight=embed_weight, qkv_weight=qkv_weight)


epsilon = 1e-06
far_below = -1e+30

def patchify(latent_grid):
    frames_in, rows_in, cols_in, chans = latent_grid.shape
    shaped = latent_grid.reshape(frames_in, rows_in // 2, 2, cols_in // 2, 2, chans)
    return shaped.transpose(0, 1, 3, 2, 4, 5).reshape(frames_in * (rows_in // 2) * (cols_in // 2), 4 * chans)

def project(embedded, qkv_weight):
    widened = embedded.astype(jnp.float32)
    normed = (widened * lax.rsqrt(lax.optimization_barrier(jnp.mean(widened * widened, axis=-1, keepdims=True)) + epsilon)).astype(jnp.bfloat16)
    return jnp.einsum('rd,mdc->rmc', normed.astype(jnp.float32), qkv_weight.astype(jnp.float32)).astype(jnp.bfloat16)

def clip_rows(clip_latents, frame_count, conv_weight, embed_weight, qkv_weight):
    frame_live = jnp.arange(FRAMES, dtype=jnp.int32) < frame_count
    masked = clip_latents * frame_live[:, None, None, None].astype(jnp.bfloat16)
    padded = jnp.pad(masked, ((1, 1), (1, 1), (1, 1), (0, 0)))
    accumulated = jnp.zeros((FRAMES * HT * WT, COUT), jnp.float32)
    for offset_t in range(3):
        for offset_h in range(3):
            for offset_w in range(3):
                window = padded[offset_t:offset_t + FRAMES, offset_h:offset_h + HT, offset_w:offset_w + WT]
                accumulated = accumulated + jnp.dot(window.reshape(-1, CIN), conv_weight[9 * offset_t + 3 * offset_h + offset_w], preferred_element_type=jnp.float32)
    latent_grid = (accumulated.reshape(FRAMES, HT, WT, COUT) * frame_live[:, None, None, None].astype(jnp.float32)).astype(jnp.bfloat16)
    patches = patchify(latent_grid)
    embedded = jnp.dot(patches, embed_weight, preferred_element_type=jnp.float32).astype(jnp.bfloat16)
    return project(embedded, qkv_weight)

def bag_attention(rows, slot_labels):
    count_slots = rows.shape[0]
    queries = rows[:, 0].reshape(count_slots, HEADS, HDIM).transpose(1, 0, 2)
    key_rows = rows[:, 1].reshape(count_slots, HEADS, HDIM).transpose(1, 0, 2)
    value_rows = rows[:, 2].reshape(count_slots, HEADS, HDIM).transpose(1, 0, 2)
    admissible = (slot_labels[None, :] == slot_labels[:, None]) & (slot_labels[None, :] >= 0)

    def one_head(operands):
        query_head, key_head, value_head = operands
        scores = jnp.dot(query_head, key_head.T, preferred_element_type=jnp.float32) * HDIM ** (-0.5)
        scores = jnp.where(admissible, scores, far_below)
        shifted = jnp.exp(scores - lax.optimization_barrier(jnp.max(scores, axis=-1, keepdims=True)))
        weights = (shifted / lax.optimization_barrier(jnp.sum(shifted, axis=-1, keepdims=True))).astype(jnp.bfloat16)
        return jnp.dot(weights, value_head, preferred_element_type=jnp.float32).astype(jnp.bfloat16)
    outputs = lax.map(one_head, (queries, key_rows, value_rows))
    return outputs.transpose(1, 0, 2).reshape(count_slots, HEADS * HDIM)

def reference(latents, frame_counts, routes, samples, conv_weight, embed_weight, qkv_weight):

    def per_clip(operands):
        return clip_rows(operands[0], operands[1], conv_weight, embed_weight, qkv_weight)
    qkv = lax.map(per_clip, (latents, frame_counts)).reshape(TOKENS, 3, D)
    per_frame = HT // 2 * (WT // 2)
    per_clip_tokens = FRAMES * per_frame
    token_ids = jnp.arange(TOKENS, dtype=jnp.int32)
    frame_of = token_ids % per_clip_tokens // per_frame
    clip_of = token_ids // per_clip_tokens
    token_live = frame_of < frame_counts[clip_of]
    labels = jnp.where(token_live, samples, -1).astype(jnp.int32)
    route_flat = routes[:, 0]
    blocks = route_flat.reshape(-1, TOK_DEV)
    onehot = (blocks[:, :, None] == jnp.arange(N_BAG, dtype=jnp.int32)[None, None, :]).astype(jnp.int32)
    slot_rank = lax.optimization_barrier(jnp.sum((jnp.cumsum(onehot, axis=1) - onehot) * onehot, axis=2)).reshape(-1)
    position = (token_ids // TOK_DEV * CAP + slot_rank).astype(jnp.int32)
    members = jnp.full((N_BAG, SLOTS), TOKENS, jnp.int32).at[route_flat, position].set(token_ids)

    def one_bag(member_ids):
        filled = member_ids < TOKENS
        safe_ids = jnp.minimum(member_ids, TOKENS - 1)
        slot_labels = jnp.where(filled, labels[safe_ids], -1).astype(jnp.int32)
        return bag_attention(qkv[safe_ids], slot_labels)
    outputs = lax.map(one_bag, members)
    spread = jnp.zeros((TOKENS, D), jnp.bfloat16).at[members.reshape(-1)].set(outputs.reshape(-1, D), mode='drop')
    return jnp.where(token_live[:, None], spread, jnp.zeros((), jnp.bfloat16))
```

```python
import functools
import jax
import jax.numpy as jnp
from jax import lax
from jax.experimental import pallas as pl
from jax.experimental.pallas import tpu as pltpu
from jax.sharding import PartitionSpec as P

HDIM = 64
TAPS = 3

epsilon = 1e-06
far_below = -1e30

SMEM = pl.BlockSpec(memory_space=pltpu.SMEM)
VMEM = pl.BlockSpec(memory_space=pltpu.VMEM)


def slot_onehot(route_row, bags, cap, keep):
    tokens = route_row.shape[1]
    bag_ids = lax.broadcasted_iota(jnp.int32, (bags, tokens), 0)
    onehot = (bag_ids == route_row).astype(jnp.float32)
    before = (
        lax.broadcasted_iota(jnp.int32, (tokens, tokens), 0)
        < lax.broadcasted_iota(jnp.int32, (tokens, tokens), 1)
    )
    earlier = jnp.dot(
        onehot.astype(jnp.bfloat16),
        before.astype(jnp.float32).astype(jnp.bfloat16),
        preferred_element_type=jnp.float32,
    )
    rank = jnp.sum(earlier * onehot, axis=0, keepdims=True).astype(jnp.int32)
    slot = route_row * cap + rank
    if keep is not None:
        slot = jnp.where(keep, slot, -1)
    slot_ids = lax.broadcasted_iota(jnp.int32, (bags * cap, tokens), 0)
    return (slot_ids == slot).astype(jnp.float32).astype(jnp.bfloat16)


def conv_kernel(
    bags, cap, rows, cols, frames, scal_ref, x_ref, prev_ref, next_ref, w_ref, route_ref, out_ref, grid_ref
):
    count, place = scal_ref[0], scal_ref[1]
    area = rows * cols
    first = place * frames

    def live(frame):
        return jnp.logical_and(frame >= 0, frame < count)

    def masked(value, frame):
        return jnp.where(live(frame), value, jnp.zeros_like(value))

    inputs = [masked(prev_ref[...], first - 1)]
    for f in range(frames):
        inputs.append(masked(x_ref[f * area : (f + 1) * area, :], first + f))
    inputs.append(masked(next_ref[...], first + frames))
    stacked = jnp.concatenate(
        [jnp.concatenate(inputs[t : t + frames], axis=0) for t in range(TAPS)], axis=1
    )
    plane = TAPS * TAPS
    products = []
    for p in range(0, plane, 2):
        pair = [
            jnp.concatenate([w_ref[plane * t + q] for t in range(TAPS)], axis=0)
            for q in range(p, min(p + 2, plane))
        ]
        weight = pair[0] if len(pair) == 1 else jnp.concatenate(pair, axis=1)
        value = jnp.dot(stacked, weight, preferred_element_type=jnp.float32)
        chans = w_ref.shape[2]
        for q in range(len(pair)):
            products.append(value[:, q * chans : (q + 1) * chans].reshape(frames, rows, cols, chans))
    chans = w_ref.shape[2]
    blank = jnp.zeros((frames, 1, cols, chans), jnp.float32)
    column = lax.broadcasted_iota(jnp.int32, (frames * area, chans), 0) % cols
    total = None
    for e in range(TAPS):
        up, mid, down = products[e], products[TAPS + e], products[2 * TAPS + e]
        merged = (
            mid
            + jnp.concatenate([blank, up[:, : rows - 1]], axis=1)
            + jnp.concatenate([down[:, 1:], blank], axis=1)
        ).reshape(frames * area, chans)
        if e == 0:
            merged = jnp.where(column == 0, 0.0, pltpu.roll(merged, 1, axis=0))
        elif e == 2:
            merged = jnp.where(column == cols - 1, 0.0, pltpu.roll(merged, frames * area - 1, axis=0))
        total = merged if total is None else total + merged
    for f in range(frames):
        part = total[f * area : (f + 1) * area]
        grid_ref[f * area : (f + 1) * area, :] = jnp.where(live(first + f), part, 0.0)
    pieces = [[None] * 2 for _ in range(2)]
    for odd in range(2):
        half = grid_ref[pl.ds(odd, frames * area // 2, stride=2), :]
        half = half.reshape(frames * rows // 2, 2, cols // 2, chans)
        for i in range(2):
            pieces[i][odd] = half[:, i].reshape(frames * area // 4, chans)
    patches = jnp.concatenate(
        [pieces[0][0], pieces[0][1], pieces[1][0], pieces[1][1]], axis=1
    ).astype(jnp.bfloat16)
    route_row = route_ref[pl.ds(place, 1), :]
    onehot = slot_onehot(route_row, bags, cap, None)
    out_ref[...] = jnp.dot(onehot, patches, preferred_element_type=jnp.float32).astype(jnp.bfloat16)


def attention_kernel(heads, q_ref, k_ref, v_ref, lab_col_ref, lab_row_ref, out_ref, bias_ref):
    @pl.when(pl.program_id(1) == 0)
    def _():
        same = jnp.logical_and(lab_col_ref[...] == lab_row_ref[...], lab_row_ref[...] >= 0)
        bias_ref[...] = jnp.where(same, 0.0, far_below)

    outs = []
    for h in range(heads):
        cols = slice(h * HDIM, (h + 1) * HDIM)
        scores = lax.dot_general(
            q_ref[:, cols], k_ref[:, cols], (((1,), (1,)), ((), ())), preferred_element_type=jnp.float32
        )
        scores = scores * HDIM ** (-0.5) + bias_ref[...]
        top = jnp.max(scores, axis=-1, keepdims=True)
        shifted = jnp.exp(scores - top)
        norm = jnp.sum(shifted, axis=-1, keepdims=True)
        mixed = jnp.dot(shifted.astype(jnp.bfloat16), v_ref[:, cols], preferred_element_type=jnp.float32)
        outs.append(mixed / norm)
    out_ref[...] = jnp.concatenate(outs, axis=1).astype(jnp.bfloat16)


def collect_kernel(bags, cap, frames, heads, scal_ref, recv_ref, route_ref, out_ref):
    count, place = scal_ref[0], scal_ref[1]
    route_row = route_ref[pl.ds(place, 1), :]
    tokens = route_row.shape[1]
    per_frame = tokens // frames
    frame = place * frames + lax.broadcasted_iota(jnp.int32, (1, tokens), 1) // per_frame
    onehot = slot_onehot(route_row, bags, cap, frame < count)
    slots = bags * cap
    width = recv_ref.shape[1]
    for h in range(heads):
        picked = lax.dot_general(
            onehot,
            recv_ref[h * slots : (h + 1) * slots, :],
            (((0,), (0,)), ((), ())),
            preferred_element_type=jnp.float32,
        )
        out_ref[:, h * width : (h + 1) * width] = picked.astype(jnp.bfloat16)


def shards(latents, frame_counts, routes, samples, conv_weight, embed_weight, qkv_weight):
    frames_dev, rows, cols, depth = latents.shape[1:]
    heads_dev = lax.axis_size("head")
    bags = lax.axis_size("bag")
    place = lax.axis_index("head")
    frame_count = frame_counts[0]
    area = rows * cols
    tok_dev = frames_dev * area // 4
    cap = 3 * tok_dev // (2 * bags)
    slots = bags * cap
    local_width = qkv_weight.shape[2]
    chans = conv_weight.shape[2]

    tile = latents.reshape(frames_dev, area, depth)
    ends = heads_dev - 1
    prev_frame = lax.ppermute(tile[frames_dev - 1], "head", [(i, i + 1) for i in range(ends)])
    next_frame = lax.ppermute(tile[0], "head", [(i + 1, i) for i in range(ends)])

    route_rows = routes[:, 0].reshape(heads_dev, tok_dev)
    per_frame = tok_dev // frames_dev
    token_frame = (
        jnp.arange(heads_dev, dtype=jnp.int32)[:, None] * frames_dev
        + (jnp.arange(tok_dev, dtype=jnp.int32) // per_frame)[None, :]
    )
    token_live = token_frame < frame_count
    bag_ids = jnp.arange(bags, dtype=jnp.int32)
    counts = jnp.sum(
        ((route_rows[None] == bag_ids[:, None, None]) & token_live[None]).astype(jnp.int32), axis=2
    )
    notes = jnp.concatenate(
        [counts, jnp.broadcast_to(samples[:1][None, :], (bags, heads_dev))], axis=1
    )
    notes = lax.all_to_all(notes, "bag", split_axis=0, concat_axis=0, tiled=True)

    scal = jnp.stack([frame_count, place.astype(jnp.int32)])
    outgoing = pl.pallas_call(
        functools.partial(conv_kernel, bags, cap, rows, cols, frames_dev),
        out_shape=jax.ShapeDtypeStruct((slots, 4 * chans), jnp.bfloat16),
        in_specs=[SMEM, VMEM, VMEM, VMEM, VMEM, VMEM],
        out_specs=VMEM,
        scratch_shapes=[pltpu.VMEM((frames_dev * area, chans), jnp.float32)],
        name="conv",
    )(scal, tile.reshape(frames_dev * area, depth), prev_frame, next_frame, conv_weight, route_rows)

    arrived = lax.all_to_all(
        outgoing.reshape(bags, cap, 4 * chans), "bag", split_axis=0, concat_axis=0, tiled=True
    ).reshape(slots, 4 * chans)
    patches = lax.all_gather(arrived, "head", axis=0, tiled=True)

    embedded = jnp.dot(patches, embed_weight, preferred_element_type=jnp.float32).astype(jnp.bfloat16)
    widened = embedded.astype(jnp.float32)
    normed = (
        widened * lax.rsqrt(jnp.mean(widened * widened, axis=-1, keepdims=True) + epsilon)
    ).astype(jnp.bfloat16)
    count_slots = heads_dev * slots
    query, key, value = [
        jnp.dot(normed, qkv_weight[m], preferred_element_type=jnp.float32).astype(jnp.bfloat16)
        for m in range(3)
    ]

    live_count = notes[:, :heads_dev].T
    labels = jnp.where(
        jnp.arange(cap, dtype=jnp.int32)[None, None, :] < live_count[:, :, None],
        notes[:, heads_dev][None, :, None],
        -1,
    ).reshape(count_slots)

    pair = 2
    wide = pair * HDIM
    q_tile = 256
    attended = pl.pallas_call(
        functools.partial(attention_kernel, pair),
        out_shape=jax.ShapeDtypeStruct((count_slots, local_width), jnp.bfloat16),
        grid=(count_slots // q_tile, local_width // wide),
        in_specs=[
            pl.BlockSpec((q_tile, wide), lambda i, h: (i, h)),
            pl.BlockSpec((count_slots, wide), lambda i, h: (0, h)),
            pl.BlockSpec((count_slots, wide), lambda i, h: (0, h)),
            pl.BlockSpec((q_tile, 1), lambda i, h: (i, 0)),
            pl.BlockSpec((1, count_slots), lambda i, h: (0, 0)),
        ],
        out_specs=pl.BlockSpec((q_tile, wide), lambda i, h: (i, h)),
        scratch_shapes=[pltpu.VMEM((q_tile, count_slots), jnp.float32)],
        name="attention",
    )(query, key, value, labels.reshape(count_slots, 1), labels.reshape(1, count_slots))

    returned = lax.all_to_all(
        attended.reshape(heads_dev * bags, cap, local_width),
        ("head", "bag"),
        split_axis=0,
        concat_axis=0,
        tiled=True,
    ).reshape(count_slots, local_width)
    return pl.pallas_call(
        functools.partial(collect_kernel, bags, cap, frames_dev, heads_dev),
        out_shape=jax.ShapeDtypeStruct((tok_dev, heads_dev * local_width), jnp.bfloat16),
        in_specs=[SMEM, VMEM, VMEM],
        out_specs=VMEM,
        name="collect",
    )(scal, returned, route_rows)


def solution(mesh):
    placed = (
        P("bag", "head", None, None, None),
        P("bag"),
        P("bag", None),
        P("bag"),
        P(),
        P(),
        P(None, None, "head"),
    )
    return jax.shard_map(
        shards, mesh=mesh, in_specs=placed, out_specs=P(("bag", "head"), None), check_vma=False
    )
```

```python
import functools
import jax
import jax.numpy as jnp
from jax import lax
from jax.experimental import pallas as pl
from jax.experimental.pallas import tpu as pltpu
from jax.sharding import PartitionSpec as P

HDIM = 64
TAPS = 3
SAMPLES = 4
LANES = 128

epsilon = 1e-06
far_below = -1e30

SMEM = pl.BlockSpec(memory_space=pltpu.SMEM)
VMEM = pl.BlockSpec(memory_space=pltpu.VMEM)


def slot_of(route_row, bags, cap, stride):
    tokens = route_row.shape[1]
    bag_ids = lax.broadcasted_iota(jnp.int32, (bags, tokens), 0)
    onehot = (bag_ids == route_row).astype(jnp.float32)
    before = (
        lax.broadcasted_iota(jnp.int32, (tokens, tokens), 0)
        < lax.broadcasted_iota(jnp.int32, (tokens, tokens), 1)
    )
    earlier = jnp.dot(
        onehot.astype(jnp.bfloat16),
        before.astype(jnp.float32).astype(jnp.bfloat16),
        preferred_element_type=jnp.float32,
    )
    rank = jnp.sum(earlier * onehot, axis=0, keepdims=True).astype(jnp.int32)
    return route_row * stride + rank


def onehot_of(slot, slots):
    slot_ids = lax.broadcasted_iota(jnp.int32, (slots, slot.shape[1]), 0)
    return (slot_ids == slot).astype(jnp.float32).astype(jnp.bfloat16)


def conv_kernel(
    bags, cap, rows, cols, frames, scal_ref, x_ref, prev_ref, next_ref, w_ref, route_ref, out_ref, grid_ref
):
    count, place, sample = scal_ref[0], scal_ref[1], scal_ref[2]
    area = rows * cols
    first = place * frames

    def live(frame):
        return jnp.logical_and(frame >= 0, frame < count)

    def masked(value, frame):
        return jnp.where(live(frame), value, jnp.zeros_like(value))

    inputs = [masked(prev_ref[...], first - 1)]
    for f in range(frames):
        inputs.append(masked(x_ref[f * area : (f + 1) * area, :], first + f))
    inputs.append(masked(next_ref[...], first + frames))
    stacked = jnp.concatenate(
        [jnp.concatenate(inputs[t : t + frames], axis=0) for t in range(TAPS)], axis=1
    )
    plane = TAPS * TAPS
    products = []
    for p in range(0, plane, 2):
        pair = [
            jnp.concatenate([w_ref[plane * t + q] for t in range(TAPS)], axis=0)
            for q in range(p, min(p + 2, plane))
        ]
        weight = pair[0] if len(pair) == 1 else jnp.concatenate(pair, axis=1)
        value = jnp.dot(stacked, weight, preferred_element_type=jnp.float32)
        chans = w_ref.shape[2]
        for q in range(len(pair)):
            products.append(value[:, q * chans : (q + 1) * chans].reshape(frames, rows, cols, chans))
    chans = w_ref.shape[2]
    blank = jnp.zeros((frames, 1, cols, chans), jnp.float32)
    column = lax.broadcasted_iota(jnp.int32, (frames * area, chans), 0) % cols
    total = None
    for e in range(TAPS):
        up, mid, down = products[e], products[TAPS + e], products[2 * TAPS + e]
        merged = (
            mid
            + jnp.concatenate([blank, up[:, : rows - 1]], axis=1)
            + jnp.concatenate([down[:, 1:], blank], axis=1)
        ).reshape(frames * area, chans)
        if e == 0:
            merged = jnp.where(column == 0, 0.0, pltpu.roll(merged, 1, axis=0))
        elif e == 2:
            merged = jnp.where(column == cols - 1, 0.0, pltpu.roll(merged, frames * area - 1, axis=0))
        total = merged if total is None else total + merged
    for f in range(frames):
        part = total[f * area : (f + 1) * area]
        grid_ref[f * area : (f + 1) * area, :] = jnp.where(live(first + f), part, 0.0)
    pieces = [[None] * 2 for _ in range(2)]
    for odd in range(2):
        half = grid_ref[pl.ds(odd, frames * area // 2, stride=2), :]
        half = half.reshape(frames * rows // 2, 2, cols // 2, chans)
        for i in range(2):
            pieces[i][odd] = half[:, i].reshape(frames * area // 4, chans)
    tokens = frames * area // 4
    frame = first + lax.broadcasted_iota(jnp.int32, (tokens, LANES), 0) // (area // 4)
    label = jnp.where(frame < count, sample + 1, 0).astype(jnp.float32)
    patches = jnp.concatenate(
        [pieces[0][0], pieces[0][1], pieces[1][0], pieces[1][1], label], axis=1
    ).astype(jnp.bfloat16)
    route_row = route_ref[pl.ds(place, 1), :]
    onehot = onehot_of(slot_of(route_row, bags, cap, cap), bags * cap)
    out_ref[...] = jnp.dot(onehot, patches, preferred_element_type=jnp.float32).astype(jnp.bfloat16)


def bag_kernel(
    clips, x_ref, e_hbm, w_hbm, out_ref, e_ref, w_ref, normed_ref, qkv_ref, m_ref, r_ref, order_ref, sems
):
    count_slots = x_ref.shape[0]
    feats = e_ref.shape[0]
    model = e_ref.shape[1]
    width = w_ref.shape[2]
    clip_rows = count_slots // clips
    copies = [pltpu.make_async_copy(e_hbm, e_ref, sems.at[0])]
    for m in range(3):
        copies.append(pltpu.make_async_copy(w_hbm.at[m], w_ref.at[m], sems.at[1 + m]))
    for copy in copies:
        copy.start()

    for c in range(clips):
        note = x_ref[c * clip_rows : (c + 1) * clip_rows, feats : feats + LANES].astype(jnp.float32)
        order_ref[clips + c] = jnp.max(note).astype(jnp.int32)
    starts = [jnp.int32(0)]
    for s in range(SAMPLES):

        def keep_clip(c, at):
            hit = order_ref[clips + c] == s + 1

            @pl.when(hit)
            def _():
                order_ref[at] = c

            return at + hit.astype(jnp.int32)

        starts.append(lax.fori_loop(0, clips, keep_clip, starts[-1]))

    row_tile = 256
    copies[0].wait()

    def embed(i, carry):
        at = pl.multiple_of(i * row_tile, row_tile)
        rows = pl.ds(at, row_tile)
        patch = x_ref[rows, :feats]
        total = jnp.zeros((row_tile, 1), jnp.float32)
        step = 512
        for n in range(0, model, step):
            part = jnp.dot(patch, e_ref[:, n : n + step], preferred_element_type=jnp.float32).astype(
                jnp.bfloat16
            )
            normed_ref[rows, n : n + step] = part
            wide = part.astype(jnp.float32)
            total = total + jnp.sum(wide * wide, axis=-1, keepdims=True)
        scale = lax.rsqrt(total * (1.0 / model) + epsilon)
        for n in range(0, model, step):
            wide = normed_ref[rows, n : n + step].astype(jnp.float32)
            normed_ref[rows, n : n + step] = (wide * scale).astype(jnp.bfloat16)
        return carry

    lax.fori_loop(0, count_slots // row_tile, embed, 0)

    col_tile = 256
    for m in range(3):
        copies[1 + m].wait()
        for n in range(0, width, col_tile):
            part = jnp.dot(
                normed_ref[...], w_ref[m, :, n : n + col_tile], preferred_element_type=jnp.float32
            ).astype(jnp.bfloat16)
            if m == 0:
                part = part * jnp.bfloat16(HDIM ** (-0.5))
            qkv_ref[m, :, n : n + col_tile] = part

    out_ref[...] = jnp.zeros_like(out_ref)
    tile = 2 * clip_rows
    lane = lax.broadcasted_iota(jnp.int32, (tile, LANES), 1)
    low = lane < HDIM
    pairs = width // LANES
    ones = jnp.ones((tile, LANES), jnp.bfloat16)
    pick = (lax.broadcasted_iota(jnp.int32, (8, LANES), 1) == 0).astype(jnp.float32).astype(jnp.bfloat16)
    key_at = lax.broadcasted_iota(jnp.int32, (1, tile), 1)

    def two(ref, a, b, *at):
        return jnp.concatenate(
            [
                ref[(*at[:-1], pl.ds(pl.multiple_of(a * clip_rows, 16), clip_rows), at[-1])],
                ref[(*at[:-1], pl.ds(pl.multiple_of(b * clip_rows, 16), clip_rows), at[-1])],
            ],
            axis=0,
        )

    for s in range(SAMPLES):
        begin, size = starts[s], starts[s + 1] - starts[s]
        tiles = (size + 1) // 2

        def members(i):
            second = 2 * i + 1 < size
            return (
                order_ref[begin + 2 * i],
                order_ref[begin + 2 * i + second.astype(jnp.int32)],
                second,
            )

        def bias_of(a, b, second):
            label = lax.dot_general(
                pick,
                two(x_ref, a, b, slice(feats, feats + LANES)),
                (((1,), (1,)), ((), ())),
                preferred_element_type=jnp.float32,
            )[:1]
            limit = jnp.where(second, tile, clip_rows)
            good = jnp.logical_and(label == s + 1.0, key_at < limit)
            return jnp.where(good, 0.0, far_below)

        def scores_of(pair, half, query, a, b, bias):
            cols = slice(pair * LANES, (pair + 1) * LANES)
            keys = two(qkv_ref, a, b, 1, cols)
            one = jnp.where(low if half == 0 else jnp.logical_not(low), query, jnp.zeros_like(query))
            return (
                lax.dot_general(one, keys, (((1,), (1,)), ((), ())), preferred_element_type=jnp.float32)
                + bias
            )

        def mix(pair, shifted, a, b):
            cols = slice(pair * LANES, (pair + 1) * LANES)
            values = jnp.concatenate([two(qkv_ref, a, b, 2, cols), ones], axis=1)
            return jnp.dot(shifted.astype(jnp.bfloat16), values, preferred_element_type=jnp.float32)

        def store(pair, a, b, results):
            cols = slice(pair * LANES, (pair + 1) * LANES)
            heads = [r[:, :LANES] / r[:, LANES:] for r in results]
            mixed = jnp.where(low, heads[0], heads[1]).astype(jnp.bfloat16)
            out_ref[pl.ds(pl.multiple_of(b * clip_rows, 16), clip_rows), cols] = mixed[clip_rows:]
            out_ref[pl.ds(pl.multiple_of(a * clip_rows, 16), clip_rows), cols] = mixed[:clip_rows]

        def query_tile(i, carry):
            qa, qb, _ = members(i)

            @pl.when(tiles == 1)
            def _():
                ka, kb, second = members(0)
                bias = bias_of(ka, kb, second)
                for pair in range(pairs):
                    query = two(qkv_ref, qa, qb, 0, slice(pair * LANES, (pair + 1) * LANES))
                    results = []
                    for half in range(2):
                        scores = scores_of(pair, half, query, ka, kb, bias)
                        top = jnp.max(scores, axis=-1, keepdims=True)
                        results.append(mix(pair, jnp.exp(scores - top), ka, kb))
                    store(pair, qa, qb, results)

            @pl.when(tiles > 1)
            def _():
                for h in range(2 * pairs):
                    m_ref[h] = jnp.full((tile, LANES), far_below, jnp.float32)
                    r_ref[h] = jnp.zeros((tile, 2 * LANES), jnp.float32)

                def key_tile(j, inner):
                    ka, kb, second = members(j)
                    bias = bias_of(ka, kb, second)
                    for pair in range(pairs):
                        query = two(qkv_ref, qa, qb, 0, slice(pair * LANES, (pair + 1) * LANES))
                        for half in range(2):
                            h = 2 * pair + half
                            scores = scores_of(pair, half, query, ka, kb, bias)
                            old = m_ref[h][:, :1]
                            top = jnp.maximum(old, jnp.max(scores, axis=-1, keepdims=True))
                            r_ref[h] = r_ref[h] * jnp.exp(old - top) + mix(
                                pair, jnp.exp(scores - top), ka, kb
                            )
                            m_ref[h] = jnp.broadcast_to(top, (tile, LANES))
                    return inner

                lax.fori_loop(0, tiles, key_tile, 0)
                for pair in range(pairs):
                    store(pair, qa, qb, [r_ref[2 * pair], r_ref[2 * pair + 1]])

            return carry

        lax.fori_loop(0, tiles, query_tile, 0)


def collect_kernel(bags, cap, frames, heads, scal_ref, recv_ref, route_ref, out_ref):
    count, place = scal_ref[0], scal_ref[1]
    route_row = route_ref[pl.ds(place, 1), :]
    tokens = route_row.shape[1]
    per_frame = tokens // frames
    frame = place * frames + lax.broadcasted_iota(jnp.int32, (1, tokens), 1) // per_frame
    slot = slot_of(route_row, bags, cap, heads * cap)
    width = recv_ref.shape[1]
    for h in range(heads):
        onehot = onehot_of(jnp.where(frame < count, slot + h * cap, -1), recv_ref.shape[0])
        picked = lax.dot_general(
            onehot,
            recv_ref[...],
            (((0,), (0,)), ((), ())),
            preferred_element_type=jnp.float32,
        )
        out_ref[:, h * width : (h + 1) * width] = picked.astype(jnp.bfloat16)


def shards(latents, frame_counts, routes, samples, conv_weight, embed_weight, qkv_weight):
    frames_dev, rows, cols, depth = latents.shape[1:]
    heads_dev = lax.axis_size("head")
    bags = lax.axis_size("bag")
    place = lax.axis_index("head")
    frame_count = frame_counts[0]
    area = rows * cols
    tok_dev = frames_dev * area // 4
    cap = 3 * tok_dev // (2 * bags)
    slots = bags * cap
    local_width = qkv_weight.shape[2]
    chans = conv_weight.shape[2]

    tile = latents.reshape(frames_dev, area, depth)
    ends = heads_dev - 1
    prev_frame = lax.ppermute(tile[frames_dev - 1], "head", [(i, i + 1) for i in range(ends)])
    next_frame = lax.ppermute(tile[0], "head", [(i + 1, i) for i in range(ends)])

    route_rows = routes[:, 0].reshape(heads_dev, tok_dev)
    scal = jnp.stack([frame_count, place.astype(jnp.int32), samples[0]])
    row_width = 4 * chans + LANES
    outgoing = pl.pallas_call(
        functools.partial(conv_kernel, bags, cap, rows, cols, frames_dev),
        out_shape=jax.ShapeDtypeStruct((slots, row_width), jnp.bfloat16),
        in_specs=[SMEM, VMEM, VMEM, VMEM, VMEM, VMEM],
        out_specs=VMEM,
        scratch_shapes=[pltpu.VMEM((frames_dev * area, chans), jnp.float32)],
        name="conv",
    )(scal, tile.reshape(frames_dev * area, depth), prev_frame, next_frame, conv_weight, route_rows)

    arrived = lax.all_to_all(
        outgoing.reshape(bags, cap, row_width), "bag", split_axis=0, concat_axis=0, tiled=True
    )
    count_slots = heads_dev * slots
    gathered = lax.all_gather(arrived, "head", axis=1, tiled=True).reshape(count_slots, row_width)

    pair_rows = 2 * heads_dev * cap
    heads_here = local_width // HDIM
    attended = pl.pallas_call(
        functools.partial(bag_kernel, bags),
        out_shape=jax.ShapeDtypeStruct((count_slots, local_width), jnp.bfloat16),
        in_specs=[VMEM, pl.BlockSpec(memory_space=pl.ANY), pl.BlockSpec(memory_space=pl.ANY)],
        out_specs=VMEM,
        scratch_shapes=[
            pltpu.VMEM(embed_weight.shape, jnp.bfloat16),
            pltpu.VMEM(qkv_weight.shape, jnp.bfloat16),
            pltpu.VMEM((count_slots, embed_weight.shape[1]), jnp.bfloat16),
            pltpu.VMEM((3, count_slots, local_width), jnp.bfloat16),
            pltpu.VMEM((heads_here, pair_rows, LANES), jnp.float32),
            pltpu.VMEM((heads_here, pair_rows, 2 * LANES), jnp.float32),
            pltpu.SMEM((2 * bags,), jnp.int32),
            pltpu.SemaphoreType.DMA((4,)),
        ],
        name="bag",
    )(gathered, embed_weight, qkv_weight)

    returned = lax.all_to_all(
        attended.reshape(heads_dev * bags, cap, local_width),
        ("bag", "head"),
        split_axis=0,
        concat_axis=0,
        tiled=True,
    ).reshape(count_slots, local_width)
    return pl.pallas_call(
        functools.partial(collect_kernel, bags, cap, frames_dev, heads_dev),
        out_shape=jax.ShapeDtypeStruct((tok_dev, heads_dev * local_width), jnp.bfloat16),
        in_specs=[SMEM, VMEM, VMEM],
        out_specs=VMEM,
        name="collect",
    )(scal, returned, route_rows)


def solution(mesh):
    placed = (
        P("bag", "head", None, None, None),
        P("bag"),
        P("bag", None),
        P("bag"),
        P(),
        P(),
        P(None, None, "head"),
    )
    return jax.shard_map(
        shards, mesh=mesh, in_specs=placed, out_specs=P(("bag", "head"), None), check_vma=False
    )
```

```python
import functools
import jax
import jax.numpy as jnp
from jax import lax
from jax.experimental import pallas as pl
from jax.experimental.pallas import tpu as pltpu
from jax.sharding import PartitionSpec as P

HDIM = 64
TAPS = 3
SAMPLES = 4
LANES = 128

epsilon = 1e-06
far_below = -1e30

SMEM = pl.BlockSpec(memory_space=pltpu.SMEM)
VMEM = pl.BlockSpec(memory_space=pltpu.VMEM)
CHUNKS = 2


def limit(mib):
    return pltpu.CompilerParams(vmem_limit_bytes=mib << 20)


def slot_of(route_row, bags, cap, stride):
    tokens = route_row.shape[1]
    bag_ids = lax.broadcasted_iota(jnp.int32, (bags, tokens), 0)
    onehot = (bag_ids == route_row).astype(jnp.float32)
    before = (
        lax.broadcasted_iota(jnp.int32, (tokens, tokens), 0)
        < lax.broadcasted_iota(jnp.int32, (tokens, tokens), 1)
    )
    earlier = jnp.dot(
        onehot.astype(jnp.bfloat16),
        before.astype(jnp.float32).astype(jnp.bfloat16),
        preferred_element_type=jnp.float32,
    )
    rank = jnp.sum(earlier * onehot, axis=0, keepdims=True).astype(jnp.int32)
    return route_row * stride + rank


def onehot_of(slot, slots):
    slot_ids = lax.broadcasted_iota(jnp.int32, (slots, slot.shape[1]), 0)
    return (slot_ids == slot).astype(jnp.float32).astype(jnp.bfloat16)


def combine(products, rows, cols):
    chans = products[0].shape[1]
    blank = jnp.zeros((cols, chans), jnp.float32)
    area = rows * cols
    column = lax.broadcasted_iota(jnp.int32, (area, chans), 0) % cols
    total = None
    for e in range(TAPS):
        up, mid, down = products[e], products[TAPS + e], products[2 * TAPS + e]
        merged = (
            mid
            + jnp.concatenate([blank, up[: area - cols]], axis=0)
            + jnp.concatenate([down[cols:], blank], axis=0)
        )
        if e == 0:
            merged = jnp.where(column == 0, 0.0, pltpu.roll(merged, 1, axis=0))
        elif e == 2:
            merged = jnp.where(column == cols - 1, 0.0, pltpu.roll(merged, area - 1, axis=0))
        total = merged if total is None else total + merged
    return total


def plane_products(pieces, w_ref):
    plane = TAPS * TAPS
    chans = w_ref.shape[2]
    stacked = pieces[0][1] if len(pieces) == 1 else jnp.concatenate([x for _, x in pieces], axis=1)
    products = []
    for p in range(0, plane, 2):
        pair = []
        for q in range(p, min(p + 2, plane)):
            taps = [w_ref[plane * t + q] for t, _ in pieces]
            pair.append(taps[0] if len(taps) == 1 else jnp.concatenate(taps, axis=0))
        weight = pair[0] if len(pair) == 1 else jnp.concatenate(pair, axis=1)
        value = jnp.dot(stacked, weight, preferred_element_type=jnp.float32)
        for q in range(len(pair)):
            products.append(value[:, q * chans : (q + 1) * chans])
    return products


def own_kernel(bags, cap, rows, cols, frames, count_ref, x_ref, w_ref, route_ref, acc_ref, onehot_ref):
    count = count_ref[0]
    place = lax.axis_index("head")
    area = rows * cols
    first = place * frames
    inputs = []
    for f in range(frames):
        value = x_ref[f * area : (f + 1) * area, :]
        inputs.append(jnp.where(first + f < count, value, jnp.zeros_like(value)))
    for f in range(frames):
        pieces = [(t, inputs[f + t - 1]) for t in range(TAPS) if 0 <= f + t - 1 < frames]
        acc_ref[f * area : (f + 1) * area, :] = combine(plane_products(pieces, w_ref), rows, cols)
    route_row = route_ref[pl.ds(place, 1), :]
    onehot_ref[...] = onehot_of(slot_of(route_row, bags, cap, cap), bags * cap)


def halo_kernel(
    rows, cols, frames, count_ref, sample_ref, acc_ref, prev_ref, next_ref, w_ref, onehot_ref, out_ref, grid_ref
):
    count = count_ref[0]
    sample = sample_ref[0]
    place = lax.axis_index("head")
    area = rows * cols
    first = place * frames
    chans = w_ref.shape[2]

    def masked(value, frame):
        live = jnp.logical_and(frame >= 0, frame < count)
        return jnp.where(live, value, jnp.zeros_like(value))

    for f in range(frames):
        part = acc_ref[f * area : (f + 1) * area, :]
        pieces = []
        if f == 0:
            pieces.append((0, masked(prev_ref[...], first - 1)))
        if f == frames - 1:
            pieces.append((2, masked(next_ref[...], first + frames)))
        if pieces:
            part = part + combine(plane_products(pieces, w_ref), rows, cols)
        grid_ref[f * area : (f + 1) * area, :] = jnp.where(first + f < count, part, 0.0)
    pieces = [[None] * 2 for _ in range(2)]
    for odd in range(2):
        half = grid_ref[pl.ds(odd, frames * area // 2, stride=2), :]
        half = half.reshape(frames * rows // 2, 2, cols // 2, chans)
        for i in range(2):
            pieces[i][odd] = half[:, i].reshape(frames * area // 4, chans)
    tokens = frames * area // 4
    frame = first + lax.broadcasted_iota(jnp.int32, (tokens, LANES), 0) // (area // 4)
    label = jnp.where(frame < count, sample + 1, 0).astype(jnp.float32)
    patches = jnp.concatenate(
        [pieces[0][0], pieces[0][1], pieces[1][0], pieces[1][1], label], axis=1
    ).astype(jnp.bfloat16)
    out_ref[...] = jnp.dot(onehot_ref[...], patches, preferred_element_type=jnp.float32).astype(
        jnp.bfloat16
    )


def bag_kernel(clips, cap, chunk, x_ref, *refs):
    first = chunk == 0
    if first:
        e_hbm, w_hbm, out_ref, normed_ref, e_ref, w_ref, qkv_ref, m_ref, r_ref, order_ref, sems = refs
    else:
        normed_ref, w_hbm, out_ref, w_ref, qkv_ref, m_ref, r_ref, order_ref, sems = refs
    count_slots = x_ref.shape[0]
    feats = x_ref.shape[1] - LANES
    model = normed_ref.shape[1]
    width = w_ref.shape[2]
    clip_rows = count_slots // clips
    copies = []
    if first:
        copies.append(pltpu.make_async_copy(e_hbm, e_ref, sems.at[3]))
        copies[0].start()
    loads = [
        pltpu.make_async_copy(
            w_hbm.at[m, :, pl.ds(chunk * width, width)], w_ref.at[m], sems.at[m]
        )
        for m in range(3)
    ]
    for load in loads:
        load.start()

    for c in range(clips):
        note = x_ref[c * clip_rows : (c + 1) * clip_rows, feats:].astype(jnp.float32)
        order_ref[clips + c] = jnp.max(note).astype(jnp.int32)
    starts = [jnp.int32(0)]
    for s in range(SAMPLES):

        def keep_clip(c, at):
            hit = order_ref[clips + c] == s + 1

            @pl.when(hit)
            def _():
                order_ref[at] = c

            return at + hit.astype(jnp.int32)

        starts.append(lax.fori_loop(0, clips, keep_clip, starts[-1]))

    if first:
        row_tile = 256
        copies[0].wait()

        def embed(i, carry):
            at = pl.multiple_of(i * row_tile, row_tile)
            rows = pl.ds(at, row_tile)
            patch = x_ref[rows, :feats]
            total = jnp.zeros((row_tile, 1), jnp.float32)
            step = 512
            for n in range(0, model, step):
                part = jnp.dot(
                    patch, e_ref[:, n : n + step], preferred_element_type=jnp.float32
                ).astype(jnp.bfloat16)
                normed_ref[rows, n : n + step] = part
                wide = part.astype(jnp.float32)
                total = total + jnp.sum(wide * wide, axis=-1, keepdims=True)
            scale = lax.rsqrt(total * (1.0 / model) + epsilon)
            for n in range(0, model, step):
                wide = normed_ref[rows, n : n + step].astype(jnp.float32)
                normed_ref[rows, n : n + step] = (wide * scale).astype(jnp.bfloat16)
            return carry

        lax.fori_loop(0, count_slots // row_tile, embed, 0)

    col_tile = min(256, width)
    for m in range(3):
        loads[m].wait()
        for n in range(0, width, col_tile):
            part = jnp.dot(
                normed_ref[...], w_ref[m, :, n : n + col_tile], preferred_element_type=jnp.float32
            ).astype(jnp.bfloat16)
            if m == 0:
                part = part * jnp.bfloat16(HDIM ** (-0.5))
            qkv_ref[m, :, n : n + col_tile] = part

    out_ref[...] = jnp.zeros_like(out_ref)
    tile = 2 * clip_rows
    lane = lax.broadcasted_iota(jnp.int32, (tile, LANES), 1)
    low = lane < HDIM
    pairs = width // LANES
    ones = jnp.ones((tile, LANES), jnp.bfloat16)
    pick = (lax.broadcasted_iota(jnp.int32, (8, LANES), 1) == 0).astype(jnp.float32).astype(jnp.bfloat16)
    key_at = lax.broadcasted_iota(jnp.int32, (1, tile), 1)

    def two(ref, a, b, *at):
        return jnp.concatenate(
            [
                ref[(*at[:-1], pl.ds(pl.multiple_of(a * clip_rows, 16), clip_rows), at[-1])],
                ref[(*at[:-1], pl.ds(pl.multiple_of(b * clip_rows, 16), clip_rows), at[-1])],
            ],
            axis=0,
        )

    for s in range(SAMPLES):
        begin, size = starts[s], starts[s + 1] - starts[s]
        tiles = (size + 1) // 2

        def members(i):
            second = 2 * i + 1 < size
            return (
                order_ref[begin + 2 * i],
                order_ref[begin + 2 * i + second.astype(jnp.int32)],
                second,
            )

        def bias_of(a, b, second):
            label = lax.dot_general(
                pick,
                two(x_ref, a, b, slice(feats, feats + LANES)),
                (((1,), (1,)), ((), ())),
                preferred_element_type=jnp.float32,
            )[:1]
            limit = jnp.where(second, tile, clip_rows)
            good = jnp.logical_and(label == s + 1.0, key_at < limit)
            return jnp.where(good, 0.0, far_below)

        def scores_of(pair, half, query, a, b, bias):
            cols = slice(pair * LANES, (pair + 1) * LANES)
            keys = two(qkv_ref, a, b, 1, cols)
            one = jnp.where(low if half == 0 else jnp.logical_not(low), query, jnp.zeros_like(query))
            return (
                lax.dot_general(one, keys, (((1,), (1,)), ((), ())), preferred_element_type=jnp.float32)
                + bias
            )

        def mix(pair, shifted, a, b):
            cols = slice(pair * LANES, (pair + 1) * LANES)
            values = jnp.concatenate([two(qkv_ref, a, b, 2, cols), ones], axis=1)
            return jnp.dot(shifted.astype(jnp.bfloat16), values, preferred_element_type=jnp.float32)

        def store(pair, a, b, results):
            cols = slice(pair * LANES, (pair + 1) * LANES)
            heads = [r[:, :LANES] / r[:, LANES:] for r in results]
            mixed = jnp.where(low, heads[0], heads[1])
            for at, clip in ((clip_rows, b), (0, a)):
                for f in range(clip_rows // cap):
                    piece = mixed[at + f * cap : at + (f + 1) * cap]
                    out_ref[f * clips + clip, :, cols] = piece.astype(jnp.bfloat16)

        def query_tile(i, carry):
            qa, qb, _ = members(i)

            @pl.when(tiles == 1)
            def _():
                ka, kb, second = members(0)
                bias = bias_of(ka, kb, second)
                for pair in range(pairs):
                    query = two(qkv_ref, qa, qb, 0, slice(pair * LANES, (pair + 1) * LANES))
                    results = []
                    for half in range(2):
                        scores = scores_of(pair, half, query, ka, kb, bias)
                        top = jnp.max(scores, axis=-1, keepdims=True)
                        results.append(mix(pair, jnp.exp(scores - top), ka, kb))
                    store(pair, qa, qb, results)

            @pl.when(tiles > 1)
            def _():
                for h in range(2 * pairs):
                    m_ref[h] = jnp.full((tile, LANES), far_below, jnp.float32)
                    r_ref[h] = jnp.zeros((tile, 2 * LANES), jnp.float32)

                def key_tile(j, inner):
                    ka, kb, second = members(j)
                    bias = bias_of(ka, kb, second)
                    for pair in range(pairs):
                        query = two(qkv_ref, qa, qb, 0, slice(pair * LANES, (pair + 1) * LANES))
                        for half in range(2):
                            h = 2 * pair + half
                            scores = scores_of(pair, half, query, ka, kb, bias)
                            old = m_ref[h][:, :1]
                            top = jnp.maximum(old, jnp.max(scores, axis=-1, keepdims=True))
                            r_ref[h] = r_ref[h] * jnp.exp(old - top) + mix(
                                pair, jnp.exp(scores - top), ka, kb
                            )
                            m_ref[h] = jnp.broadcast_to(top, (tile, LANES))
                    return inner

                lax.fori_loop(0, tiles, key_tile, 0)
                for pair in range(pairs):
                    store(pair, qa, qb, [r_ref[2 * pair], r_ref[2 * pair + 1]])

            return carry

        lax.fori_loop(0, tiles, query_tile, 0)


def collect_kernel(frames, heads, chunks, count_ref, onehot_ref, *refs):
    recv_refs, out_ref = refs[:chunks], refs[chunks]
    count = count_ref[0]
    place = lax.axis_index("head")
    slots, tokens = onehot_ref.shape
    frame = place * frames + lax.broadcasted_iota(jnp.int32, (slots, tokens), 1) // (tokens // frames)
    onehot = jnp.where(frame < count, onehot_ref[...], jnp.zeros((), jnp.bfloat16))
    width = recv_refs[0].shape[1]
    for h in range(heads):
        for c in range(chunks):
            picked = lax.dot_general(
                onehot,
                recv_refs[c][h * slots : (h + 1) * slots, :],
                (((0,), (0,)), ((), ())),
                preferred_element_type=jnp.float32,
            )
            at = (h * chunks + c) * width
            out_ref[:, at : at + width] = picked.astype(jnp.bfloat16)


def shards(latents, frame_counts, routes, samples, conv_weight, embed_weight, qkv_weight):
    frames_dev, rows, cols, depth = latents.shape[1:]
    heads_dev = lax.axis_size("head")
    bags = lax.axis_size("bag")
    area = rows * cols
    tok_dev = frames_dev * area // 4
    cap = 3 * tok_dev // (2 * bags)
    slots = bags * cap
    local_width = qkv_weight.shape[2]
    chans = conv_weight.shape[2]

    tile = latents.reshape(frames_dev, area, depth)
    ends = heads_dev - 1
    prev_frame = lax.ppermute(tile[frames_dev - 1], "head", [(i, i + 1) for i in range(ends)])
    next_frame = lax.ppermute(tile[0], "head", [(i + 1, i) for i in range(ends)])

    route_rows = routes[:, 0].reshape(heads_dev, tok_dev)
    row_width = 4 * chans + LANES
    acc, onehot = pl.pallas_call(
        functools.partial(own_kernel, bags, cap, rows, cols, frames_dev),
        out_shape=(
            jax.ShapeDtypeStruct((frames_dev * area, chans), jnp.float32),
            jax.ShapeDtypeStruct((slots, tok_dev), jnp.bfloat16),
        ),
        in_specs=[SMEM, VMEM, VMEM, VMEM],
        out_specs=(VMEM, VMEM),
        compiler_params=limit(16),
        cost_estimate=pl.CostEstimate(flops=1200000000, bytes_accessed=4500000, transcendentals=0),
        name="own",
    )(frame_counts, tile.reshape(frames_dev * area, depth), conv_weight, route_rows)
    outgoing = pl.pallas_call(
        functools.partial(halo_kernel, rows, cols, frames_dev),
        out_shape=jax.ShapeDtypeStruct((slots, row_width), jnp.bfloat16),
        in_specs=[SMEM, SMEM, VMEM, VMEM, VMEM, VMEM, VMEM],
        out_specs=VMEM,
        scratch_shapes=[pltpu.VMEM((frames_dev * area, chans), jnp.float32)],
        compiler_params=limit(16),
        cost_estimate=pl.CostEstimate(flops=600000000, bytes_accessed=4500000, transcendentals=0),
        name="halo",
    )(frame_counts, samples, acc, prev_frame, next_frame, conv_weight, onehot)

    arrived = lax.all_to_all(
        outgoing.reshape(bags, cap, row_width), "bag", split_axis=0, concat_axis=0, tiled=True
    )
    count_slots = heads_dev * slots
    gathered = lax.all_gather(arrived, "head", axis=1, tiled=True).reshape(count_slots, row_width)

    pair_rows = 2 * heads_dev * cap
    model = embed_weight.shape[1]
    chunks = CHUNKS if local_width % (CHUNKS * LANES) == 0 else 1
    width = local_width // chunks
    heads_here = width // HDIM
    received = []
    normed = None
    for chunk in range(chunks):
        scratch = [
            pltpu.VMEM((3, model, width), jnp.bfloat16),
            pltpu.VMEM((3, count_slots, width), jnp.bfloat16),
            pltpu.VMEM((heads_here, pair_rows, LANES), jnp.float32),
            pltpu.VMEM((heads_here, pair_rows, 2 * LANES), jnp.float32),
            pltpu.SMEM((2 * bags,), jnp.int32),
            pltpu.SemaphoreType.DMA((4,)),
        ]
        out_shape = [jax.ShapeDtypeStruct((heads_dev * bags, cap, width), jnp.bfloat16)]
        if chunk == 0:
            out_shape.append(jax.ShapeDtypeStruct((count_slots, model), jnp.bfloat16))
            scratch.insert(0, pltpu.VMEM(embed_weight.shape, jnp.bfloat16))
            operands = (gathered, embed_weight, qkv_weight)
            in_specs = [VMEM, pl.BlockSpec(memory_space=pl.ANY), pl.BlockSpec(memory_space=pl.ANY)]
        else:
            operands = (gathered, normed, qkv_weight)
            in_specs = [VMEM, VMEM, pl.BlockSpec(memory_space=pl.ANY)]
        results = pl.pallas_call(
            functools.partial(bag_kernel, bags, cap, chunk),
            out_shape=out_shape,
            in_specs=in_specs,
            out_specs=[VMEM] * len(out_shape),
            scratch_shapes=scratch,
            compiler_params=limit(28),
            cost_estimate=pl.CostEstimate(
                flops=3000000000, bytes_accessed=8000000, transcendentals=600000
            ),
            name=f"bag{chunk}",
        )(*operands)
        if chunk == 0:
            normed = results[1]
        received.append(
            lax.all_to_all(results[0], ("head", "bag"), split_axis=0, concat_axis=0, tiled=True).reshape(
                count_slots, width
            )
        )
    return pl.pallas_call(
        functools.partial(collect_kernel, frames_dev, heads_dev, chunks),
        out_shape=jax.ShapeDtypeStruct((tok_dev, heads_dev * local_width), jnp.bfloat16),
        in_specs=[SMEM, VMEM] + [VMEM] * chunks,
        out_specs=VMEM,
        compiler_params=limit(16),
        name="collect",
    )(frame_counts, onehot, *received)


def solution(mesh):
    placed = (
        P("bag", "head", None, None, None),
        P("bag"),
        P("bag", None),
        P("bag"),
        P(),
        P(),
        P(None, None, "head"),
    )
    return jax.shard_map(
        shards, mesh=mesh, in_specs=placed, out_specs=P(("bag", "head"), None), check_vma=False
    )
```

```python
import functools
import jax
import jax.numpy as jnp
from jax import lax
from jax.experimental import pallas as pl
from jax.experimental.pallas import tpu as pltpu
from jax.sharding import PartitionSpec as P

HDIM = 64
TAPS = 3
SAMPLES = 4
LANES = 128

epsilon = 1e-06
far_below = -1e30

SMEM = pl.BlockSpec(memory_space=pltpu.SMEM)
VMEM = pl.BlockSpec(memory_space=pltpu.VMEM)
HBM = pl.BlockSpec(memory_space=pltpu.HBM)


def limit(mib):
    return pltpu.CompilerParams(vmem_limit_bytes=mib << 20)


def slot_of(route_row, bags, cap, stride):
    tokens = route_row.shape[1]
    bag_ids = lax.broadcasted_iota(jnp.int32, (bags, tokens), 0)
    onehot = (bag_ids == route_row).astype(jnp.float32)
    before = (
        lax.broadcasted_iota(jnp.int32, (tokens, tokens), 0)
        < lax.broadcasted_iota(jnp.int32, (tokens, tokens), 1)
    )
    earlier = jnp.dot(
        onehot.astype(jnp.bfloat16),
        before.astype(jnp.float32).astype(jnp.bfloat16),
        preferred_element_type=jnp.float32,
    )
    rank = jnp.sum(earlier * onehot, axis=0, keepdims=True).astype(jnp.int32)
    return route_row * stride + rank


def onehot_of(slot, slots):
    slot_ids = lax.broadcasted_iota(jnp.int32, (slots, slot.shape[1]), 0)
    return (slot_ids == slot).astype(jnp.float32).astype(jnp.bfloat16)


def combine(products, rows, cols):
    chans = products[0].shape[1]
    blank = jnp.zeros((cols, chans), jnp.float32)
    area = rows * cols
    column = lax.broadcasted_iota(jnp.int32, (area, chans), 0) % cols
    total = None
    for e in range(TAPS):
        up, mid, down = products[e], products[TAPS + e], products[2 * TAPS + e]
        merged = (
            mid
            + jnp.concatenate([blank, up[: area - cols]], axis=0)
            + jnp.concatenate([down[cols:], blank], axis=0)
        )
        if e == 0:
            merged = jnp.where(column == 0, 0.0, pltpu.roll(merged, 1, axis=0))
        elif e == 2:
            merged = jnp.where(column == cols - 1, 0.0, pltpu.roll(merged, area - 1, axis=0))
        total = merged if total is None else total + merged
    return total


def plane_products(pieces, w_ref):
    plane = TAPS * TAPS
    chans = w_ref.shape[2]
    stacked = pieces[0][1] if len(pieces) == 1 else jnp.concatenate([x for _, x in pieces], axis=1)
    products = []
    for p in range(0, plane, 2):
        pair = []
        for q in range(p, min(p + 2, plane)):
            taps = [w_ref[plane * t + q] for t, _ in pieces]
            pair.append(taps[0] if len(taps) == 1 else jnp.concatenate(taps, axis=0))
        weight = pair[0] if len(pair) == 1 else jnp.concatenate(pair, axis=1)
        value = jnp.dot(stacked, weight, preferred_element_type=jnp.float32)
        for q in range(len(pair)):
            products.append(value[:, q * chans : (q + 1) * chans])
    return products


def own_kernel(
    bags, cap, rows, cols, frames, count_ref, x_hbm, w_hbm, route_ref, acc_ref, onehot_ref, w_ref, x_ref, sems
):
    loads = [
        pltpu.make_async_copy(x_hbm, x_ref, sems.at[0]),
        pltpu.make_async_copy(w_hbm, w_ref, sems.at[1]),
    ]
    for load in loads:
        load.start()
    count = count_ref[0]
    place = lax.axis_index("head")
    area = rows * cols
    first = place * frames
    route_row = route_ref[pl.ds(place, 1), :]
    onehot_ref[...] = onehot_of(slot_of(route_row, bags, cap, cap), bags * cap)
    for load in loads:
        load.wait()
    inputs = []
    for f in range(frames):
        value = x_ref[f * area : (f + 1) * area, :]
        inputs.append(jnp.where(first + f < count, value, jnp.zeros_like(value)))
    for f in range(frames):
        pieces = [(t, inputs[f + t - 1]) for t in range(TAPS) if 0 <= f + t - 1 < frames]
        acc_ref[f * area : (f + 1) * area, :] = combine(plane_products(pieces, w_ref), rows, cols)


def halo_kernel(
    rows, cols, frames, count_ref, sample_ref, acc_ref, prev_ref, next_ref, w_ref, onehot_ref, out_ref, grid_ref
):
    count = count_ref[0]
    sample = sample_ref[0]
    place = lax.axis_index("head")
    area = rows * cols
    first = place * frames
    chans = w_ref.shape[2]

    def masked(value, frame):
        live = jnp.logical_and(frame >= 0, frame < count)
        return jnp.where(live, value, jnp.zeros_like(value))

    for f in range(frames):
        part = acc_ref[f * area : (f + 1) * area, :]
        pieces = []
        if f == 0:
            pieces.append((0, masked(prev_ref[...], first - 1)))
        if f == frames - 1:
            pieces.append((2, masked(next_ref[...], first + frames)))
        if pieces:
            part = part + combine(plane_products(pieces, w_ref), rows, cols)
        grid_ref[f * area : (f + 1) * area, :] = jnp.where(first + f < count, part, 0.0)
    pieces = [[None] * 2 for _ in range(2)]
    for odd in range(2):
        half = grid_ref[pl.ds(odd, frames * area // 2, stride=2), :]
        half = half.reshape(frames * rows // 2, 2, cols // 2, chans)
        for i in range(2):
            pieces[i][odd] = half[:, i].reshape(frames * area // 4, chans)
    tokens = frames * area // 4
    frame = first + lax.broadcasted_iota(jnp.int32, (tokens, LANES), 0) // (area // 4)
    label = jnp.where(frame < count, sample + 1, 0).astype(jnp.float32)
    patches = jnp.concatenate(
        [pieces[0][0], pieces[0][1], pieces[1][0], pieces[1][1], label], axis=1
    ).astype(jnp.bfloat16)
    out_ref[...] = jnp.dot(onehot_ref[...], patches, preferred_element_type=jnp.float32).astype(
        jnp.bfloat16
    )


def fold_kernel(e_hbm, w_hbm, e_ref, fold_ref, w_ref, sems):
    feats = e_ref.shape[0]
    width = w_ref.shape[2]
    loads = [pltpu.make_async_copy(e_hbm, e_ref, sems.at[3])]
    for m in range(3):
        loads.append(pltpu.make_async_copy(w_hbm.at[m], w_ref.at[m], sems.at[m]))
    for load in loads:
        load.start()
    loads[0].wait()
    col_tile = 256
    for m in range(3):
        loads[1 + m].wait()
        for n in range(0, width, col_tile):
            cols = slice(n, n + col_tile)
            product = jnp.dot(e_ref[...], w_ref[m, :, cols], preferred_element_type=jnp.float32)
            if m == 0:
                product = product * HDIM ** (-0.5)
            high = product.astype(jnp.bfloat16)
            fold_ref[m, :feats, cols] = high
            fold_ref[m, feats:, cols] = (product - high.astype(jnp.float32)).astype(jnp.bfloat16)


def bag_kernel(
    clips, cap, x_ref, e_ref, fold_ref, out_ref, qkv_ref, total_ref, m_ref, r_ref, order_ref
):
    count_slots = x_ref.shape[0]
    feats, model = e_ref.shape
    width = fold_ref.shape[2]
    clip_rows = count_slots // clips

    for c in range(clips):
        note = x_ref[c * clip_rows : (c + 1) * clip_rows, feats:].astype(jnp.float32)
        order_ref[clips + c] = jnp.max(note).astype(jnp.int32)
    starts = [jnp.int32(0)]
    for s in range(SAMPLES):

        def keep_clip(c, at):
            hit = order_ref[clips + c] == s + 1

            @pl.when(hit)
            def _():
                order_ref[at] = c

            return at + hit.astype(jnp.int32)

        starts.append(lax.fori_loop(0, clips, keep_clip, starts[-1]))

    col_tile = 256
    patch = x_ref[:, :feats]
    for n in range(0, model, col_tile):
        part = jnp.dot(patch, e_ref[:, n : n + col_tile], preferred_element_type=jnp.float32)
        squares = part * part
        both = squares[:, :LANES] + squares[:, LANES:]
        total_ref[...] = both if n == 0 else total_ref[...] + both
    mean = jnp.sum(total_ref[...], axis=-1, keepdims=True) * (1.0 / model)
    total_ref[...] = jnp.broadcast_to(lax.rsqrt(mean + epsilon), total_ref.shape)
    twice = jnp.concatenate([patch, patch], axis=1)
    for m in range(3):
        for n in range(0, width, col_tile):
            part = jnp.dot(twice, fold_ref[m, :, n : n + col_tile], preferred_element_type=jnp.float32)
            scale = total_ref[...]
            qkv_ref[m, :, n : n + col_tile] = (
                part * jnp.concatenate([scale] * (col_tile // LANES), axis=1)
            ).astype(jnp.bfloat16)

    out_ref[...] = jnp.zeros_like(out_ref)
    tile = 2 * clip_rows
    lane = lax.broadcasted_iota(jnp.int32, (tile, LANES), 1)
    low = lane < HDIM
    pairs = width // LANES
    ones = jnp.ones((tile, LANES), jnp.bfloat16)
    pick = (lax.broadcasted_iota(jnp.int32, (8, LANES), 1) == 0).astype(jnp.float32).astype(jnp.bfloat16)
    key_at = lax.broadcasted_iota(jnp.int32, (1, tile), 1)

    def two(ref, a, b, *at):
        return jnp.concatenate(
            [
                ref[(*at[:-1], pl.ds(pl.multiple_of(a * clip_rows, 16), clip_rows), at[-1])],
                ref[(*at[:-1], pl.ds(pl.multiple_of(b * clip_rows, 16), clip_rows), at[-1])],
            ],
            axis=0,
        )

    for s in range(SAMPLES):
        begin, size = starts[s], starts[s + 1] - starts[s]
        tiles = (size + 1) // 2

        def members(i):
            second = 2 * i + 1 < size
            return (
                order_ref[begin + 2 * i],
                order_ref[begin + 2 * i + second.astype(jnp.int32)],
                second,
            )

        def bias_of(a, b, second):
            label = lax.dot_general(
                pick,
                two(x_ref, a, b, slice(feats, feats + LANES)),
                (((1,), (1,)), ((), ())),
                preferred_element_type=jnp.float32,
            )[:1]
            limit = jnp.where(second, tile, clip_rows)
            good = jnp.logical_and(label == s + 1.0, key_at < limit)
            return jnp.where(good, 0.0, far_below)

        def scores_of(pair, half, query, a, b, bias):
            cols = slice(pair * LANES, (pair + 1) * LANES)
            keys = two(qkv_ref, a, b, 1, cols)
            one = jnp.where(low if half == 0 else jnp.logical_not(low), query, jnp.zeros_like(query))
            return (
                lax.dot_general(one, keys, (((1,), (1,)), ((), ())), preferred_element_type=jnp.float32)
                + bias
            )

        def mix(pair, shifted, a, b):
            cols = slice(pair * LANES, (pair + 1) * LANES)
            values = jnp.concatenate([two(qkv_ref, a, b, 2, cols), ones], axis=1)
            return jnp.dot(shifted.astype(jnp.bfloat16), values, preferred_element_type=jnp.float32)

        def store(pair, a, b, results):
            cols = slice(pair * LANES, (pair + 1) * LANES)
            heads = [r[:, :LANES] / r[:, LANES:] for r in results]
            mixed = jnp.where(low, heads[0], heads[1])
            for at, clip in ((clip_rows, b), (0, a)):
                for f in range(clip_rows // cap):
                    piece = mixed[at + f * cap : at + (f + 1) * cap]
                    out_ref[f * clips + clip, :, cols] = piece.astype(jnp.bfloat16)

        def query_tile(i, carry):
            qa, qb, _ = members(i)

            @pl.when(tiles == 1)
            def _():
                ka, kb, second = members(0)
                bias = bias_of(ka, kb, second)
                for pair in range(pairs):
                    query = two(qkv_ref, qa, qb, 0, slice(pair * LANES, (pair + 1) * LANES))
                    results = []
                    for half in range(2):
                        scores = scores_of(pair, half, query, ka, kb, bias)
                        top = jnp.max(scores, axis=-1, keepdims=True)
                        results.append(mix(pair, jnp.exp(scores - top), ka, kb))
                    store(pair, qa, qb, results)

            @pl.when(tiles > 1)
            def _():
                for h in range(2 * pairs):
                    m_ref[h] = jnp.full((tile, LANES), far_below, jnp.float32)
                    r_ref[h] = jnp.zeros((tile, 2 * LANES), jnp.float32)

                def key_tile(j, inner):
                    ka, kb, second = members(j)
                    bias = bias_of(ka, kb, second)
                    for pair in range(pairs):
                        query = two(qkv_ref, qa, qb, 0, slice(pair * LANES, (pair + 1) * LANES))
                        for half in range(2):
                            h = 2 * pair + half
                            scores = scores_of(pair, half, query, ka, kb, bias)
                            old = m_ref[h][:, :1]
                            top = jnp.maximum(old, jnp.max(scores, axis=-1, keepdims=True))
                            r_ref[h] = r_ref[h] * jnp.exp(old - top) + mix(
                                pair, jnp.exp(scores - top), ka, kb
                            )
                            m_ref[h] = jnp.broadcast_to(top, (tile, LANES))
                    return inner

                lax.fori_loop(0, tiles, key_tile, 0)
                for pair in range(pairs):
                    store(pair, qa, qb, [r_ref[2 * pair], r_ref[2 * pair + 1]])

            return carry

        lax.fori_loop(0, tiles, query_tile, 0)


def collect_kernel(frames, heads, count_ref, onehot_ref, recv_ref, out_ref):
    count = count_ref[0]
    place = lax.axis_index("head")
    slots, tokens = onehot_ref.shape
    frame = place * frames + lax.broadcasted_iota(jnp.int32, (slots, tokens), 1) // (tokens // frames)
    onehot = jnp.where(frame < count, onehot_ref[...], jnp.zeros((), jnp.bfloat16))
    width = recv_ref.shape[1]
    for h in range(heads):
        picked = lax.dot_general(
            onehot,
            recv_ref[h * slots : (h + 1) * slots, :],
            (((0,), (0,)), ((), ())),
            preferred_element_type=jnp.float32,
        )
        out_ref[:, h * width : (h + 1) * width] = picked.astype(jnp.bfloat16)


def shards(latents, frame_counts, routes, samples, conv_weight, embed_weight, qkv_weight):
    frames_dev, rows, cols, depth = latents.shape[1:]
    heads_dev = lax.axis_size("head")
    bags = lax.axis_size("bag")
    area = rows * cols
    tok_dev = frames_dev * area // 4
    cap = 3 * tok_dev // (2 * bags)
    slots = bags * cap
    local_width = qkv_weight.shape[2]
    chans = conv_weight.shape[2]

    tile = latents.reshape(frames_dev, area, depth)
    ends = heads_dev - 1
    prev_frame = lax.ppermute(tile[frames_dev - 1], "head", [(i, i + 1) for i in range(ends)])
    next_frame = lax.ppermute(tile[0], "head", [(i + 1, i) for i in range(ends)])

    route_rows = routes[:, 0].reshape(heads_dev, tok_dev)
    row_width = 4 * chans + LANES
    model = embed_weight.shape[1]
    acc, onehot, conv_near = pl.pallas_call(
        functools.partial(own_kernel, bags, cap, rows, cols, frames_dev),
        out_shape=(
            jax.ShapeDtypeStruct((frames_dev * area, chans), jnp.float32),
            jax.ShapeDtypeStruct((slots, tok_dev), jnp.bfloat16),
            jax.ShapeDtypeStruct(conv_weight.shape, jnp.bfloat16),
        ),
        in_specs=[SMEM, HBM, HBM, VMEM],
        out_specs=(VMEM, VMEM, VMEM),
        scratch_shapes=[
            pltpu.VMEM((frames_dev * area, depth), jnp.bfloat16),
            pltpu.SemaphoreType.DMA((2,)),
        ],
        compiler_params=limit(16),
        cost_estimate=pl.CostEstimate(flops=1200000000, bytes_accessed=4500000, transcendentals=0),
        name="own",
    )(frame_counts, tile.reshape(frames_dev * area, depth), conv_weight, route_rows)
    outgoing = pl.pallas_call(
        functools.partial(halo_kernel, rows, cols, frames_dev),
        out_shape=jax.ShapeDtypeStruct((slots, row_width), jnp.bfloat16),
        in_specs=[SMEM, SMEM, VMEM, VMEM, VMEM, VMEM, VMEM],
        out_specs=VMEM,
        scratch_shapes=[pltpu.VMEM((frames_dev * area, chans), jnp.float32)],
        compiler_params=limit(16),
        cost_estimate=pl.CostEstimate(flops=600000000, bytes_accessed=4500000, transcendentals=0),
        name="halo",
    )(frame_counts, samples, acc, prev_frame, next_frame, conv_near, onehot)

    arrived = lax.all_to_all(
        outgoing.reshape(bags, cap, row_width), "bag", split_axis=0, concat_axis=0, tiled=True
    )
    embed_near, folded = pl.pallas_call(
        fold_kernel,
        out_shape=(
            jax.ShapeDtypeStruct(embed_weight.shape, jnp.bfloat16),
            jax.ShapeDtypeStruct((3, 2 * embed_weight.shape[0], local_width), jnp.bfloat16),
        ),
        in_specs=[HBM, HBM],
        out_specs=(VMEM, VMEM),
        scratch_shapes=[
            pltpu.VMEM(qkv_weight.shape, jnp.bfloat16),
            pltpu.SemaphoreType.DMA((4,)),
        ],
        compiler_params=limit(24),
        cost_estimate=pl.CostEstimate(flops=3300000000, bytes_accessed=14000000, transcendentals=0),
        name="fold",
    )(embed_weight, qkv_weight)
    count_slots = heads_dev * slots
    gathered = lax.all_gather(arrived, "head", axis=1, tiled=True).reshape(count_slots, row_width)

    pair_rows = 2 * heads_dev * cap
    heads_here = local_width // HDIM
    attended = pl.pallas_call(
        functools.partial(bag_kernel, bags, cap),
        out_shape=jax.ShapeDtypeStruct((heads_dev * bags, cap, local_width), jnp.bfloat16),
        in_specs=[VMEM, VMEM, VMEM],
        out_specs=VMEM,
        scratch_shapes=[
            pltpu.VMEM((3, count_slots, local_width), jnp.bfloat16),
            pltpu.VMEM((count_slots, LANES), jnp.float32),
            pltpu.VMEM((heads_here, pair_rows, LANES), jnp.float32),
            pltpu.VMEM((heads_here, pair_rows, 2 * LANES), jnp.float32),
            pltpu.SMEM((2 * bags,), jnp.int32),
        ],
        compiler_params=limit(28),
        cost_estimate=pl.CostEstimate(flops=5000000000, bytes_accessed=8000000, transcendentals=1200000),
        name="bag",
    )(gathered, embed_near, folded)
    received = lax.all_to_all(attended, ("head", "bag"), split_axis=0, concat_axis=0, tiled=True)
    return pl.pallas_call(
        functools.partial(collect_kernel, frames_dev, heads_dev),
        out_shape=jax.ShapeDtypeStruct((tok_dev, heads_dev * local_width), jnp.bfloat16),
        in_specs=[SMEM, VMEM, VMEM],
        out_specs=VMEM,
        compiler_params=limit(16),
        name="collect",
    )(frame_counts, onehot, received.reshape(count_slots, local_width))


def solution(mesh):
    placed = (
        P("bag", "head", None, None, None),
        P("bag"),
        P("bag", None),
        P("bag"),
        P(),
        P(),
        P(None, None, "head"),
    )
    return jax.shard_map(
        shards, mesh=mesh, in_specs=placed, out_specs=P(("bag", "head"), None), check_vma=False
    )
```

```python
import functools
import jax
import jax.numpy as jnp
from jax import lax
from jax.experimental import pallas as pl
from jax.experimental.pallas import tpu as pltpu
from jax.sharding import PartitionSpec as P

HDIM = 64
TAPS = 3
SAMPLES = 4
LANES = 128

epsilon = 1e-06
far_below = -1e30

SMEM = pl.BlockSpec(memory_space=pltpu.SMEM)
VMEM = pl.BlockSpec(memory_space=pltpu.VMEM)
ANY = pl.BlockSpec(memory_space=pl.ANY)


def limit(mib):
    return pltpu.CompilerParams(vmem_limit_bytes=mib << 20)


def slot_of(route_row, bags, cap, stride):
    tokens = route_row.shape[1]
    bag_ids = lax.broadcasted_iota(jnp.int32, (bags, tokens), 0)
    onehot = (bag_ids == route_row).astype(jnp.float32)
    before = (
        lax.broadcasted_iota(jnp.int32, (tokens, tokens), 0)
        < lax.broadcasted_iota(jnp.int32, (tokens, tokens), 1)
    )
    earlier = jnp.dot(
        onehot.astype(jnp.bfloat16),
        before.astype(jnp.float32).astype(jnp.bfloat16),
        preferred_element_type=jnp.float32,
    )
    rank = jnp.sum(earlier * onehot, axis=0, keepdims=True).astype(jnp.int32)
    return route_row * stride + rank


def onehot_of(slot, slots):
    slot_ids = lax.broadcasted_iota(jnp.int32, (slots, slot.shape[1]), 0)
    return (slot_ids == slot).astype(jnp.float32).astype(jnp.bfloat16)


def combine(products, rows, cols):
    chans = products[0].shape[1]
    blank = jnp.zeros((cols, chans), jnp.float32)
    area = rows * cols
    column = lax.broadcasted_iota(jnp.int32, (area, chans), 0) % cols
    total = None
    for e in range(TAPS):
        up, mid, down = products[e], products[TAPS + e], products[2 * TAPS + e]
        merged = (
            mid
            + jnp.concatenate([blank, up[: area - cols]], axis=0)
            + jnp.concatenate([down[cols:], blank], axis=0)
        )
        if e == 0:
            merged = jnp.where(column == 0, 0.0, pltpu.roll(merged, 1, axis=0))
        elif e == 2:
            merged = jnp.where(column == cols - 1, 0.0, pltpu.roll(merged, area - 1, axis=0))
        total = merged if total is None else total + merged
    return total


def plane_products(pieces, w_ref):
    plane = TAPS * TAPS
    chans = w_ref.shape[2]
    stacked = pieces[0][1] if len(pieces) == 1 else jnp.concatenate([x for _, x in pieces], axis=1)
    products = []
    for p in range(0, plane, 2):
        pair = []
        for q in range(p, min(p + 2, plane)):
            taps = [w_ref[plane * t + q] for t, _ in pieces]
            pair.append(taps[0] if len(taps) == 1 else jnp.concatenate(taps, axis=0))
        weight = pair[0] if len(pair) == 1 else jnp.concatenate(pair, axis=1)
        value = jnp.dot(stacked, weight, preferred_element_type=jnp.float32)
        for q in range(len(pair)):
            products.append(value[:, q * chans : (q + 1) * chans])
    return products


def own_kernel(
    bags, cap, rows, cols, frames, count_ref, x_hbm, w_hbm, route_ref, acc_ref, onehot_ref, x_ref, w_ref, sems
):
    loads = [
        pltpu.make_async_copy(x_hbm, x_ref, sems.at[0]),
        pltpu.make_async_copy(w_hbm, w_ref, sems.at[1]),
    ]
    for load in loads:
        load.start()
    count = count_ref[0]
    place = lax.axis_index("head")
    area = rows * cols
    first = place * frames
    route_row = route_ref[pl.ds(place, 1), :]
    onehot_ref[...] = onehot_of(slot_of(route_row, bags, cap, cap), bags * cap)
    for load in loads:
        load.wait()
    inputs = []
    for f in range(frames):
        value = x_ref[f * area : (f + 1) * area, :]
        inputs.append(jnp.where(first + f < count, value, jnp.zeros_like(value)))
    for f in range(frames):
        pieces = [(t, inputs[f + t - 1]) for t in range(TAPS) if 0 <= f + t - 1 < frames]
        acc_ref[f * area : (f + 1) * area, :] = combine(plane_products(pieces, w_ref), rows, cols)


def halo_kernel(
    rows, cols, frames, count_ref, sample_ref, acc_ref, prev_ref, next_ref, w_ref, onehot_ref, out_ref, grid_ref
):
    count = count_ref[0]
    sample = sample_ref[0]
    place = lax.axis_index("head")
    area = rows * cols
    first = place * frames
    chans = w_ref.shape[2]

    def masked(value, frame):
        live = jnp.logical_and(frame >= 0, frame < count)
        return jnp.where(live, value, jnp.zeros_like(value))

    for f in range(frames):
        part = acc_ref[f * area : (f + 1) * area, :]
        pieces = []
        if f == 0:
            pieces.append((0, masked(prev_ref[...], first - 1)))
        if f == frames - 1:
            pieces.append((2, masked(next_ref[...], first + frames)))
        if pieces:
            part = part + combine(plane_products(pieces, w_ref), rows, cols)
        grid_ref[f * area : (f + 1) * area, :] = jnp.where(first + f < count, part, 0.0)
    pieces = [[None] * 2 for _ in range(2)]
    for odd in range(2):
        half = grid_ref[pl.ds(odd, frames * area // 2, stride=2), :]
        half = half.reshape(frames * rows // 2, 2, cols // 2, chans)
        for i in range(2):
            pieces[i][odd] = half[:, i].reshape(frames * area // 4, chans)
    tokens = frames * area // 4
    frame = first + lax.broadcasted_iota(jnp.int32, (tokens, LANES), 0) // (area // 4)
    label = jnp.where(frame < count, sample + 1, 0).astype(jnp.float32)
    patches = jnp.concatenate(
        [pieces[0][0], pieces[0][1], pieces[1][0], pieces[1][1], label], axis=1
    ).astype(jnp.bfloat16)
    out_ref[...] = jnp.dot(onehot_ref[...], patches, preferred_element_type=jnp.float32).astype(
        jnp.bfloat16
    )


def fold_kernel(e_hbm, w_hbm, fold_ref, e_ref, w_ref, sems):
    feats = e_ref.shape[0]
    width = w_ref.shape[2]
    loads = [pltpu.make_async_copy(e_hbm, e_ref, sems.at[3])]
    for m in range(3):
        loads.append(pltpu.make_async_copy(w_hbm.at[m], w_ref.at[m], sems.at[m]))
    for load in loads:
        load.start()
    loads[0].wait()
    col_tile = 256
    for m in range(3):
        loads[1 + m].wait()
        for n in range(0, width, col_tile):
            cols = slice(n, n + col_tile)
            product = jnp.dot(e_ref[...], w_ref[m, :, cols], preferred_element_type=jnp.float32)
            if m == 0:
                product = product * HDIM ** (-0.5)
            high = product.astype(jnp.bfloat16)
            fold_ref[m, :feats, cols] = high
            fold_ref[m, feats:, cols] = (product - high.astype(jnp.float32)).astype(jnp.bfloat16)


def bag_kernel(
    clips, cap, x_ref, e_hbm, fold_hbm, out_ref, e_ref, fold_ref, qkv_ref, total_ref, m_ref, r_ref, order_ref, sems
):
    loads = [
        pltpu.make_async_copy(e_hbm, e_ref, sems.at[0]),
        pltpu.make_async_copy(fold_hbm, fold_ref, sems.at[1]),
    ]
    for load in loads:
        load.start()
    count_slots = x_ref.shape[0]
    feats, model = e_ref.shape
    width = fold_ref.shape[2]
    clip_rows = count_slots // clips

    for c in range(clips):
        note = x_ref[c * clip_rows : (c + 1) * clip_rows, feats:].astype(jnp.float32)
        order_ref[clips + c] = jnp.max(note).astype(jnp.int32)
    starts = [jnp.int32(0)]
    for s in range(SAMPLES):

        def keep_clip(c, at):
            hit = order_ref[clips + c] == s + 1

            @pl.when(hit)
            def _():
                order_ref[at] = c

            return at + hit.astype(jnp.int32)

        starts.append(lax.fori_loop(0, clips, keep_clip, starts[-1]))

    col_tile = 256
    patch = x_ref[:, :feats]
    loads[0].wait()
    for n in range(0, model, col_tile):
        part = jnp.dot(patch, e_ref[:, n : n + col_tile], preferred_element_type=jnp.float32)
        squares = part * part
        both = squares[:, :LANES] + squares[:, LANES:]
        total_ref[...] = both if n == 0 else total_ref[...] + both
    mean = jnp.sum(total_ref[...], axis=-1, keepdims=True) * (1.0 / model)
    total_ref[...] = jnp.broadcast_to(lax.rsqrt(mean + epsilon), total_ref.shape)
    twice = jnp.concatenate([patch, patch], axis=1)
    loads[1].wait()
    for m in range(3):
        for n in range(0, width, col_tile):
            part = jnp.dot(twice, fold_ref[m, :, n : n + col_tile], preferred_element_type=jnp.float32)
            scale = total_ref[...]
            qkv_ref[m, :, n : n + col_tile] = (
                part * jnp.concatenate([scale] * (col_tile // LANES), axis=1)
            ).astype(jnp.bfloat16)

    out_ref[...] = jnp.zeros_like(out_ref)
    tile = 2 * clip_rows
    lane = lax.broadcasted_iota(jnp.int32, (tile, LANES), 1)
    low = lane < HDIM
    pairs = width // LANES
    ones = jnp.ones((tile, LANES), jnp.bfloat16)
    pick = (lax.broadcasted_iota(jnp.int32, (8, LANES), 1) == 0).astype(jnp.float32).astype(jnp.bfloat16)
    key_at = lax.broadcasted_iota(jnp.int32, (1, tile), 1)

    def two(ref, a, b, *at):
        return jnp.concatenate(
            [
                ref[(*at[:-1], pl.ds(pl.multiple_of(a * clip_rows, 16), clip_rows), at[-1])],
                ref[(*at[:-1], pl.ds(pl.multiple_of(b * clip_rows, 16), clip_rows), at[-1])],
            ],
            axis=0,
        )

    for s in range(SAMPLES):
        begin, size = starts[s], starts[s + 1] - starts[s]
        tiles = (size + 1) // 2

        def members(i):
            second = 2 * i + 1 < size
            return (
                order_ref[begin + 2 * i],
                order_ref[begin + 2 * i + second.astype(jnp.int32)],
                second,
            )

        def bias_of(a, b, second):
            label = lax.dot_general(
                pick,
                two(x_ref, a, b, slice(feats, feats + LANES)),
                (((1,), (1,)), ((), ())),
                preferred_element_type=jnp.float32,
            )[:1]
            limit = jnp.where(second, tile, clip_rows)
            good = jnp.logical_and(label == s + 1.0, key_at < limit)
            return jnp.where(good, 0.0, far_below)

        def scores_of(pair, half, query, a, b, bias):
            cols = slice(pair * LANES, (pair + 1) * LANES)
            keys = two(qkv_ref, a, b, 1, cols)
            one = jnp.where(low if half == 0 else jnp.logical_not(low), query, jnp.zeros_like(query))
            return (
                lax.dot_general(one, keys, (((1,), (1,)), ((), ())), preferred_element_type=jnp.float32)
                + bias
            )

        def mix(pair, shifted, a, b):
            cols = slice(pair * LANES, (pair + 1) * LANES)
            values = jnp.concatenate([two(qkv_ref, a, b, 2, cols), ones], axis=1)
            return jnp.dot(shifted.astype(jnp.bfloat16), values, preferred_element_type=jnp.float32)

        def store(pair, a, b, results):
            cols = slice(pair * LANES, (pair + 1) * LANES)
            heads = [r[:, :LANES] / r[:, LANES:] for r in results]
            mixed = jnp.where(low, heads[0], heads[1])
            for at, clip in ((clip_rows, b), (0, a)):
                for f in range(clip_rows // cap):
                    piece = mixed[at + f * cap : at + (f + 1) * cap]
                    out_ref[f * clips + clip, :, cols] = piece.astype(jnp.bfloat16)

        def query_tile(i, carry):
            qa, qb, _ = members(i)

            @pl.when(tiles == 1)
            def _():
                ka, kb, second = members(0)
                bias = bias_of(ka, kb, second)
                for pair in range(pairs):
                    query = two(qkv_ref, qa, qb, 0, slice(pair * LANES, (pair + 1) * LANES))
                    results = []
                    for half in range(2):
                        scores = scores_of(pair, half, query, ka, kb, bias)
                        top = jnp.max(scores, axis=-1, keepdims=True)
                        results.append(mix(pair, jnp.exp(scores - top), ka, kb))
                    store(pair, qa, qb, results)

            @pl.when(tiles > 1)
            def _():
                for h in range(2 * pairs):
                    m_ref[h] = jnp.full((tile, LANES), far_below, jnp.float32)
                    r_ref[h] = jnp.zeros((tile, 2 * LANES), jnp.float32)

                def key_tile(j, inner):
                    ka, kb, second = members(j)
                    bias = bias_of(ka, kb, second)
                    for pair in range(pairs):
                        query = two(qkv_ref, qa, qb, 0, slice(pair * LANES, (pair + 1) * LANES))
                        for half in range(2):
                            h = 2 * pair + half
                            scores = scores_of(pair, half, query, ka, kb, bias)
                            old = m_ref[h][:, :1]
                            top = jnp.maximum(old, jnp.max(scores, axis=-1, keepdims=True))
                            r_ref[h] = r_ref[h] * jnp.exp(old - top) + mix(
                                pair, jnp.exp(scores - top), ka, kb
                            )
                            m_ref[h] = jnp.broadcast_to(top, (tile, LANES))
                    return inner

                lax.fori_loop(0, tiles, key_tile, 0)
                for pair in range(pairs):
                    store(pair, qa, qb, [r_ref[2 * pair], r_ref[2 * pair + 1]])

            return carry

        lax.fori_loop(0, tiles, query_tile, 0)


def collect_kernel(frames, heads, count_ref, onehot_ref, recv_ref, out_ref):
    count = count_ref[0]
    place = lax.axis_index("head")
    slots, tokens = onehot_ref.shape
    frame = place * frames + lax.broadcasted_iota(jnp.int32, (slots, tokens), 1) // (tokens // frames)
    onehot = jnp.where(frame < count, onehot_ref[...], jnp.zeros((), jnp.bfloat16))
    width = recv_ref.shape[1]
    for h in range(heads):
        picked = lax.dot_general(
            onehot,
            recv_ref[h * slots : (h + 1) * slots, :],
            (((0,), (0,)), ((), ())),
            preferred_element_type=jnp.float32,
        )
        out_ref[:, h * width : (h + 1) * width] = picked.astype(jnp.bfloat16)


def shards(latents, frame_counts, routes, samples, conv_weight, embed_weight, qkv_weight):
    frames_dev, rows, cols, depth = latents.shape[1:]
    heads_dev = lax.axis_size("head")
    bags = lax.axis_size("bag")
    area = rows * cols
    tok_dev = frames_dev * area // 4
    cap = 3 * tok_dev // (2 * bags)
    slots = bags * cap
    local_width = qkv_weight.shape[2]
    chans = conv_weight.shape[2]

    tile = latents.reshape(frames_dev, area, depth)
    ends = heads_dev - 1
    prev_frame = lax.ppermute(tile[frames_dev - 1], "head", [(i, i + 1) for i in range(ends)])
    next_frame = lax.ppermute(tile[0], "head", [(i + 1, i) for i in range(ends)])

    route_rows = routes[:, 0].reshape(heads_dev, tok_dev)
    row_width = 4 * chans + LANES
    model = embed_weight.shape[1]
    acc, onehot = pl.pallas_call(
        functools.partial(own_kernel, bags, cap, rows, cols, frames_dev),
        out_shape=(
            jax.ShapeDtypeStruct((frames_dev * area, chans), jnp.float32),
            jax.ShapeDtypeStruct((slots, tok_dev), jnp.bfloat16),
        ),
        in_specs=[SMEM, ANY, ANY, VMEM],
        out_specs=(VMEM, VMEM),
        scratch_shapes=[
            pltpu.VMEM((frames_dev * area, depth), jnp.bfloat16),
            pltpu.VMEM(conv_weight.shape, jnp.bfloat16),
            pltpu.SemaphoreType.DMA((2,)),
        ],
        cost_estimate=pl.CostEstimate(flops=1200000000, bytes_accessed=4500000, transcendentals=0),
        name="own",
    )(frame_counts, tile.reshape(frames_dev * area, depth), conv_weight, route_rows)
    outgoing = pl.pallas_call(
        functools.partial(halo_kernel, rows, cols, frames_dev),
        out_shape=jax.ShapeDtypeStruct((slots, row_width), jnp.bfloat16),
        in_specs=[SMEM, SMEM, VMEM, VMEM, VMEM, VMEM, VMEM],
        out_specs=VMEM,
        scratch_shapes=[pltpu.VMEM((frames_dev * area, chans), jnp.float32)],
        compiler_params=limit(16),
        cost_estimate=pl.CostEstimate(flops=600000000, bytes_accessed=4500000, transcendentals=0),
        name="halo",
    )(frame_counts, samples, acc, prev_frame, next_frame, conv_weight, onehot)

    arrived = lax.all_to_all(
        outgoing.reshape(bags, cap, row_width), "bag", split_axis=0, concat_axis=0, tiled=True
    )
    folded = pl.pallas_call(
        fold_kernel,
        out_shape=jax.ShapeDtypeStruct((3, 2 * embed_weight.shape[0], local_width), jnp.bfloat16),
        in_specs=[ANY, ANY],
        out_specs=VMEM,
        scratch_shapes=[
            pltpu.VMEM(embed_weight.shape, jnp.bfloat16),
            pltpu.VMEM(qkv_weight.shape, jnp.bfloat16),
            pltpu.SemaphoreType.DMA((4,)),
        ],
        cost_estimate=pl.CostEstimate(flops=3300000000, bytes_accessed=14000000, transcendentals=0),
        name="fold",
    )(embed_weight, qkv_weight)
    count_slots = heads_dev * slots
    gathered = lax.all_gather(arrived, "head", axis=1, tiled=True).reshape(count_slots, row_width)

    pair_rows = 2 * heads_dev * cap
    heads_here = local_width // HDIM
    attended = pl.pallas_call(
        functools.partial(bag_kernel, bags, cap),
        out_shape=jax.ShapeDtypeStruct((heads_dev * bags, cap, local_width), jnp.bfloat16),
        in_specs=[VMEM, ANY, ANY],
        out_specs=VMEM,
        scratch_shapes=[
            pltpu.VMEM(embed_weight.shape, jnp.bfloat16),
            pltpu.VMEM(folded.shape, jnp.bfloat16),
            pltpu.VMEM((3, count_slots, local_width), jnp.bfloat16),
            pltpu.VMEM((count_slots, LANES), jnp.float32),
            pltpu.VMEM((heads_here, pair_rows, LANES), jnp.float32),
            pltpu.VMEM((heads_here, pair_rows, 2 * LANES), jnp.float32),
            pltpu.SMEM((2 * bags,), jnp.int32),
            pltpu.SemaphoreType.DMA((2,)),
        ],
        cost_estimate=pl.CostEstimate(flops=5000000000, bytes_accessed=8000000, transcendentals=1200000),
        name="bag",
    )(gathered, embed_weight, folded)
    received = lax.all_to_all(attended, ("head", "bag"), split_axis=0, concat_axis=0, tiled=True)
    return pl.pallas_call(
        functools.partial(collect_kernel, frames_dev, heads_dev),
        out_shape=jax.ShapeDtypeStruct((tok_dev, heads_dev * local_width), jnp.bfloat16),
        in_specs=[SMEM, VMEM, VMEM],
        out_specs=VMEM,
        compiler_params=limit(16),
        name="collect",
    )(frame_counts, onehot, received.reshape(count_slots, local_width))


def solution(mesh):
    placed = (
        P("bag", "head", None, None, None),
        P("bag"),
        P("bag", None),
        P("bag"),
        P(),
        P(),
        P(None, None, "head"),
    )
    return jax.shard_map(
        shards, mesh=mesh, in_specs=placed, out_specs=P(("bag", "head"), None), check_vma=False
    )
```

```python
import functools
import jax
import jax.numpy as jnp
from jax import lax
from jax.experimental import pallas as pl
from jax.experimental.pallas import tpu as pltpu
from jax.sharding import PartitionSpec as P

HDIM = 64
TAPS = 3
SAMPLES = 4
LANES = 128

epsilon = 1e-06
far_below = -1e30

VMEM = pl.BlockSpec(memory_space=pltpu.VMEM)
ANY = pl.BlockSpec(memory_space=pl.ANY)
FOLD_LIMIT = 24


def limit(mib):
    return pltpu.CompilerParams(vmem_limit_bytes=mib << 20)


def slot_of(route_row, bags, cap, stride):
    tokens = route_row.shape[1]
    bag_ids = lax.broadcasted_iota(jnp.int32, (bags, tokens), 0)
    onehot = (bag_ids == route_row).astype(jnp.float32)
    before = (
        lax.broadcasted_iota(jnp.int32, (tokens, tokens), 0)
        < lax.broadcasted_iota(jnp.int32, (tokens, tokens), 1)
    )
    earlier = jnp.dot(
        onehot.astype(jnp.bfloat16),
        before.astype(jnp.float32).astype(jnp.bfloat16),
        preferred_element_type=jnp.float32,
    )
    rank = jnp.sum(earlier * onehot, axis=0, keepdims=True).astype(jnp.int32)
    return route_row * stride + rank


def onehot_of(slot, slots):
    slot_ids = lax.broadcasted_iota(jnp.int32, (slots, slot.shape[1]), 0)
    return (slot_ids == slot).astype(jnp.float32).astype(jnp.bfloat16)


def combine(products, rows, cols):
    chans = products[0].shape[1]
    blank = jnp.zeros((cols, chans), jnp.float32)
    area = rows * cols
    column = lax.broadcasted_iota(jnp.int32, (area, chans), 0) % cols
    total = None
    for e in range(TAPS):
        up, mid, down = products[e], products[TAPS + e], products[2 * TAPS + e]
        merged = (
            mid
            + jnp.concatenate([blank, up[: area - cols]], axis=0)
            + jnp.concatenate([down[cols:], blank], axis=0)
        )
        if e == 0:
            merged = jnp.where(column == 0, 0.0, pltpu.roll(merged, 1, axis=0))
        elif e == 2:
            merged = jnp.where(column == cols - 1, 0.0, pltpu.roll(merged, area - 1, axis=0))
        total = merged if total is None else total + merged
    return total


def plane_products(pieces, w_ref):
    plane = TAPS * TAPS
    chans = w_ref.shape[2]
    stacked = pieces[0][1] if len(pieces) == 1 else jnp.concatenate([x for _, x in pieces], axis=1)
    products = []
    for p in range(0, plane, 2):
        pair = []
        for q in range(p, min(p + 2, plane)):
            taps = [w_ref[plane * t + q] for t, _ in pieces]
            pair.append(taps[0] if len(taps) == 1 else jnp.concatenate(taps, axis=0))
        weight = pair[0] if len(pair) == 1 else jnp.concatenate(pair, axis=1)
        value = jnp.dot(stacked, weight, preferred_element_type=jnp.float32)
        for q in range(len(pair)):
            products.append(value[:, q * chans : (q + 1) * chans])
    return products


def scalar_of(ref):
    return jnp.max(ref[...])


def edge_kernel(rows, cols, frames, count_ref, x_hbm, w_hbm, up_ref, down_ref, x_ref, w_ref, sems):
    loads = [
        pltpu.make_async_copy(x_hbm, x_ref, sems.at[0]),
        pltpu.make_async_copy(w_hbm, w_ref, sems.at[1]),
    ]
    for load in loads:
        load.start()
    count = scalar_of(count_ref)
    area = rows * cols
    first = lax.axis_index("head") * frames
    for load in loads:
        load.wait()
    for out_ref, f, tap in ((up_ref, frames - 1, 0), (down_ref, 0, 2)):
        value = x_ref[f * area : (f + 1) * area, :]
        value = jnp.where(first + f < count, value, jnp.zeros_like(value))
        out_ref[...] = combine(plane_products([(tap, value)], w_ref), rows, cols)


def own_kernel(bags, cap, rows, cols, frames, count_ref, x_ref, w_ref, route_ref, acc_ref, onehot_ref):
    count = scalar_of(count_ref)
    place = lax.axis_index("head")
    area = rows * cols
    first = place * frames
    inputs = []
    for f in range(frames):
        value = x_ref[f * area : (f + 1) * area, :]
        inputs.append(jnp.where(first + f < count, value, jnp.zeros_like(value)))
    for f in range(frames):
        pieces = [(t, inputs[f + t - 1]) for t in range(TAPS) if 0 <= f + t - 1 < frames]
        acc_ref[f * area : (f + 1) * area, :] = combine(plane_products(pieces, w_ref), rows, cols)
    route_row = route_ref[pl.ds(place, 1), :]
    onehot_ref[...] = onehot_of(slot_of(route_row, bags, cap, cap), bags * cap)


def join_kernel(
    rows, cols, frames, count_ref, sample_ref, acc_ref, prev_ref, next_ref, onehot_ref, e_ref, out_ref, grid_ref
):
    count = scalar_of(count_ref)
    sample = scalar_of(sample_ref)
    area = rows * cols
    first = lax.axis_index("head") * frames
    chans = acc_ref.shape[1]
    for f in range(frames):
        part = acc_ref[f * area : (f + 1) * area, :]
        if f == 0:
            part = part + prev_ref[...]
        if f == frames - 1:
            part = part + next_ref[...]
        grid_ref[f * area : (f + 1) * area, :] = jnp.where(first + f < count, part, 0.0)
    pieces = [[None] * 2 for _ in range(2)]
    for odd in range(2):
        half = grid_ref[pl.ds(odd, frames * area // 2, stride=2), :]
        half = half.reshape(frames * rows // 2, 2, cols // 2, chans)
        for i in range(2):
            pieces[i][odd] = half[:, i].reshape(frames * area // 4, chans)
    tokens = frames * area // 4
    patches = jnp.concatenate(
        [pieces[0][0], pieces[0][1], pieces[1][0], pieces[1][1]], axis=1
    ).astype(jnp.bfloat16)
    model = e_ref.shape[1]
    col_tile = 256
    total = None
    for n in range(0, model, col_tile):
        part = jnp.dot(patches, e_ref[:, n : n + col_tile], preferred_element_type=jnp.float32)
        squares = part * part
        both = squares[:, :LANES] + squares[:, LANES:]
        total = both if total is None else total + both
    scale = lax.rsqrt(jnp.sum(total, axis=-1, keepdims=True) * (1.0 / model) + epsilon)
    high = scale.astype(jnp.bfloat16).astype(jnp.float32)
    frame = first + lax.broadcasted_iota(jnp.int32, (tokens, LANES), 0) // (area // 4)
    lane = lax.broadcasted_iota(jnp.int32, (tokens, LANES), 1)
    label = jnp.where(frame < count, sample + 1, 0).astype(jnp.float32)
    notes = jnp.where(lane == 0, label, jnp.where(lane == 1, high, jnp.where(lane == 2, scale - high, 0.0)))
    patches = jnp.concatenate([patches, notes.astype(jnp.bfloat16)], axis=1)
    out_ref[...] = jnp.dot(onehot_ref[...], patches, preferred_element_type=jnp.float32).astype(
        jnp.bfloat16
    )


def fold_kernel(e_hbm, w_hbm, fold_ref, e_ref, w_ref, sems):
    feats = e_ref.shape[0]
    width = w_ref.shape[2]
    loads = [pltpu.make_async_copy(e_hbm, e_ref, sems.at[3])]
    for m in range(3):
        loads.append(pltpu.make_async_copy(w_hbm.at[m], w_ref.at[m], sems.at[m]))
    for load in loads:
        load.start()
    loads[0].wait()
    col_tile = 256
    for m in range(3):
        loads[1 + m].wait()
        for n in range(0, width, col_tile):
            cols = slice(n, n + col_tile)
            product = jnp.dot(e_ref[...], w_ref[m, :, cols], preferred_element_type=jnp.float32)
            if m == 0:
                product = product * HDIM ** (-0.5)
            high = product.astype(jnp.bfloat16)
            fold_ref[m, :feats, cols] = high
            fold_ref[m, feats:, cols] = (product - high.astype(jnp.float32)).astype(jnp.bfloat16)


def bag_kernel(clips, cap, x_ref, fold_ref, out_ref, qkv_ref, m_ref, r_ref, order_ref):
    count_slots = x_ref.shape[0]
    feats = x_ref.shape[1] - LANES
    width = fold_ref.shape[2]
    clip_rows = count_slots // clips

    for c in range(clips):
        note = x_ref[c * clip_rows : (c + 1) * clip_rows, feats : feats + LANES].astype(jnp.float32)
        order_ref[clips + c] = jnp.max(note[:, :1]).astype(jnp.int32)
    starts = [jnp.int32(0)]
    for s in range(SAMPLES):

        def keep_clip(c, at):
            hit = order_ref[clips + c] == s + 1

            @pl.when(hit)
            def _():
                order_ref[at] = c

            return at + hit.astype(jnp.int32)

        starts.append(lax.fori_loop(0, clips, keep_clip, starts[-1]))

    col_tile = 256
    patch = x_ref[:, :feats]
    notes = x_ref[:, feats:].astype(jnp.float32)
    scale = jnp.broadcast_to(notes[:, 1:2] + notes[:, 2:3], (count_slots, col_tile))
    twice = jnp.concatenate([patch, patch], axis=1)
    for m in range(3):
        for n in range(0, width, col_tile):
            part = jnp.dot(twice, fold_ref[m, :, n : n + col_tile], preferred_element_type=jnp.float32)
            qkv_ref[m, :, n : n + col_tile] = (part * scale).astype(jnp.bfloat16)

    out_ref[...] = jnp.zeros_like(out_ref)
    tile = 2 * clip_rows
    lane = lax.broadcasted_iota(jnp.int32, (tile, LANES), 1)
    low = lane < HDIM
    pairs = width // LANES
    ones = jnp.ones((tile, LANES), jnp.bfloat16)
    pick = (lax.broadcasted_iota(jnp.int32, (8, LANES), 1) == 0).astype(jnp.float32).astype(jnp.bfloat16)
    key_at = lax.broadcasted_iota(jnp.int32, (1, tile), 1)

    def two(ref, a, b, *at):
        return jnp.concatenate(
            [
                ref[(*at[:-1], pl.ds(pl.multiple_of(a * clip_rows, 16), clip_rows), at[-1])],
                ref[(*at[:-1], pl.ds(pl.multiple_of(b * clip_rows, 16), clip_rows), at[-1])],
            ],
            axis=0,
        )

    for s in range(SAMPLES):
        begin, size = starts[s], starts[s + 1] - starts[s]
        tiles = (size + 1) // 2

        def members(i):
            second = 2 * i + 1 < size
            return (
                order_ref[begin + 2 * i],
                order_ref[begin + 2 * i + second.astype(jnp.int32)],
                second,
            )

        def bias_of(a, b, second):
            label = lax.dot_general(
                pick,
                two(x_ref, a, b, slice(feats, feats + LANES)),
                (((1,), (1,)), ((), ())),
                preferred_element_type=jnp.float32,
            )[:1]
            limit = jnp.where(second, tile, clip_rows)
            good = jnp.logical_and(label == s + 1.0, key_at < limit)
            return jnp.where(good, 0.0, far_below)

        def scores_of(pair, half, query, a, b, bias):
            cols = slice(pair * LANES, (pair + 1) * LANES)
            keys = two(qkv_ref, a, b, 1, cols)
            one = jnp.where(low if half == 0 else jnp.logical_not(low), query, jnp.zeros_like(query))
            return (
                lax.dot_general(one, keys, (((1,), (1,)), ((), ())), preferred_element_type=jnp.float32)
                + bias
            )

        def mix(pair, shifted, a, b):
            cols = slice(pair * LANES, (pair + 1) * LANES)
            values = jnp.concatenate([two(qkv_ref, a, b, 2, cols), ones], axis=1)
            return jnp.dot(shifted.astype(jnp.bfloat16), values, preferred_element_type=jnp.float32)

        def store(pair, a, b, results):
            cols = slice(pair * LANES, (pair + 1) * LANES)
            heads = [r[:, :LANES] / r[:, LANES:] for r in results]
            mixed = jnp.where(low, heads[0], heads[1])
            for at, clip in ((clip_rows, b), (0, a)):
                for f in range(clip_rows // cap):
                    piece = mixed[at + f * cap : at + (f + 1) * cap]
                    out_ref[f * clips + clip, :, cols] = piece.astype(jnp.bfloat16)

        def query_tile(i, carry):
            qa, qb, _ = members(i)

            @pl.when(tiles == 1)
            def _():
                ka, kb, second = members(0)
                bias = bias_of(ka, kb, second)
                for pair in range(pairs):
                    query = two(qkv_ref, qa, qb, 0, slice(pair * LANES, (pair + 1) * LANES))
                    results = []
                    for half in range(2):
                        scores = scores_of(pair, half, query, ka, kb, bias)
                        top = jnp.max(scores, axis=-1, keepdims=True)
                        results.append(mix(pair, jnp.exp(scores - top), ka, kb))
                    store(pair, qa, qb, results)

            @pl.when(tiles > 1)
            def _():
                for h in range(2 * pairs):
                    m_ref[h] = jnp.full((tile, LANES), far_below, jnp.float32)
                    r_ref[h] = jnp.zeros((tile, 2 * LANES), jnp.float32)

                def key_tile(j, inner):
                    ka, kb, second = members(j)
                    bias = bias_of(ka, kb, second)
                    for pair in range(pairs):
                        query = two(qkv_ref, qa, qb, 0, slice(pair * LANES, (pair + 1) * LANES))
                        for half in range(2):
                            h = 2 * pair + half
                            scores = scores_of(pair, half, query, ka, kb, bias)
                            old = m_ref[h][:, :1]
                            top = jnp.maximum(old, jnp.max(scores, axis=-1, keepdims=True))
                            r_ref[h] = r_ref[h] * jnp.exp(old - top) + mix(
                                pair, jnp.exp(scores - top), ka, kb
                            )
                            m_ref[h] = jnp.broadcast_to(top, (tile, LANES))
                    return inner

                lax.fori_loop(0, tiles, key_tile, 0)
                for pair in range(pairs):
                    store(pair, qa, qb, [r_ref[2 * pair], r_ref[2 * pair + 1]])

            return carry

        lax.fori_loop(0, tiles, query_tile, 0)


def collect_kernel(frames, heads, count_ref, onehot_ref, recv_ref, out_ref):
    count = scalar_of(count_ref)
    place = lax.axis_index("head")
    slots, tokens = onehot_ref.shape
    frame = place * frames + lax.broadcasted_iota(jnp.int32, (slots, tokens), 1) // (tokens // frames)
    onehot = jnp.where(frame < count, onehot_ref[...], jnp.zeros((), jnp.bfloat16))
    width = recv_ref.shape[1]
    for h in range(heads):
        picked = lax.dot_general(
            onehot,
            recv_ref[h * slots : (h + 1) * slots, :],
            (((0,), (0,)), ((), ())),
            preferred_element_type=jnp.float32,
        )
        out_ref[:, h * width : (h + 1) * width] = picked.astype(jnp.bfloat16)


def shards(latents, frame_counts, routes, samples, conv_weight, embed_weight, qkv_weight):
    frames_dev, rows, cols, depth = latents.shape[1:]
    heads_dev = lax.axis_size("head")
    bags = lax.axis_size("bag")
    area = rows * cols
    tok_dev = frames_dev * area // 4
    cap = 3 * tok_dev // (2 * bags)
    slots = bags * cap
    local_width = qkv_weight.shape[2]
    chans = conv_weight.shape[2]

    tile = latents.reshape(frames_dev * area, depth)
    count = frame_counts.reshape(1, 1)
    edge = jax.ShapeDtypeStruct((area, chans), jnp.float32)
    upward, downward = pl.pallas_call(
        functools.partial(edge_kernel, rows, cols, frames_dev),
        out_shape=(edge, edge),
        in_specs=[VMEM, ANY, ANY],
        out_specs=(VMEM, VMEM),
        scratch_shapes=[
            pltpu.VMEM(tile.shape, jnp.bfloat16),
            pltpu.VMEM(conv_weight.shape, jnp.bfloat16),
            pltpu.SemaphoreType.DMA((2,)),
        ],
        cost_estimate=pl.CostEstimate(flops=600000000, bytes_accessed=4500000, transcendentals=0),
        name="edge",
    )(count, tile, conv_weight)
    ends = heads_dev - 1
    from_prev = lax.ppermute(upward, "head", [(i, i + 1) for i in range(ends)])
    from_next = lax.ppermute(downward, "head", [(i + 1, i) for i in range(ends)])

    route_rows = routes[:, 0].reshape(heads_dev, tok_dev)
    row_width = 4 * chans + LANES
    acc, onehot = pl.pallas_call(
        functools.partial(own_kernel, bags, cap, rows, cols, frames_dev),
        out_shape=(
            jax.ShapeDtypeStruct((frames_dev * area, chans), jnp.float32),
            jax.ShapeDtypeStruct((slots, tok_dev), jnp.bfloat16),
        ),
        in_specs=[VMEM, VMEM, VMEM, VMEM],
        out_specs=(VMEM, VMEM),
        compiler_params=limit(16),
        cost_estimate=pl.CostEstimate(flops=1200000000, bytes_accessed=4500000, transcendentals=0),
        name="own",
    )(count, tile, conv_weight, route_rows)
    outgoing = pl.pallas_call(
        functools.partial(join_kernel, rows, cols, frames_dev),
        out_shape=jax.ShapeDtypeStruct((slots, row_width), jnp.bfloat16),
        in_specs=[VMEM] * 7,
        out_specs=VMEM,
        scratch_shapes=[pltpu.VMEM((frames_dev * area, chans), jnp.float32)],
        compiler_params=limit(16),
        cost_estimate=pl.CostEstimate(flops=300000000, bytes_accessed=3000000, transcendentals=0),
        name="join",
    )(count, samples.reshape(heads_dev, tok_dev), acc, from_prev, from_next, onehot, embed_weight)

    arrived = lax.all_to_all(
        outgoing.reshape(bags, cap, row_width), "bag", split_axis=0, concat_axis=0, tiled=True
    )
    folded = pl.pallas_call(
        fold_kernel,
        out_shape=jax.ShapeDtypeStruct((3, 2 * embed_weight.shape[0], local_width), jnp.bfloat16),
        in_specs=[ANY, ANY],
        out_specs=VMEM,
        scratch_shapes=[
            pltpu.VMEM(embed_weight.shape, jnp.bfloat16),
            pltpu.VMEM(qkv_weight.shape, jnp.bfloat16),
            pltpu.SemaphoreType.DMA((4,)),
        ],
        compiler_params=limit(FOLD_LIMIT),
        cost_estimate=pl.CostEstimate(flops=3300000000, bytes_accessed=14000000, transcendentals=0),
        name="fold",
    )(embed_weight, qkv_weight)
    count_slots = heads_dev * slots
    gathered = lax.all_gather(arrived, "head", axis=1, tiled=True).reshape(count_slots, row_width)

    pair_rows = 2 * heads_dev * cap
    heads_here = local_width // HDIM
    attended = pl.pallas_call(
        functools.partial(bag_kernel, bags, cap),
        out_shape=jax.ShapeDtypeStruct((heads_dev * bags, cap, local_width), jnp.bfloat16),
        in_specs=[VMEM, VMEM],
        out_specs=VMEM,
        scratch_shapes=[
            pltpu.VMEM((3, count_slots, local_width), jnp.bfloat16),
            pltpu.VMEM((heads_here, pair_rows, LANES), jnp.float32),
            pltpu.VMEM((heads_here, pair_rows, 2 * LANES), jnp.float32),
            pltpu.SMEM((2 * bags,), jnp.int32),
        ],
        compiler_params=limit(28),
        cost_estimate=pl.CostEstimate(flops=3000000000, bytes_accessed=5000000, transcendentals=1200000),
        name="bag",
    )(gathered, folded)
    received = lax.all_to_all(attended, ("head", "bag"), split_axis=0, concat_axis=0, tiled=True)
    return pl.pallas_call(
        functools.partial(collect_kernel, frames_dev, heads_dev),
        out_shape=jax.ShapeDtypeStruct((tok_dev, heads_dev * local_width), jnp.bfloat16),
        in_specs=[VMEM, VMEM, VMEM],
        out_specs=VMEM,
        compiler_params=limit(16),
        name="collect",
    )(count, onehot, received.reshape(count_slots, local_width))


def solution(mesh):
    placed = (
        P("bag", "head", None, None, None),
        P("bag"),
        P("bag", None),
        P("bag"),
        P(),
        P(),
        P(None, None, "head"),
    )
    return jax.shard_map(
        shards, mesh=mesh, in_specs=placed, out_specs=P(("bag", "head"), None), check_vma=False
    )
```

```python
import functools
import jax
import jax.numpy as jnp
from jax import lax
from jax.experimental import pallas as pl
from jax.experimental.pallas import tpu as pltpu
from jax.sharding import PartitionSpec as P

HDIM = 64
TAPS = 3
SAMPLES = 4
LANES = 128

epsilon = 1e-06
far_below = -1e30

VMEM = pl.BlockSpec(memory_space=pltpu.VMEM)
ANY = pl.BlockSpec(memory_space=pl.ANY)
EDGE_LIMIT = 60


def limit(mib):
    return pltpu.CompilerParams(vmem_limit_bytes=mib << 20)


def slot_of(route_row, bags, cap, stride):
    tokens = route_row.shape[1]
    bag_ids = lax.broadcasted_iota(jnp.int32, (bags, tokens), 0)
    onehot = (bag_ids == route_row).astype(jnp.float32)
    before = (
        lax.broadcasted_iota(jnp.int32, (tokens, tokens), 0)
        < lax.broadcasted_iota(jnp.int32, (tokens, tokens), 1)
    )
    earlier = jnp.dot(
        onehot.astype(jnp.bfloat16),
        before.astype(jnp.float32).astype(jnp.bfloat16),
        preferred_element_type=jnp.float32,
    )
    rank = jnp.sum(earlier * onehot, axis=0, keepdims=True).astype(jnp.int32)
    return route_row * stride + rank


def onehot_of(slot, slots):
    slot_ids = lax.broadcasted_iota(jnp.int32, (slots, slot.shape[1]), 0)
    return (slot_ids == slot).astype(jnp.float32).astype(jnp.bfloat16)


def combine(products, rows, cols):
    chans = products[0].shape[1]
    blank = jnp.zeros((cols, chans), jnp.float32)
    area = rows * cols
    column = lax.broadcasted_iota(jnp.int32, (area, chans), 0) % cols
    total = None
    for e in range(TAPS):
        up, mid, down = products[e], products[TAPS + e], products[2 * TAPS + e]
        merged = (
            mid
            + jnp.concatenate([blank, up[: area - cols]], axis=0)
            + jnp.concatenate([down[cols:], blank], axis=0)
        )
        if e == 0:
            merged = jnp.where(column == 0, 0.0, pltpu.roll(merged, 1, axis=0))
        elif e == 2:
            merged = jnp.where(column == cols - 1, 0.0, pltpu.roll(merged, area - 1, axis=0))
        total = merged if total is None else total + merged
    return total


def plane_products(pieces, w_ref):
    plane = TAPS * TAPS
    chans = w_ref.shape[2]
    stacked = pieces[0][1] if len(pieces) == 1 else jnp.concatenate([x for _, x in pieces], axis=1)
    products = []
    for p in range(0, plane, 2):
        pair = []
        for q in range(p, min(p + 2, plane)):
            taps = [w_ref[plane * t + q] for t, _ in pieces]
            pair.append(taps[0] if len(taps) == 1 else jnp.concatenate(taps, axis=0))
        weight = pair[0] if len(pair) == 1 else jnp.concatenate(pair, axis=1)
        value = jnp.dot(stacked, weight, preferred_element_type=jnp.float32)
        for q in range(len(pair)):
            products.append(value[:, q * chans : (q + 1) * chans])
    return products


def scalar_of(ref):
    return jnp.max(ref[...])


def edge_kernel(rows, cols, frames, count_ref, x_hbm, w_hbm, up_ref, down_ref, x_ref, w_ref, sems):
    area = rows * cols
    plane = TAPS * TAPS
    jobs = ((up_ref, frames - 1, 0), (down_ref, 0, 2))
    loads = []
    for i, (_, f, tap) in enumerate(jobs):
        loads.append(
            (
                pltpu.make_async_copy(
                    x_hbm.at[pl.ds(f * area, area)], x_ref.at[pl.ds(i * area, area)], sems.at[2 * i]
                ),
                pltpu.make_async_copy(
                    w_hbm.at[pl.ds(tap * plane, plane)], w_ref.at[pl.ds(i * plane, plane)], sems.at[2 * i + 1]
                ),
            )
        )
    for pair in loads:
        for load in pair:
            load.start()
    count = scalar_of(count_ref)
    first = lax.axis_index("head") * frames
    for i, (out_ref, f, _) in enumerate(jobs):
        for load in loads[i]:
            load.wait()
        value = x_ref[i * area : (i + 1) * area, :]
        value = jnp.where(first + f < count, value, jnp.zeros_like(value))
        out_ref[...] = combine(plane_products([(i, value)], w_ref), rows, cols)


def own_kernel(bags, cap, rows, cols, frames, count_ref, x_ref, w_ref, route_ref, acc_ref, onehot_ref):
    count = scalar_of(count_ref)
    place = lax.axis_index("head")
    area = rows * cols
    first = place * frames
    inputs = []
    for f in range(frames):
        value = x_ref[f * area : (f + 1) * area, :]
        inputs.append(jnp.where(first + f < count, value, jnp.zeros_like(value)))
    for f in range(frames):
        pieces = [(t, inputs[f + t - 1]) for t in range(TAPS) if 0 <= f + t - 1 < frames]
        acc_ref[f * area : (f + 1) * area, :] = combine(plane_products(pieces, w_ref), rows, cols)
    route_row = route_ref[pl.ds(place, 1), :]
    onehot_ref[...] = onehot_of(slot_of(route_row, bags, cap, cap), bags * cap)


def join_kernel(
    rows, cols, frames, count_ref, sample_ref, acc_ref, prev_ref, next_ref, onehot_ref, e_ref, out_ref, grid_ref
):
    count = scalar_of(count_ref)
    sample = scalar_of(sample_ref)
    area = rows * cols
    first = lax.axis_index("head") * frames
    chans = acc_ref.shape[1]
    for f in range(frames):
        part = acc_ref[f * area : (f + 1) * area, :]
        if f == 0:
            part = part + prev_ref[...]
        if f == frames - 1:
            part = part + next_ref[...]
        grid_ref[f * area : (f + 1) * area, :] = jnp.where(first + f < count, part, 0.0)
    pieces = [[None] * 2 for _ in range(2)]
    for odd in range(2):
        half = grid_ref[pl.ds(odd, frames * area // 2, stride=2), :]
        half = half.reshape(frames * rows // 2, 2, cols // 2, chans)
        for i in range(2):
            pieces[i][odd] = half[:, i].reshape(frames * area // 4, chans)
    tokens = frames * area // 4
    patches = jnp.concatenate(
        [pieces[0][0], pieces[0][1], pieces[1][0], pieces[1][1]], axis=1
    ).astype(jnp.bfloat16)
    model = e_ref.shape[1]
    col_tile = 256
    total = None
    for n in range(0, model, col_tile):
        part = jnp.dot(patches, e_ref[:, n : n + col_tile], preferred_element_type=jnp.float32)
        squares = part * part
        both = squares[:, :LANES] + squares[:, LANES:]
        total = both if total is None else total + both
    scale = lax.rsqrt(jnp.sum(total, axis=-1, keepdims=True) * (1.0 / model) + epsilon)
    high = scale.astype(jnp.bfloat16).astype(jnp.float32)
    frame = first + lax.broadcasted_iota(jnp.int32, (tokens, LANES), 0) // (area // 4)
    lane = lax.broadcasted_iota(jnp.int32, (tokens, LANES), 1)
    label = jnp.where(frame < count, sample + 1, 0).astype(jnp.float32)
    notes = jnp.where(lane == 0, label, jnp.where(lane == 1, high, jnp.where(lane == 2, scale - high, 0.0)))
    patches = jnp.concatenate([patches, notes.astype(jnp.bfloat16)], axis=1)
    out_ref[...] = jnp.dot(onehot_ref[...], patches, preferred_element_type=jnp.float32).astype(
        jnp.bfloat16
    )


def fold_kernel(e_ref, w_ref, after_ref, fold_ref):
    feats = e_ref.shape[0]
    width = w_ref.shape[2]
    col_tile = 256
    for m in range(3):
        for n in range(0, width, col_tile):
            cols = slice(n, n + col_tile)
            product = jnp.dot(e_ref[...], w_ref[m, :, cols], preferred_element_type=jnp.float32)
            if m == 0:
                product = product * HDIM ** (-0.5)
            high = product.astype(jnp.bfloat16)
            fold_ref[m, :feats, cols] = high
            fold_ref[m, feats:, cols] = (product - high.astype(jnp.float32)).astype(jnp.bfloat16)


def bag_kernel(clips, cap, masks, *refs):
    pieces, (fold_ref, out_ref, qkv_ref, note_ref, m_ref, r_ref, order_ref) = refs[: len(masks)], refs[len(masks) :]
    place = lax.axis_index("head")
    slots = pieces[0].shape[0]
    feats = pieces[0].shape[1] - LANES
    width = fold_ref.shape[2]
    clip_rows = len(masks) * cap
    count_slots = clips * clip_rows

    def by_clip(value, c):
        return jnp.concatenate(
            [value[j * slots + c * cap : j * slots + (c + 1) * cap] for j in range(len(masks))], axis=0
        )

    notes = jnp.concatenate([ref[:, feats:].astype(jnp.float32) for ref in pieces], axis=0)
    for c in range(clips):
        note = by_clip(notes, c)
        note_ref[c * clip_rows : (c + 1) * clip_rows, :] = note.astype(jnp.bfloat16)
        order_ref[clips + c] = jnp.max(note[:, :1]).astype(jnp.int32)
    starts = [jnp.int32(0)]
    for s in range(SAMPLES):

        def keep_clip(c, at):
            hit = order_ref[clips + c] == s + 1

            @pl.when(hit)
            def _():
                order_ref[at] = c

            return at + hit.astype(jnp.int32)

        starts.append(lax.fori_loop(0, clips, keep_clip, starts[-1]))

    col_tile = 256
    patch = jnp.concatenate([ref[:, :feats] for ref in pieces], axis=0)
    scale = jnp.broadcast_to(notes[:, 1:2] + notes[:, 2:3], (count_slots, col_tile))
    twice = jnp.concatenate([patch, patch], axis=1)
    for m in range(3):
        for n in range(0, width, col_tile):
            part = jnp.dot(twice, fold_ref[m, :, n : n + col_tile], preferred_element_type=jnp.float32)
            part = part * scale
            for c in range(clips):
                qkv_ref[m, c * clip_rows : (c + 1) * clip_rows, n : n + col_tile] = by_clip(part, c).astype(
                    jnp.bfloat16
                )

    out_ref[...] = jnp.zeros_like(out_ref)
    tile = 2 * clip_rows
    lane = lax.broadcasted_iota(jnp.int32, (tile, LANES), 1)
    low = lane < HDIM
    pairs = width // LANES
    ones = jnp.ones((tile, LANES), jnp.bfloat16)
    pick = (lax.broadcasted_iota(jnp.int32, (8, LANES), 1) == 0).astype(jnp.float32).astype(jnp.bfloat16)
    key_at = lax.broadcasted_iota(jnp.int32, (1, tile), 1)

    def two(ref, a, b, *at):
        return jnp.concatenate(
            [
                ref[(*at[:-1], pl.ds(pl.multiple_of(a * clip_rows, 16), clip_rows), at[-1])],
                ref[(*at[:-1], pl.ds(pl.multiple_of(b * clip_rows, 16), clip_rows), at[-1])],
            ],
            axis=0,
        )

    for s in range(SAMPLES):
        begin, size = starts[s], starts[s + 1] - starts[s]
        tiles = (size + 1) // 2

        def members(i):
            second = 2 * i + 1 < size
            return (
                order_ref[begin + 2 * i],
                order_ref[begin + 2 * i + second.astype(jnp.int32)],
                second,
            )

        def bias_of(a, b, second):
            label = lax.dot_general(
                pick,
                two(note_ref, a, b, slice(0, LANES)),
                (((1,), (1,)), ((), ())),
                preferred_element_type=jnp.float32,
            )[:1]
            limit = jnp.where(second, tile, clip_rows)
            good = jnp.logical_and(label == s + 1.0, key_at < limit)
            return jnp.where(good, 0.0, far_below)

        def scores_of(pair, half, query, a, b, bias):
            cols = slice(pair * LANES, (pair + 1) * LANES)
            keys = two(qkv_ref, a, b, 1, cols)
            one = jnp.where(low if half == 0 else jnp.logical_not(low), query, jnp.zeros_like(query))
            return (
                lax.dot_general(one, keys, (((1,), (1,)), ((), ())), preferred_element_type=jnp.float32)
                + bias
            )

        def mix(pair, shifted, a, b):
            cols = slice(pair * LANES, (pair + 1) * LANES)
            values = jnp.concatenate([two(qkv_ref, a, b, 2, cols), ones], axis=1)
            return jnp.dot(shifted.astype(jnp.bfloat16), values, preferred_element_type=jnp.float32)

        def store(pair, a, b, results):
            cols = slice(pair * LANES, (pair + 1) * LANES)
            heads = [r[:, :LANES] / r[:, LANES:] for r in results]
            mixed = jnp.where(low, heads[0], heads[1])
            for at, clip in ((clip_rows, b), (0, a)):
                for j, mask in enumerate(masks):
                    piece = mixed[at + j * cap : at + (j + 1) * cap]
                    out_ref[jnp.bitwise_xor(place, mask) * clips + clip, :, cols] = piece.astype(jnp.bfloat16)

        def query_tile(i, carry):
            qa, qb, _ = members(i)

            @pl.when(tiles == 1)
            def _():
                ka, kb, second = members(0)
                bias = bias_of(ka, kb, second)
                for pair in range(pairs):
                    query = two(qkv_ref, qa, qb, 0, slice(pair * LANES, (pair + 1) * LANES))
                    results = []
                    for half in range(2):
                        scores = scores_of(pair, half, query, ka, kb, bias)
                        top = jnp.max(scores, axis=-1, keepdims=True)
                        results.append(mix(pair, jnp.exp(scores - top), ka, kb))
                    store(pair, qa, qb, results)

            @pl.when(tiles > 1)
            def _():
                for h in range(2 * pairs):
                    m_ref[h] = jnp.full((tile, LANES), far_below, jnp.float32)
                    r_ref[h] = jnp.zeros((tile, 2 * LANES), jnp.float32)

                def key_tile(j, inner):
                    ka, kb, second = members(j)
                    bias = bias_of(ka, kb, second)
                    for pair in range(pairs):
                        query = two(qkv_ref, qa, qb, 0, slice(pair * LANES, (pair + 1) * LANES))
                        for half in range(2):
                            h = 2 * pair + half
                            scores = scores_of(pair, half, query, ka, kb, bias)
                            old = m_ref[h][:, :1]
                            top = jnp.maximum(old, jnp.max(scores, axis=-1, keepdims=True))
                            r_ref[h] = r_ref[h] * jnp.exp(old - top) + mix(
                                pair, jnp.exp(scores - top), ka, kb
                            )
                            m_ref[h] = jnp.broadcast_to(top, (tile, LANES))
                    return inner

                lax.fori_loop(0, tiles, key_tile, 0)
                for pair in range(pairs):
                    store(pair, qa, qb, [r_ref[2 * pair], r_ref[2 * pair + 1]])

            return carry

        lax.fori_loop(0, tiles, query_tile, 0)


def collect_kernel(frames, heads, count_ref, onehot_ref, recv_ref, out_ref):
    count = scalar_of(count_ref)
    place = lax.axis_index("head")
    slots, tokens = onehot_ref.shape
    frame = place * frames + lax.broadcasted_iota(jnp.int32, (slots, tokens), 1) // (tokens // frames)
    onehot = jnp.where(frame < count, onehot_ref[...], jnp.zeros((), jnp.bfloat16))
    width = recv_ref.shape[1]
    for h in range(heads):
        picked = lax.dot_general(
            onehot,
            recv_ref[h * slots : (h + 1) * slots, :],
            (((0,), (0,)), ((), ())),
            preferred_element_type=jnp.float32,
        )
        out_ref[:, h * width : (h + 1) * width] = picked.astype(jnp.bfloat16)


def shards(latents, frame_counts, routes, samples, conv_weight, embed_weight, qkv_weight):
    frames_dev, rows, cols, depth = latents.shape[1:]
    heads_dev = lax.axis_size("head")
    bags = lax.axis_size("bag")
    area = rows * cols
    tok_dev = frames_dev * area // 4
    cap = 3 * tok_dev // (2 * bags)
    slots = bags * cap
    local_width = qkv_weight.shape[2]
    chans = conv_weight.shape[2]

    tile = latents.reshape(frames_dev * area, depth)
    count = frame_counts
    edge = jax.ShapeDtypeStruct((area, chans), jnp.float32)
    upward, downward = pl.pallas_call(
        functools.partial(edge_kernel, rows, cols, frames_dev),
        out_shape=(edge, edge),
        in_specs=[VMEM, ANY, ANY],
        out_specs=(VMEM, VMEM),
        scratch_shapes=[
            pltpu.VMEM((2 * area, depth), jnp.bfloat16),
            pltpu.VMEM((2 * TAPS * TAPS, depth, chans), jnp.bfloat16),
            pltpu.SemaphoreType.DMA((4,)),
        ],
        compiler_params=limit(EDGE_LIMIT),
        cost_estimate=pl.CostEstimate(flops=600000000, bytes_accessed=4500000, transcendentals=0),
        name="edge",
    )(count, tile, conv_weight)
    ends = heads_dev - 1
    from_prev = lax.ppermute(upward, "head", [(i, i + 1) for i in range(ends)])
    from_next = lax.ppermute(downward, "head", [(i + 1, i) for i in range(ends)])

    route_rows = routes[:, 0].reshape(heads_dev, tok_dev)
    row_width = 4 * chans + LANES
    acc, onehot = pl.pallas_call(
        functools.partial(own_kernel, bags, cap, rows, cols, frames_dev),
        out_shape=(
            jax.ShapeDtypeStruct((frames_dev * area, chans), jnp.float32),
            jax.ShapeDtypeStruct((slots, tok_dev), jnp.bfloat16),
        ),
        in_specs=[VMEM, VMEM, VMEM, VMEM],
        out_specs=(VMEM, VMEM),
        compiler_params=limit(16),
        cost_estimate=pl.CostEstimate(flops=1200000000, bytes_accessed=4500000, transcendentals=0),
        name="own",
    )(count, tile, conv_weight, route_rows)
    outgoing = pl.pallas_call(
        functools.partial(join_kernel, rows, cols, frames_dev),
        out_shape=jax.ShapeDtypeStruct((slots, row_width), jnp.bfloat16),
        in_specs=[VMEM] * 7,
        out_specs=VMEM,
        scratch_shapes=[pltpu.VMEM((frames_dev * area, chans), jnp.float32)],
        compiler_params=limit(16),
        cost_estimate=pl.CostEstimate(flops=300000000, bytes_accessed=3000000, transcendentals=0),
        name="join",
    )(count, samples.reshape(heads_dev, tok_dev), acc, from_prev, from_next, onehot, embed_weight)

    arrived = lax.all_to_all(
        outgoing.reshape(bags, cap, row_width), "bag", split_axis=0, concat_axis=0, tiled=True
    )
    arrived = arrived.reshape(slots, row_width)
    pieces = {0: arrived}
    bit = heads_dev // 2
    swap = [(i, i ^ bit) for i in range(heads_dev)]
    far = lax.ppermute(arrived, "head", swap)
    folded = pl.pallas_call(
        fold_kernel,
        out_shape=jax.ShapeDtypeStruct((3, 2 * embed_weight.shape[0], local_width), jnp.bfloat16),
        in_specs=[VMEM, VMEM, ANY],
        out_specs=VMEM,
        compiler_params=limit(16),
        cost_estimate=pl.CostEstimate(flops=3300000000, bytes_accessed=14000000, transcendentals=0),
        name="fold",
    )(embed_weight, qkv_weight, arrived)
    far, folded = lax.optimization_barrier((far, folded))
    pieces = {0: arrived, bit: far}
    while bit > 1:
        bit //= 2
        swap = [(i, i ^ bit) for i in range(heads_dev)]
        pieces.update({mask | bit: lax.ppermute(piece, "head", swap) for mask, piece in pieces.items()})
    count_slots = heads_dev * slots
    masks = tuple(pieces)

    pair_rows = 2 * heads_dev * cap
    heads_here = local_width // HDIM
    attended = pl.pallas_call(
        functools.partial(bag_kernel, bags, cap, masks),
        out_shape=jax.ShapeDtypeStruct((heads_dev * bags, cap, local_width), jnp.bfloat16),
        in_specs=[VMEM] * (len(masks) + 1),
        out_specs=VMEM,
        scratch_shapes=[
            pltpu.VMEM((3, count_slots, local_width), jnp.bfloat16),
            pltpu.VMEM((count_slots, LANES), jnp.bfloat16),
            pltpu.VMEM((heads_here, pair_rows, LANES), jnp.float32),
            pltpu.VMEM((heads_here, pair_rows, 2 * LANES), jnp.float32),
            pltpu.SMEM((2 * bags,), jnp.int32),
        ],
        compiler_params=limit(28),
        cost_estimate=pl.CostEstimate(flops=3000000000, bytes_accessed=5000000, transcendentals=1200000),
        name="bag",
    )(*pieces.values(), folded)
    received = lax.all_to_all(attended, ("head", "bag"), split_axis=0, concat_axis=0, tiled=True)
    return pl.pallas_call(
        functools.partial(collect_kernel, frames_dev, heads_dev),
        out_shape=jax.ShapeDtypeStruct((tok_dev, heads_dev * local_width), jnp.bfloat16),
        in_specs=[VMEM, VMEM, VMEM],
        out_specs=VMEM,
        compiler_params=limit(16),
        name="collect",
    )(count, onehot, received.reshape(count_slots, local_width))


def solution(mesh):
    placed = (
        P("bag", "head", None, None, None),
        P("bag"),
        P("bag", None),
        P("bag"),
        P(),
        P(),
        P(None, None, "head"),
    )
    return jax.shard_map(
        shards, mesh=mesh, in_specs=placed, out_specs=P(("bag", "head"), None), check_vma=False
    )
```

```python
import functools
import jax
import jax.numpy as jnp
from jax import lax
from jax.experimental import pallas as pl
from jax.experimental.pallas import tpu as pltpu
from jax.sharding import PartitionSpec as P

HDIM = 64
TAPS = 3
SAMPLES = 4
LANES = 128

epsilon = 1e-06
far_below = -1e30

VMEM = pl.BlockSpec(memory_space=pltpu.VMEM)
ANY = pl.BlockSpec(memory_space=pl.ANY)
EDGE_LIMIT = 60


def limit(mib):
    return pltpu.CompilerParams(vmem_limit_bytes=mib << 20)


def slot_of(route_row, bags, cap, stride):
    tokens = route_row.shape[1]
    bag_ids = lax.broadcasted_iota(jnp.int32, (bags, tokens), 0)
    onehot = (bag_ids == route_row).astype(jnp.float32)
    before = (
        lax.broadcasted_iota(jnp.int32, (tokens, tokens), 0)
        < lax.broadcasted_iota(jnp.int32, (tokens, tokens), 1)
    )
    earlier = jnp.dot(
        onehot.astype(jnp.bfloat16),
        before.astype(jnp.float32).astype(jnp.bfloat16),
        preferred_element_type=jnp.float32,
    )
    rank = jnp.sum(earlier * onehot, axis=0, keepdims=True).astype(jnp.int32)
    return route_row * stride + rank


def onehot_of(slot, slots):
    slot_ids = lax.broadcasted_iota(jnp.int32, (slots, slot.shape[1]), 0)
    return (slot_ids == slot).astype(jnp.float32).astype(jnp.bfloat16)


def combine(products, rows, cols):
    chans = products[0].shape[1]
    blank = jnp.zeros((cols, chans), jnp.float32)
    area = rows * cols
    column = lax.broadcasted_iota(jnp.int32, (area, chans), 0) % cols
    total = None
    for e in range(TAPS):
        up, mid, down = products[e], products[TAPS + e], products[2 * TAPS + e]
        merged = (
            mid
            + jnp.concatenate([blank, up[: area - cols]], axis=0)
            + jnp.concatenate([down[cols:], blank], axis=0)
        )
        if e == 0:
            merged = jnp.where(column == 0, 0.0, pltpu.roll(merged, 1, axis=0))
        elif e == 2:
            merged = jnp.where(column == cols - 1, 0.0, pltpu.roll(merged, area - 1, axis=0))
        total = merged if total is None else total + merged
    return total


def plane_products(pieces, w_ref):
    plane = TAPS * TAPS
    chans = w_ref.shape[2]
    stacked = pieces[0][1] if len(pieces) == 1 else jnp.concatenate([x for _, x in pieces], axis=1)
    products = []
    for p in range(0, plane, 2):
        pair = []
        for q in range(p, min(p + 2, plane)):
            taps = [w_ref[plane * t + q] for t, _ in pieces]
            pair.append(taps[0] if len(taps) == 1 else jnp.concatenate(taps, axis=0))
        weight = pair[0] if len(pair) == 1 else jnp.concatenate(pair, axis=1)
        value = jnp.dot(stacked, weight, preferred_element_type=jnp.float32)
        for q in range(len(pair)):
            products.append(value[:, q * chans : (q + 1) * chans])
    return products


def scalar_of(ref):
    return jnp.max(ref[...])


def edge_kernel(rows, cols, frames, x_hbm, w_hbm, near_ref, far_ref, x_ref, w_ref, sems):
    area = rows * cols
    plane = TAPS * TAPS
    jobs = ((frames - 1, 0), (0, 2))
    loads = []
    for i, (f, tap) in enumerate(jobs):
        loads.append(
            (
                pltpu.make_async_copy(
                    x_hbm.at[pl.ds(f * area, area)], x_ref.at[pl.ds(i * area, area)], sems.at[2 * i]
                ),
                pltpu.make_async_copy(
                    w_hbm.at[pl.ds(tap * plane, plane)], w_ref.at[pl.ds(i * plane, plane)], sems.at[2 * i + 1]
                ),
            )
        )
    for pair in loads:
        for load in pair:
            load.start()
    even = lax.axis_index("head") % 2 == 0
    sums = []
    for i in range(2):
        for load in loads[i]:
            load.wait()
        value = x_ref[i * area : (i + 1) * area, :]
        sums.append(combine(plane_products([(i, value)], w_ref), rows, cols))
    up, down = sums
    near_ref[...] = jnp.where(even, up, down)
    far_ref[...] = jnp.where(even, down, up)


def own_kernel(bags, cap, rows, cols, frames, count_ref, x_ref, w_ref, route_ref, acc_ref, onehot_ref):
    count = scalar_of(count_ref)
    place = lax.axis_index("head")
    area = rows * cols
    first = place * frames
    inputs = []
    for f in range(frames):
        value = x_ref[f * area : (f + 1) * area, :]
        inputs.append(jnp.where(first + f < count, value, jnp.zeros_like(value)))
    for f in range(frames):
        pieces = [(t, inputs[f + t - 1]) for t in range(TAPS) if 0 <= f + t - 1 < frames]
        acc_ref[f * area : (f + 1) * area, :] = combine(plane_products(pieces, w_ref), rows, cols)
    route_row = route_ref[pl.ds(place, 1), :]
    onehot_ref[...] = onehot_of(slot_of(route_row, bags, cap, cap), bags * cap)


def join_kernel(
    rows, cols, frames, count_ref, sample_ref, acc_ref, near_ref, far_ref, onehot_ref, e_ref, out_ref, grid_ref
):
    count = scalar_of(count_ref)
    sample = scalar_of(sample_ref)
    area = rows * cols
    place = lax.axis_index("head")
    even = place % 2 == 0
    first = place * frames
    chans = acc_ref.shape[1]
    near, far = near_ref[...], far_ref[...]
    for f in range(frames):
        part = acc_ref[f * area : (f + 1) * area, :]
        if f == 0:
            before = jnp.logical_and(first > 0, first - 1 < count)
            part = part + jnp.where(before, jnp.where(even, far, near), 0.0)
        if f == frames - 1:
            part = part + jnp.where(first + frames < count, jnp.where(even, near, far), 0.0)
        grid_ref[f * area : (f + 1) * area, :] = jnp.where(first + f < count, part, 0.0)
    pieces = [[None] * 2 for _ in range(2)]
    for odd in range(2):
        half = grid_ref[pl.ds(odd, frames * area // 2, stride=2), :]
        half = half.reshape(frames * rows // 2, 2, cols // 2, chans)
        for i in range(2):
            pieces[i][odd] = half[:, i].reshape(frames * area // 4, chans)
    tokens = frames * area // 4
    patches = jnp.concatenate(
        [pieces[0][0], pieces[0][1], pieces[1][0], pieces[1][1]], axis=1
    ).astype(jnp.bfloat16)
    model = e_ref.shape[1]
    col_tile = 256
    total = None
    for n in range(0, model, col_tile):
        part = jnp.dot(patches, e_ref[:, n : n + col_tile], preferred_element_type=jnp.float32)
        squares = part * part
        both = squares[:, :LANES] + squares[:, LANES:]
        total = both if total is None else total + both
    scale = lax.rsqrt(jnp.sum(total, axis=-1, keepdims=True) * (1.0 / model) + epsilon)
    high = scale.astype(jnp.bfloat16).astype(jnp.float32)
    frame = first + lax.broadcasted_iota(jnp.int32, (tokens, LANES), 0) // (area // 4)
    lane = lax.broadcasted_iota(jnp.int32, (tokens, LANES), 1)
    label = jnp.where(frame < count, sample + 1, 0).astype(jnp.float32)
    notes = jnp.where(lane == 0, label, jnp.where(lane == 1, high, jnp.where(lane == 2, scale - high, 0.0)))
    patches = jnp.concatenate([patches, notes.astype(jnp.bfloat16)], axis=1)
    out_ref[...] = jnp.dot(onehot_ref[...], patches, preferred_element_type=jnp.float32).astype(
        jnp.bfloat16
    )


def fold_kernel(e_ref, w_ref, after_ref, fold_ref):
    feats = e_ref.shape[0]
    width = w_ref.shape[2]
    col_tile = 256
    for m in range(3):
        for n in range(0, width, col_tile):
            cols = slice(n, n + col_tile)
            product = jnp.dot(e_ref[...], w_ref[m, :, cols], preferred_element_type=jnp.float32)
            if m == 0:
                product = product * HDIM ** (-0.5)
            high = product.astype(jnp.bfloat16)
            fold_ref[m, :feats, cols] = high
            fold_ref[m, feats:, cols] = (product - high.astype(jnp.float32)).astype(jnp.bfloat16)


def bag_kernel(clips, cap, masks, *refs):
    pieces, (fold_ref, out_ref, qkv_ref, note_ref, m_ref, r_ref, order_ref) = refs[: len(masks)], refs[len(masks) :]
    place = lax.axis_index("head")
    slots = pieces[0].shape[0]
    feats = pieces[0].shape[1] - LANES
    width = fold_ref.shape[2]
    clip_rows = len(masks) * cap
    count_slots = clips * clip_rows

    def by_clip(value, c):
        return jnp.concatenate(
            [value[j * slots + c * cap : j * slots + (c + 1) * cap] for j in range(len(masks))], axis=0
        )

    notes = jnp.concatenate([ref[:, feats:].astype(jnp.float32) for ref in pieces], axis=0)
    for c in range(clips):
        note = by_clip(notes, c)
        note_ref[c * clip_rows : (c + 1) * clip_rows, :] = note.astype(jnp.bfloat16)
        order_ref[clips + c] = jnp.max(note[:, :1]).astype(jnp.int32)
    starts = [jnp.int32(0)]
    for s in range(SAMPLES):

        def keep_clip(c, at):
            hit = order_ref[clips + c] == s + 1

            @pl.when(hit)
            def _():
                order_ref[at] = c

            return at + hit.astype(jnp.int32)

        starts.append(lax.fori_loop(0, clips, keep_clip, starts[-1]))

    col_tile = 256
    patch = jnp.concatenate([ref[:, :feats] for ref in pieces], axis=0)
    scale = jnp.broadcast_to(notes[:, 1:2] + notes[:, 2:3], (count_slots, col_tile))
    twice = jnp.concatenate([patch, patch], axis=1)
    for m in range(3):
        for n in range(0, width, col_tile):
            part = jnp.dot(twice, fold_ref[m, :, n : n + col_tile], preferred_element_type=jnp.float32)
            part = part * scale
            for c in range(clips):
                qkv_ref[m, c * clip_rows : (c + 1) * clip_rows, n : n + col_tile] = by_clip(part, c).astype(
                    jnp.bfloat16
                )

    out_ref[...] = jnp.zeros_like(out_ref)
    tile = 2 * clip_rows
    lane = lax.broadcasted_iota(jnp.int32, (tile, LANES), 1)
    low = lane < HDIM
    pairs = width // LANES
    ones = jnp.ones((tile, LANES), jnp.bfloat16)
    pick = (lax.broadcasted_iota(jnp.int32, (8, LANES), 1) == 0).astype(jnp.float32).astype(jnp.bfloat16)
    key_at = lax.broadcasted_iota(jnp.int32, (1, tile), 1)

    def two(ref, a, b, *at):
        return jnp.concatenate(
            [
                ref[(*at[:-1], pl.ds(pl.multiple_of(a * clip_rows, 16), clip_rows), at[-1])],
                ref[(*at[:-1], pl.ds(pl.multiple_of(b * clip_rows, 16), clip_rows), at[-1])],
            ],
            axis=0,
        )

    for s in range(SAMPLES):
        begin, size = starts[s], starts[s + 1] - starts[s]
        tiles = (size + 1) // 2

        def members(i):
            second = 2 * i + 1 < size
            return (
                order_ref[begin + 2 * i],
                order_ref[begin + 2 * i + second.astype(jnp.int32)],
                second,
            )

        def bias_of(a, b, second):
            label = lax.dot_general(
                pick,
                two(note_ref, a, b, slice(0, LANES)),
                (((1,), (1,)), ((), ())),
                preferred_element_type=jnp.float32,
            )[:1]
            limit = jnp.where(second, tile, clip_rows)
            good = jnp.logical_and(label == s + 1.0, key_at < limit)
            return jnp.where(good, 0.0, far_below)

        def scores_of(pair, half, query, a, b, bias):
            cols = slice(pair * LANES, (pair + 1) * LANES)
            keys = two(qkv_ref, a, b, 1, cols)
            one = jnp.where(low if half == 0 else jnp.logical_not(low), query, jnp.zeros_like(query))
            return (
                lax.dot_general(one, keys, (((1,), (1,)), ((), ())), preferred_element_type=jnp.float32)
                + bias
            )

        def mix(pair, shifted, a, b):
            cols = slice(pair * LANES, (pair + 1) * LANES)
            values = jnp.concatenate([two(qkv_ref, a, b, 2, cols), ones], axis=1)
            return jnp.dot(shifted.astype(jnp.bfloat16), values, preferred_element_type=jnp.float32)

        def store(pair, a, b, results):
            cols = slice(pair * LANES, (pair + 1) * LANES)
            heads = [r[:, :LANES] / r[:, LANES:] for r in results]
            mixed = jnp.where(low, heads[0], heads[1])
            for at, clip in ((clip_rows, b), (0, a)):
                for j, mask in enumerate(masks):
                    piece = mixed[at + j * cap : at + (j + 1) * cap]
                    out_ref[jnp.bitwise_xor(place, mask) * clips + clip, :, cols] = piece.astype(jnp.bfloat16)

        def query_tile(i, carry):
            qa, qb, _ = members(i)

            @pl.when(tiles == 1)
            def _():
                ka, kb, second = members(0)
                bias = bias_of(ka, kb, second)
                for pair in range(pairs):
                    query = two(qkv_ref, qa, qb, 0, slice(pair * LANES, (pair + 1) * LANES))
                    results = []
                    for half in range(2):
                        scores = scores_of(pair, half, query, ka, kb, bias)
                        top = jnp.max(scores, axis=-1, keepdims=True)
                        results.append(mix(pair, jnp.exp(scores - top), ka, kb))
                    store(pair, qa, qb, results)

            @pl.when(tiles > 1)
            def _():
                for h in range(2 * pairs):
                    m_ref[h] = jnp.full((tile, LANES), far_below, jnp.float32)
                    r_ref[h] = jnp.zeros((tile, 2 * LANES), jnp.float32)

                def key_tile(j, inner):
                    ka, kb, second = members(j)
                    bias = bias_of(ka, kb, second)
                    for pair in range(pairs):
                        query = two(qkv_ref, qa, qb, 0, slice(pair * LANES, (pair + 1) * LANES))
                        for half in range(2):
                            h = 2 * pair + half
                            scores = scores_of(pair, half, query, ka, kb, bias)
                            old = m_ref[h][:, :1]
                            top = jnp.maximum(old, jnp.max(scores, axis=-1, keepdims=True))
                            r_ref[h] = r_ref[h] * jnp.exp(old - top) + mix(
                                pair, jnp.exp(scores - top), ka, kb
                            )
                            m_ref[h] = jnp.broadcast_to(top, (tile, LANES))
                    return inner

                lax.fori_loop(0, tiles, key_tile, 0)
                for pair in range(pairs):
                    store(pair, qa, qb, [r_ref[2 * pair], r_ref[2 * pair + 1]])

            return carry

        lax.fori_loop(0, tiles, query_tile, 0)


def collect_kernel(frames, heads, count_ref, onehot_ref, recv_ref, out_ref):
    count = scalar_of(count_ref)
    place = lax.axis_index("head")
    slots, tokens = onehot_ref.shape
    frame = place * frames + lax.broadcasted_iota(jnp.int32, (slots, tokens), 1) // (tokens // frames)
    onehot = jnp.where(frame < count, onehot_ref[...], jnp.zeros((), jnp.bfloat16))
    width = recv_ref.shape[1]
    for h in range(heads):
        picked = lax.dot_general(
            onehot,
            recv_ref[h * slots : (h + 1) * slots, :],
            (((0,), (0,)), ((), ())),
            preferred_element_type=jnp.float32,
        )
        out_ref[:, h * width : (h + 1) * width] = picked.astype(jnp.bfloat16)


def shards(latents, frame_counts, routes, samples, conv_weight, embed_weight, qkv_weight):
    frames_dev, rows, cols, depth = latents.shape[1:]
    heads_dev = lax.axis_size("head")
    bags = lax.axis_size("bag")
    area = rows * cols
    tok_dev = frames_dev * area // 4
    cap = 3 * tok_dev // (2 * bags)
    slots = bags * cap
    local_width = qkv_weight.shape[2]
    chans = conv_weight.shape[2]

    tile = latents.reshape(frames_dev * area, depth)
    count = frame_counts
    edge = jax.ShapeDtypeStruct((area, chans), jnp.float32)
    near, far = pl.pallas_call(
        functools.partial(edge_kernel, rows, cols, frames_dev),
        out_shape=(edge, edge),
        in_specs=[ANY, ANY],
        out_specs=(VMEM, VMEM),
        scratch_shapes=[
            pltpu.VMEM((2 * area, depth), jnp.bfloat16),
            pltpu.VMEM((2 * TAPS * TAPS, depth, chans), jnp.bfloat16),
            pltpu.SemaphoreType.DMA((4,)),
        ],
        compiler_params=limit(EDGE_LIMIT),
        cost_estimate=pl.CostEstimate(flops=600000000, bytes_accessed=4500000, transcendentals=0),
        name="edge",
    )(tile, conv_weight)
    across = [(i, i + 1) for i in range(1, heads_dev - 1, 2)]
    far = lax.ppermute(far, "head", across + [(j, i) for i, j in across])
    near = lax.ppermute(near, "head", [(i, i ^ 1) for i in range(heads_dev)])

    route_rows = routes[:, 0].reshape(heads_dev, tok_dev)
    row_width = 4 * chans + LANES
    acc, onehot = pl.pallas_call(
        functools.partial(own_kernel, bags, cap, rows, cols, frames_dev),
        out_shape=(
            jax.ShapeDtypeStruct((frames_dev * area, chans), jnp.float32),
            jax.ShapeDtypeStruct((slots, tok_dev), jnp.bfloat16),
        ),
        in_specs=[VMEM, VMEM, VMEM, VMEM],
        out_specs=(VMEM, VMEM),
        compiler_params=limit(16),
        cost_estimate=pl.CostEstimate(flops=1200000000, bytes_accessed=4500000, transcendentals=0),
        name="own",
    )(count, tile, conv_weight, route_rows)
    outgoing = pl.pallas_call(
        functools.partial(join_kernel, rows, cols, frames_dev),
        out_shape=jax.ShapeDtypeStruct((slots, row_width), jnp.bfloat16),
        in_specs=[VMEM] * 7,
        out_specs=VMEM,
        scratch_shapes=[pltpu.VMEM((frames_dev * area, chans), jnp.float32)],
        compiler_params=limit(16),
        cost_estimate=pl.CostEstimate(flops=300000000, bytes_accessed=3000000, transcendentals=0),
        name="join",
    )(count, samples.reshape(heads_dev, tok_dev), acc, near, far, onehot, embed_weight)

    arrived = lax.all_to_all(
        outgoing.reshape(bags, cap, row_width), "bag", split_axis=0, concat_axis=0, tiled=True
    )
    arrived = arrived.reshape(slots, row_width)
    pieces = {0: arrived}
    bit = heads_dev // 2
    swap = [(i, i ^ bit) for i in range(heads_dev)]
    across = lax.ppermute(arrived, "head", swap)
    folded = pl.pallas_call(
        fold_kernel,
        out_shape=jax.ShapeDtypeStruct((3, 2 * embed_weight.shape[0], local_width), jnp.bfloat16),
        in_specs=[VMEM, VMEM, ANY],
        out_specs=VMEM,
        compiler_params=limit(16),
        cost_estimate=pl.CostEstimate(flops=3300000000, bytes_accessed=14000000, transcendentals=0),
        name="fold",
    )(embed_weight, qkv_weight, arrived)
    across, folded = lax.optimization_barrier((across, folded))
    pieces = {0: arrived, bit: across}
    while bit > 1:
        bit //= 2
        swap = [(i, i ^ bit) for i in range(heads_dev)]
        pieces.update({mask | bit: lax.ppermute(piece, "head", swap) for mask, piece in pieces.items()})
    count_slots = heads_dev * slots
    masks = tuple(pieces)

    pair_rows = 2 * heads_dev * cap
    heads_here = local_width // HDIM
    attended = pl.pallas_call(
        functools.partial(bag_kernel, bags, cap, masks),
        out_shape=jax.ShapeDtypeStruct((heads_dev * bags, cap, local_width), jnp.bfloat16),
        in_specs=[VMEM] * (len(masks) + 1),
        out_specs=VMEM,
        scratch_shapes=[
            pltpu.VMEM((3, count_slots, local_width), jnp.bfloat16),
            pltpu.VMEM((count_slots, LANES), jnp.bfloat16),
            pltpu.VMEM((heads_here, pair_rows, LANES), jnp.float32),
            pltpu.VMEM((heads_here, pair_rows, 2 * LANES), jnp.float32),
            pltpu.SMEM((2 * bags,), jnp.int32),
        ],
        compiler_params=limit(28),
        cost_estimate=pl.CostEstimate(flops=3000000000, bytes_accessed=5000000, transcendentals=1200000),
        name="bag",
    )(*pieces.values(), folded)
    received = lax.all_to_all(attended, ("head", "bag"), split_axis=0, concat_axis=0, tiled=True)
    return pl.pallas_call(
        functools.partial(collect_kernel, frames_dev, heads_dev),
        out_shape=jax.ShapeDtypeStruct((tok_dev, heads_dev * local_width), jnp.bfloat16),
        in_specs=[VMEM, VMEM, VMEM],
        out_specs=VMEM,
        compiler_params=limit(16),
        name="collect",
    )(count, onehot, received.reshape(count_slots, local_width))


def solution(mesh):
    placed = (
        P("bag", "head", None, None, None),
        P("bag"),
        P("bag", None),
        P("bag"),
        P(),
        P(),
        P(None, None, "head"),
    )
    return jax.shard_map(
        shards, mesh=mesh, in_specs=placed, out_specs=P(("bag", "head"), None), check_vma=False
    )
```

```python
import functools
import jax
import jax.numpy as jnp
from jax import lax
from jax.experimental import pallas as pl
from jax.experimental.pallas import tpu as pltpu
from jax.sharding import PartitionSpec as P

HDIM = 64
TAPS = 3
SAMPLES = 4
LANES = 128

epsilon = 1e-06
far_below = -1e30

VMEM = pl.BlockSpec(memory_space=pltpu.VMEM)
ANY = pl.BlockSpec(memory_space=pl.ANY)
EDGE_LIMIT = 60


def limit(mib):
    return pltpu.CompilerParams(vmem_limit_bytes=mib << 20)


def slot_of(route_row, bags, cap, stride):
    tokens = route_row.shape[1]
    bag_ids = lax.broadcasted_iota(jnp.int32, (bags, tokens), 0)
    onehot = (bag_ids == route_row).astype(jnp.float32)
    before = (
        lax.broadcasted_iota(jnp.int32, (tokens, tokens), 0)
        < lax.broadcasted_iota(jnp.int32, (tokens, tokens), 1)
    )
    earlier = jnp.dot(
        onehot.astype(jnp.bfloat16),
        before.astype(jnp.float32).astype(jnp.bfloat16),
        preferred_element_type=jnp.float32,
    )
    rank = jnp.sum(earlier * onehot, axis=0, keepdims=True).astype(jnp.int32)
    return route_row * stride + rank


def onehot_of(slot, slots):
    slot_ids = lax.broadcasted_iota(jnp.int32, (slots, slot.shape[1]), 0)
    return (slot_ids == slot).astype(jnp.float32).astype(jnp.bfloat16)


def combine(products, rows, cols):
    chans = products[0].shape[1]
    blank = jnp.zeros((cols, chans), jnp.float32)
    area = rows * cols
    column = lax.broadcasted_iota(jnp.int32, (area, chans), 0) % cols
    total = None
    for e in range(TAPS):
        up, mid, down = products[e], products[TAPS + e], products[2 * TAPS + e]
        merged = (
            mid
            + jnp.concatenate([blank, up[: area - cols]], axis=0)
            + jnp.concatenate([down[cols:], blank], axis=0)
        )
        if e == 0:
            merged = jnp.where(column == 0, 0.0, pltpu.roll(merged, 1, axis=0))
        elif e == 2:
            merged = jnp.where(column == cols - 1, 0.0, pltpu.roll(merged, area - 1, axis=0))
        total = merged if total is None else total + merged
    return total


def plane_products(pieces, w_ref):
    plane = TAPS * TAPS
    chans = w_ref.shape[2]
    stacked = pieces[0][1] if len(pieces) == 1 else jnp.concatenate([x for _, x in pieces], axis=1)
    products = []
    for p in range(0, plane, 2):
        pair = []
        for q in range(p, min(p + 2, plane)):
            taps = [w_ref[plane * t + q] for t, _ in pieces]
            pair.append(taps[0] if len(taps) == 1 else jnp.concatenate(taps, axis=0))
        weight = pair[0] if len(pair) == 1 else jnp.concatenate(pair, axis=1)
        value = jnp.dot(stacked, weight, preferred_element_type=jnp.float32)
        for q in range(len(pair)):
            products.append(value[:, q * chans : (q + 1) * chans])
    return products


def scalar_of(ref):
    return jnp.max(ref[...])


def edge_kernel(rows, cols, frames, x_hbm, w_hbm, near_ref, far_ref, x_ref, w_ref, sems):
    area = rows * cols
    plane = TAPS * TAPS
    jobs = ((frames - 1, 0), (0, 2))
    loads = []
    for i, (f, tap) in enumerate(jobs):
        loads.append(
            (
                pltpu.make_async_copy(
                    x_hbm.at[pl.ds(f * area, area)], x_ref.at[pl.ds(i * area, area)], sems.at[2 * i]
                ),
                pltpu.make_async_copy(
                    w_hbm.at[pl.ds(tap * plane, plane)], w_ref.at[pl.ds(i * plane, plane)], sems.at[2 * i + 1]
                ),
            )
        )
    for pair in loads:
        for load in pair:
            load.start()
    even = lax.axis_index("head") % 2 == 0
    sums = []
    for i in range(2):
        for load in loads[i]:
            load.wait()
        value = x_ref[i * area : (i + 1) * area, :]
        sums.append(combine(plane_products([(i, value)], w_ref), rows, cols))
    up, down = sums
    near_ref[...] = jnp.where(even, up, down)
    far_ref[...] = jnp.where(even, down, up)


def own_kernel(bags, cap, rows, cols, frames, count_ref, x_ref, w_ref, route_ref, acc_ref, onehot_ref):
    count = scalar_of(count_ref)
    place = lax.axis_index("head")
    area = rows * cols
    first = place * frames
    inputs = []
    for f in range(frames):
        value = x_ref[f * area : (f + 1) * area, :]
        inputs.append(jnp.where(first + f < count, value, jnp.zeros_like(value)))
    for f in range(frames):
        pieces = [(t, inputs[f + t - 1]) for t in range(TAPS) if 0 <= f + t - 1 < frames]
        acc_ref[f * area : (f + 1) * area, :] = combine(plane_products(pieces, w_ref), rows, cols)
    route_row = route_ref[pl.ds(place, 1), :]
    onehot_ref[...] = onehot_of(slot_of(route_row, bags, cap, cap), bags * cap)


def join_kernel(
    rows, cols, frames, count_ref, sample_ref, acc_ref, near_ref, far_ref, onehot_ref, e_ref, out_ref, grid_ref
):
    count = scalar_of(count_ref)
    sample = scalar_of(sample_ref)
    area = rows * cols
    place = lax.axis_index("head")
    even = place % 2 == 0
    first = place * frames
    chans = acc_ref.shape[1]
    near, far = near_ref[...], far_ref[...]
    for f in range(frames):
        part = acc_ref[f * area : (f + 1) * area, :]
        if f == 0:
            before = jnp.logical_and(first > 0, first - 1 < count)
            part = part + jnp.where(before, jnp.where(even, far, near), 0.0)
        if f == frames - 1:
            part = part + jnp.where(first + frames < count, jnp.where(even, near, far), 0.0)
        grid_ref[f * area : (f + 1) * area, :] = jnp.where(first + f < count, part, 0.0)
    pieces = [[None] * 2 for _ in range(2)]
    for odd in range(2):
        half = grid_ref[pl.ds(odd, frames * area // 2, stride=2), :]
        half = half.reshape(frames * rows // 2, 2, cols // 2, chans)
        for i in range(2):
            pieces[i][odd] = half[:, i].reshape(frames * area // 4, chans)
    tokens = frames * area // 4
    patches = jnp.concatenate(
        [pieces[0][0], pieces[0][1], pieces[1][0], pieces[1][1]], axis=1
    ).astype(jnp.bfloat16)
    model = e_ref.shape[1]
    col_tile = 256
    total = None
    for n in range(0, model, col_tile):
        part = jnp.dot(patches, e_ref[:, n : n + col_tile], preferred_element_type=jnp.float32)
        squares = part * part
        both = squares[:, :LANES] + squares[:, LANES:]
        total = both if total is None else total + both
    scale = lax.rsqrt(jnp.sum(total, axis=-1, keepdims=True) * (1.0 / model) + epsilon)
    high = scale.astype(jnp.bfloat16).astype(jnp.float32)
    frame = first + lax.broadcasted_iota(jnp.int32, (tokens, LANES), 0) // (area // 4)
    lane = lax.broadcasted_iota(jnp.int32, (tokens, LANES), 1)
    label = jnp.where(frame < count, sample + 1, 0).astype(jnp.float32)
    notes = jnp.where(lane == 0, label, jnp.where(lane == 1, high, jnp.where(lane == 2, scale - high, 0.0)))
    patches = jnp.concatenate([patches, notes.astype(jnp.bfloat16)], axis=1)
    out_ref[...] = jnp.dot(onehot_ref[...], patches, preferred_element_type=jnp.float32).astype(
        jnp.bfloat16
    )


def fold_kernel(e_ref, w_ref, after_ref, fold_ref):
    feats = e_ref.shape[0]
    width = w_ref.shape[2]
    col_tile = 256
    for m in range(3):
        for n in range(0, width, col_tile):
            cols = slice(n, n + col_tile)
            product = jnp.dot(e_ref[...], w_ref[m, :, cols], preferred_element_type=jnp.float32)
            if m == 0:
                product = product * HDIM ** (-0.5)
            high = product.astype(jnp.bfloat16)
            fold_ref[m, :feats, cols] = high
            fold_ref[m, feats:, cols] = (product - high.astype(jnp.float32)).astype(jnp.bfloat16)


def qkv_kernel(*refs):
    pieces, fold_ref, out_ref = refs[:-2], refs[-2], refs[-1]
    for m, at, part in qkv_parts(pieces, fold_ref):
        out_ref[m, :, at : at + part.shape[1]] = part


def qkv_parts(pieces, fold_ref):
    feats = pieces[0].shape[1] - LANES
    col_tile = 256
    patch = jnp.concatenate([ref[:, :feats] for ref in pieces], axis=0)
    notes = jnp.concatenate([ref[:, feats:].astype(jnp.float32) for ref in pieces], axis=0)
    scale = jnp.broadcast_to(notes[:, 1:2] + notes[:, 2:3], (notes.shape[0], col_tile))
    twice = jnp.concatenate([patch, patch], axis=1)
    for m in range(3):
        for n in range(0, fold_ref.shape[2], col_tile):
            part = jnp.dot(twice, fold_ref[m, :, n : n + col_tile], preferred_element_type=jnp.float32)
            yield m, n, part * scale


def bag_kernel(clips, cap, masks, *refs):
    count = len(masks)
    pieces, (near_ref, fold_ref, out_ref, qkv_ref, note_ref, m_ref, r_ref, order_ref) = refs[:count], refs[count:]
    place = lax.axis_index("head")
    slots = pieces[0].shape[0]
    feats = pieces[0].shape[1] - LANES
    width = fold_ref.shape[2]
    clip_rows = count * cap
    half = count // 2

    def by_clip(values, c):
        return jnp.concatenate(
            [value[j * slots + c * cap : j * slots + (c + 1) * cap] for value in values for j in range(half)], axis=0
        )

    notes = [
        jnp.concatenate([ref[:, feats:].astype(jnp.float32) for ref in group], axis=0)
        for group in (pieces[:half], pieces[half:])
    ]
    for c in range(clips):
        note = by_clip(notes, c)
        note_ref[c * clip_rows : (c + 1) * clip_rows, :] = note.astype(jnp.bfloat16)
        order_ref[clips + c] = jnp.max(note[:, :1]).astype(jnp.int32)
    starts = [jnp.int32(0)]
    for s in range(SAMPLES):

        def keep_clip(c, at):
            hit = order_ref[clips + c] == s + 1

            @pl.when(hit)
            def _():
                order_ref[at] = c

            return at + hit.astype(jnp.int32)

        starts.append(lax.fori_loop(0, clips, keep_clip, starts[-1]))

    for m, at, part in qkv_parts(pieces[half:], fold_ref):
        cols = slice(at, at + part.shape[1])
        both = (near_ref[m, :, cols], part)
        for c in range(clips):
            qkv_ref[m, c * clip_rows : (c + 1) * clip_rows, cols] = by_clip(both, c).astype(jnp.bfloat16)

    out_ref[...] = jnp.zeros_like(out_ref)
    tile = 2 * clip_rows
    lane = lax.broadcasted_iota(jnp.int32, (tile, LANES), 1)
    low = lane < HDIM
    pairs = width // LANES
    ones = jnp.ones((tile, LANES), jnp.bfloat16)
    pick = (lax.broadcasted_iota(jnp.int32, (8, LANES), 1) == 0).astype(jnp.float32).astype(jnp.bfloat16)
    key_at = lax.broadcasted_iota(jnp.int32, (1, tile), 1)

    def two(ref, a, b, *at):
        return jnp.concatenate(
            [
                ref[(*at[:-1], pl.ds(pl.multiple_of(a * clip_rows, 16), clip_rows), at[-1])],
                ref[(*at[:-1], pl.ds(pl.multiple_of(b * clip_rows, 16), clip_rows), at[-1])],
            ],
            axis=0,
        )

    for s in range(SAMPLES):
        begin, size = starts[s], starts[s + 1] - starts[s]
        tiles = (size + 1) // 2

        def members(i):
            second = 2 * i + 1 < size
            return (
                order_ref[begin + 2 * i],
                order_ref[begin + 2 * i + second.astype(jnp.int32)],
                second,
            )

        def bias_of(a, b, second):
            label = lax.dot_general(
                pick,
                two(note_ref, a, b, slice(0, LANES)),
                (((1,), (1,)), ((), ())),
                preferred_element_type=jnp.float32,
            )[:1]
            limit = jnp.where(second, tile, clip_rows)
            good = jnp.logical_and(label == s + 1.0, key_at < limit)
            return jnp.where(good, 0.0, far_below)

        def scores_of(pair, half, query, a, b, bias):
            cols = slice(pair * LANES, (pair + 1) * LANES)
            keys = two(qkv_ref, a, b, 1, cols)
            one = jnp.where(low if half == 0 else jnp.logical_not(low), query, jnp.zeros_like(query))
            return (
                lax.dot_general(one, keys, (((1,), (1,)), ((), ())), preferred_element_type=jnp.float32)
                + bias
            )

        def mix(pair, shifted, a, b):
            cols = slice(pair * LANES, (pair + 1) * LANES)
            values = jnp.concatenate([two(qkv_ref, a, b, 2, cols), ones], axis=1)
            return jnp.dot(shifted.astype(jnp.bfloat16), values, preferred_element_type=jnp.float32)

        def store(pair, a, b, results):
            cols = slice(pair * LANES, (pair + 1) * LANES)
            heads = [r[:, :LANES] / r[:, LANES:] for r in results]
            mixed = jnp.where(low, heads[0], heads[1])
            for at, clip in ((clip_rows, b), (0, a)):
                for j, mask in enumerate(masks):
                    piece = mixed[at + j * cap : at + (j + 1) * cap]
                    out_ref[jnp.bitwise_xor(place, mask) * clips + clip, :, cols] = piece.astype(jnp.bfloat16)

        def query_tile(i, carry):
            qa, qb, _ = members(i)

            @pl.when(tiles == 1)
            def _():
                ka, kb, second = members(0)
                bias = bias_of(ka, kb, second)
                for pair in range(pairs):
                    query = two(qkv_ref, qa, qb, 0, slice(pair * LANES, (pair + 1) * LANES))
                    results = []
                    for half in range(2):
                        scores = scores_of(pair, half, query, ka, kb, bias)
                        top = jnp.max(scores, axis=-1, keepdims=True)
                        results.append(mix(pair, jnp.exp(scores - top), ka, kb))
                    store(pair, qa, qb, results)

            @pl.when(tiles > 1)
            def _():
                for h in range(2 * pairs):
                    m_ref[h] = jnp.full((tile, LANES), far_below, jnp.float32)
                    r_ref[h] = jnp.zeros((tile, 2 * LANES), jnp.float32)

                def key_tile(j, inner):
                    ka, kb, second = members(j)
                    bias = bias_of(ka, kb, second)
                    for pair in range(pairs):
                        query = two(qkv_ref, qa, qb, 0, slice(pair * LANES, (pair + 1) * LANES))
                        for half in range(2):
                            h = 2 * pair + half
                            scores = scores_of(pair, half, query, ka, kb, bias)
                            old = m_ref[h][:, :1]
                            top = jnp.maximum(old, jnp.max(scores, axis=-1, keepdims=True))
                            r_ref[h] = r_ref[h] * jnp.exp(old - top) + mix(
                                pair, jnp.exp(scores - top), ka, kb
                            )
                            m_ref[h] = jnp.broadcast_to(top, (tile, LANES))
                    return inner

                lax.fori_loop(0, tiles, key_tile, 0)
                for pair in range(pairs):
                    store(pair, qa, qb, [r_ref[2 * pair], r_ref[2 * pair + 1]])

            return carry

        lax.fori_loop(0, tiles, query_tile, 0)


def collect_kernel(frames, heads, count_ref, onehot_ref, recv_ref, out_ref):
    count = scalar_of(count_ref)
    place = lax.axis_index("head")
    slots, tokens = onehot_ref.shape
    frame = place * frames + lax.broadcasted_iota(jnp.int32, (slots, tokens), 1) // (tokens // frames)
    onehot = jnp.where(frame < count, onehot_ref[...], jnp.zeros((), jnp.bfloat16))
    width = recv_ref.shape[1]
    for h in range(heads):
        picked = lax.dot_general(
            onehot,
            recv_ref[h * slots : (h + 1) * slots, :],
            (((0,), (0,)), ((), ())),
            preferred_element_type=jnp.float32,
        )
        out_ref[:, h * width : (h + 1) * width] = picked.astype(jnp.bfloat16)


def shards(latents, frame_counts, routes, samples, conv_weight, embed_weight, qkv_weight):
    frames_dev, rows, cols, depth = latents.shape[1:]
    heads_dev = lax.axis_size("head")
    bags = lax.axis_size("bag")
    area = rows * cols
    tok_dev = frames_dev * area // 4
    cap = 3 * tok_dev // (2 * bags)
    slots = bags * cap
    local_width = qkv_weight.shape[2]
    chans = conv_weight.shape[2]

    tile = latents.reshape(frames_dev * area, depth)
    count = frame_counts
    edge = jax.ShapeDtypeStruct((area, chans), jnp.float32)
    near, far = pl.pallas_call(
        functools.partial(edge_kernel, rows, cols, frames_dev),
        out_shape=(edge, edge),
        in_specs=[ANY, ANY],
        out_specs=(VMEM, VMEM),
        scratch_shapes=[
            pltpu.VMEM((2 * area, depth), jnp.bfloat16),
            pltpu.VMEM((2 * TAPS * TAPS, depth, chans), jnp.bfloat16),
            pltpu.SemaphoreType.DMA((4,)),
        ],
        compiler_params=limit(EDGE_LIMIT),
        cost_estimate=pl.CostEstimate(flops=600000000, bytes_accessed=4500000, transcendentals=0),
        name="edge",
    )(tile, conv_weight)
    across = [(i, i + 1) for i in range(1, heads_dev - 1, 2)]
    far = lax.ppermute(far, "head", across + [(j, i) for i, j in across])
    near = lax.ppermute(near, "head", [(i, i ^ 1) for i in range(heads_dev)])

    route_rows = routes[:, 0].reshape(heads_dev, tok_dev)
    row_width = 4 * chans + LANES
    acc, onehot = pl.pallas_call(
        functools.partial(own_kernel, bags, cap, rows, cols, frames_dev),
        out_shape=(
            jax.ShapeDtypeStruct((frames_dev * area, chans), jnp.float32),
            jax.ShapeDtypeStruct((slots, tok_dev), jnp.bfloat16),
        ),
        in_specs=[VMEM, VMEM, VMEM, VMEM],
        out_specs=(VMEM, VMEM),
        compiler_params=limit(16),
        cost_estimate=pl.CostEstimate(flops=1200000000, bytes_accessed=4500000, transcendentals=0),
        name="own",
    )(count, tile, conv_weight, route_rows)
    outgoing = pl.pallas_call(
        functools.partial(join_kernel, rows, cols, frames_dev),
        out_shape=jax.ShapeDtypeStruct((slots, row_width), jnp.bfloat16),
        in_specs=[VMEM] * 7,
        out_specs=VMEM,
        scratch_shapes=[pltpu.VMEM((frames_dev * area, chans), jnp.float32)],
        compiler_params=limit(16),
        cost_estimate=pl.CostEstimate(flops=300000000, bytes_accessed=3000000, transcendentals=0),
        name="join",
    )(count, samples.reshape(heads_dev, tok_dev), acc, near, far, onehot, embed_weight)

    arrived = lax.all_to_all(
        outgoing.reshape(bags, cap, row_width), "bag", split_axis=0, concat_axis=0, tiled=True
    )
    arrived = arrived.reshape(slots, row_width)
    pieces = {0: arrived}
    bit = heads_dev // 2
    swap = [(i, i ^ bit) for i in range(heads_dev)]
    across = lax.ppermute(arrived, "head", swap)
    folded = pl.pallas_call(
        fold_kernel,
        out_shape=jax.ShapeDtypeStruct((3, 2 * embed_weight.shape[0], local_width), jnp.bfloat16),
        in_specs=[VMEM, VMEM, ANY],
        out_specs=VMEM,
        compiler_params=limit(16),
        cost_estimate=pl.CostEstimate(flops=3300000000, bytes_accessed=14000000, transcendentals=0),
        name="fold",
    )(embed_weight, qkv_weight, arrived)
    def spread(start, bits):
        found = dict(start)
        for lower in bits:
            pairs = [(i, i ^ lower) for i in range(heads_dev)]
            found.update({mask | lower: lax.ppermute(piece, "head", pairs) for mask, piece in found.items()})
        return found

    lower_bits = [1 << i for i in reversed(range(bit.bit_length() - 1))]
    close = spread({0: arrived}, lower_bits)
    near_qkv = pl.pallas_call(
        qkv_kernel,
        out_shape=jax.ShapeDtypeStruct((3, len(close) * slots, local_width), jnp.float32),
        in_specs=[VMEM] * (len(close) + 1),
        out_specs=VMEM,
        compiler_params=limit(16),
        cost_estimate=pl.CostEstimate(flops=1200000000, bytes_accessed=6000000, transcendentals=0),
        name="near_qkv",
    )(*close.values(), folded)
    across, near_qkv = lax.optimization_barrier((across, near_qkv))
    pieces = dict(close)
    pieces.update(spread({bit: across}, lower_bits))
    count_slots = heads_dev * slots
    masks = tuple(pieces)

    pair_rows = 2 * heads_dev * cap
    heads_here = local_width // HDIM
    attended = pl.pallas_call(
        functools.partial(bag_kernel, bags, cap, masks),
        out_shape=jax.ShapeDtypeStruct((heads_dev * bags, cap, local_width), jnp.bfloat16),
        in_specs=[VMEM] * (len(masks) + 2),
        out_specs=VMEM,
        scratch_shapes=[
            pltpu.VMEM((3, count_slots, local_width), jnp.bfloat16),
            pltpu.VMEM((count_slots, LANES), jnp.bfloat16),
            pltpu.VMEM((heads_here, pair_rows, LANES), jnp.float32),
            pltpu.VMEM((heads_here, pair_rows, 2 * LANES), jnp.float32),
            pltpu.SMEM((2 * bags,), jnp.int32),
        ],
        compiler_params=limit(28),
        cost_estimate=pl.CostEstimate(flops=3000000000, bytes_accessed=5000000, transcendentals=1200000),
        name="bag",
    )(*pieces.values(), near_qkv, folded)
    received = lax.all_to_all(attended, ("head", "bag"), split_axis=0, concat_axis=0, tiled=True)
    return pl.pallas_call(
        functools.partial(collect_kernel, frames_dev, heads_dev),
        out_shape=jax.ShapeDtypeStruct((tok_dev, heads_dev * local_width), jnp.bfloat16),
        in_specs=[VMEM, VMEM, VMEM],
        out_specs=VMEM,
        compiler_params=limit(16),
        name="collect",
    )(count, onehot, received.reshape(count_slots, local_width))


def solution(mesh):
    placed = (
        P("bag", "head", None, None, None),
        P("bag"),
        P("bag", None),
        P("bag"),
        P(),
        P(),
        P(None, None, "head"),
    )
    return jax.shard_map(
        shards, mesh=mesh, in_specs=placed, out_specs=P(("bag", "head"), None), check_vma=False
    )
```

```python
import functools
import jax
import jax.numpy as jnp
from jax import lax
from jax.experimental import pallas as pl
from jax.experimental.pallas import tpu as pltpu
from jax.sharding import PartitionSpec as P

HDIM = 64
TAPS = 3
SAMPLES = 4
LANES = 128

epsilon = 1e-06
far_below = -1e30

VMEM = pl.BlockSpec(memory_space=pltpu.VMEM)
ANY = pl.BlockSpec(memory_space=pl.ANY)
EDGE_LIMIT = 60


def limit(mib):
    return pltpu.CompilerParams(vmem_limit_bytes=mib << 20)


def slot_of(route_row, bags, cap, stride):
    tokens = route_row.shape[1]
    bag_ids = lax.broadcasted_iota(jnp.int32, (bags, tokens), 0)
    onehot = (bag_ids == route_row).astype(jnp.float32)
    before = (
        lax.broadcasted_iota(jnp.int32, (tokens, tokens), 0)
        < lax.broadcasted_iota(jnp.int32, (tokens, tokens), 1)
    )
    earlier = jnp.dot(
        onehot.astype(jnp.bfloat16),
        before.astype(jnp.float32).astype(jnp.bfloat16),
        preferred_element_type=jnp.float32,
    )
    rank = jnp.sum(earlier * onehot, axis=0, keepdims=True).astype(jnp.int32)
    return route_row * stride + rank


def onehot_of(slot, slots):
    slot_ids = lax.broadcasted_iota(jnp.int32, (slots, slot.shape[1]), 0)
    return (slot_ids == slot).astype(jnp.float32).astype(jnp.bfloat16)


def combine(products, rows, cols):
    chans = products[0].shape[1]
    blank = jnp.zeros((cols, chans), jnp.float32)
    area = rows * cols
    column = lax.broadcasted_iota(jnp.int32, (area, chans), 0) % cols
    total = None
    for e in range(TAPS):
        up, mid, down = products[e], products[TAPS + e], products[2 * TAPS + e]
        merged = (
            mid
            + jnp.concatenate([blank, up[: area - cols]], axis=0)
            + jnp.concatenate([down[cols:], blank], axis=0)
        )
        if e == 0:
            merged = jnp.where(column == 0, 0.0, pltpu.roll(merged, 1, axis=0))
        elif e == 2:
            merged = jnp.where(column == cols - 1, 0.0, pltpu.roll(merged, area - 1, axis=0))
        total = merged if total is None else total + merged
    return total


def plane_products(pieces, w_ref):
    plane = TAPS * TAPS
    chans = w_ref.shape[2]
    stacked = pieces[0][1] if len(pieces) == 1 else jnp.concatenate([x for _, x in pieces], axis=1)
    products = []
    for p in range(0, plane, 2):
        pair = []
        for q in range(p, min(p + 2, plane)):
            taps = [w_ref[plane * t + q] for t, _ in pieces]
            pair.append(taps[0] if len(taps) == 1 else jnp.concatenate(taps, axis=0))
        weight = pair[0] if len(pair) == 1 else jnp.concatenate(pair, axis=1)
        value = jnp.dot(stacked, weight, preferred_element_type=jnp.float32)
        for q in range(len(pair)):
            products.append(value[:, q * chans : (q + 1) * chans])
    return products


def scalar_of(ref):
    return jnp.max(ref[...])


def edge_jobs(frames):
    even = lax.axis_index("head") % 2 == 0
    last, zero, two = jnp.int32(frames - 1), jnp.int32(0), jnp.int32(2)
    up, down = (last, zero), (zero, two)
    near = tuple(jnp.where(even, a, b) for a, b in zip(up, down))
    far = tuple(jnp.where(even, b, a) for a, b in zip(up, down))
    return near, far


def edge_kernel(rows, cols, frames, x_hbm, w_hbm, far_ref, x_ref, w_ref, sems):
    area = rows * cols
    plane = TAPS * TAPS
    _, (frame, tap) = edge_jobs(frames)
    loads = [
        pltpu.make_async_copy(x_hbm.at[pl.ds(pl.multiple_of(frame * area, area), area)], x_ref, sems.at[0]),
        pltpu.make_async_copy(w_hbm.at[pl.ds(tap * plane, plane)], w_ref, sems.at[1]),
    ]
    for load in loads:
        load.start()
    for load in loads:
        load.wait()
    far_ref[...] = combine(plane_products([(0, x_ref[...])], w_ref), rows, cols)


def own_kernel(
    bags, cap, rows, cols, frames, count_ref, x_ref, w_ref, route_ref, near_ref, acc_ref, onehot_ref
):
    count = scalar_of(count_ref)
    place = lax.axis_index("head")
    area = rows * cols
    first = place * frames
    (frame, tap), _ = edge_jobs(frames)
    value = x_ref[pl.ds(pl.multiple_of(frame * area, area), area), :]
    near_ref[...] = combine(plane_products([(tap, value)], w_ref), rows, cols)
    inputs = []
    for f in range(frames):
        value = x_ref[f * area : (f + 1) * area, :]
        inputs.append(jnp.where(first + f < count, value, jnp.zeros_like(value)))
    for f in range(frames):
        pieces = [(t, inputs[f + t - 1]) for t in range(TAPS) if 0 <= f + t - 1 < frames]
        acc_ref[f * area : (f + 1) * area, :] = combine(plane_products(pieces, w_ref), rows, cols)
    route_row = route_ref[pl.ds(place, 1), :]
    onehot_ref[...] = onehot_of(slot_of(route_row, bags, cap, cap), bags * cap)


def join_kernel(
    rows, cols, frames, count_ref, sample_ref, acc_ref, near_ref, far_ref, onehot_ref, e_ref, out_ref, grid_ref
):
    count = scalar_of(count_ref)
    sample = scalar_of(sample_ref)
    area = rows * cols
    place = lax.axis_index("head")
    even = place % 2 == 0
    first = place * frames
    chans = acc_ref.shape[1]
    near, far = near_ref[...], far_ref[...]
    for f in range(frames):
        part = acc_ref[f * area : (f + 1) * area, :]
        if f == 0:
            before = jnp.logical_and(first > 0, first - 1 < count)
            part = part + jnp.where(before, jnp.where(even, far, near), 0.0)
        if f == frames - 1:
            part = part + jnp.where(first + frames < count, jnp.where(even, near, far), 0.0)
        grid_ref[f * area : (f + 1) * area, :] = jnp.where(first + f < count, part, 0.0)
    pieces = [[None] * 2 for _ in range(2)]
    for odd in range(2):
        half = grid_ref[pl.ds(odd, frames * area // 2, stride=2), :]
        half = half.reshape(frames * rows // 2, 2, cols // 2, chans)
        for i in range(2):
            pieces[i][odd] = half[:, i].reshape(frames * area // 4, chans)
    tokens = frames * area // 4
    patches = jnp.concatenate(
        [pieces[0][0], pieces[0][1], pieces[1][0], pieces[1][1]], axis=1
    ).astype(jnp.bfloat16)
    model = e_ref.shape[1]
    col_tile = 256
    total = None
    for n in range(0, model, col_tile):
        part = jnp.dot(patches, e_ref[:, n : n + col_tile], preferred_element_type=jnp.float32)
        squares = part * part
        both = squares[:, :LANES] + squares[:, LANES:]
        total = both if total is None else total + both
    scale = lax.rsqrt(jnp.sum(total, axis=-1, keepdims=True) * (1.0 / model) + epsilon)
    high = scale.astype(jnp.bfloat16).astype(jnp.float32)
    frame = first + lax.broadcasted_iota(jnp.int32, (tokens, LANES), 0) // (area // 4)
    lane = lax.broadcasted_iota(jnp.int32, (tokens, LANES), 1)
    label = jnp.where(frame < count, sample + 1, 0).astype(jnp.float32)
    notes = jnp.where(lane == 0, label, jnp.where(lane == 1, high, jnp.where(lane == 2, scale - high, 0.0)))
    patches = jnp.concatenate([patches, notes.astype(jnp.bfloat16)], axis=1)
    out_ref[...] = jnp.dot(onehot_ref[...], patches, preferred_element_type=jnp.float32).astype(
        jnp.bfloat16
    )


def fold_kernel(e_ref, w_ref, after_ref, fold_ref):
    feats = e_ref.shape[0]
    width = w_ref.shape[2]
    col_tile = 256
    for m in range(3):
        for n in range(0, width, col_tile):
            cols = slice(n, n + col_tile)
            product = jnp.dot(e_ref[...], w_ref[m, :, cols], preferred_element_type=jnp.float32)
            if m == 0:
                product = product * HDIM ** (-0.5)
            high = product.astype(jnp.bfloat16)
            fold_ref[m, :feats, cols] = high
            fold_ref[m, feats:, cols] = (product - high.astype(jnp.float32)).astype(jnp.bfloat16)


def qkv_kernel(*refs):
    pieces, fold_ref, out_ref = refs[:-2], refs[-2], refs[-1]
    for m, at, part in qkv_parts(pieces, fold_ref):
        out_ref[m, :, at : at + part.shape[1]] = part


def qkv_parts(pieces, fold_ref):
    feats = pieces[0].shape[1] - LANES
    col_tile = 256
    patch = jnp.concatenate([ref[:, :feats] for ref in pieces], axis=0)
    notes = jnp.concatenate([ref[:, feats:].astype(jnp.float32) for ref in pieces], axis=0)
    scale = jnp.broadcast_to(notes[:, 1:2] + notes[:, 2:3], (notes.shape[0], col_tile))
    twice = jnp.concatenate([patch, patch], axis=1)
    for m in range(3):
        for n in range(0, fold_ref.shape[2], col_tile):
            part = jnp.dot(twice, fold_ref[m, :, n : n + col_tile], preferred_element_type=jnp.float32)
            yield m, n, part * scale


def bag_kernel(clips, cap, masks, *refs):
    count = len(masks)
    pieces, (near_ref, fold_ref, out_ref, qkv_ref, note_ref, m_ref, r_ref, order_ref) = refs[:count], refs[count:]
    place = lax.axis_index("head")
    slots = pieces[0].shape[0]
    feats = pieces[0].shape[1] - LANES
    width = fold_ref.shape[2]
    clip_rows = count * cap
    half = count // 2

    def by_clip(values, c):
        return jnp.concatenate(
            [value[j * slots + c * cap : j * slots + (c + 1) * cap] for value in values for j in range(half)], axis=0
        )

    notes = [
        jnp.concatenate([ref[:, feats:].astype(jnp.float32) for ref in group], axis=0)
        for group in (pieces[:half], pieces[half:])
    ]
    for c in range(clips):
        note = by_clip(notes, c)
        note_ref[c * clip_rows : (c + 1) * clip_rows, :] = note.astype(jnp.bfloat16)
        order_ref[clips + c] = jnp.max(note[:, :1]).astype(jnp.int32)
    starts = [jnp.int32(0)]
    for s in range(SAMPLES):

        def keep_clip(c, at):
            hit = order_ref[clips + c] == s + 1

            @pl.when(hit)
            def _():
                order_ref[at] = c

            return at + hit.astype(jnp.int32)

        starts.append(lax.fori_loop(0, clips, keep_clip, starts[-1]))

    for m, at, part in qkv_parts(pieces[half:], fold_ref):
        cols = slice(at, at + part.shape[1])
        both = (near_ref[m, :, cols], part)
        for c in range(clips):
            qkv_ref[m, c * clip_rows : (c + 1) * clip_rows, cols] = by_clip(both, c).astype(jnp.bfloat16)

    out_ref[...] = jnp.zeros_like(out_ref)
    tile = 2 * clip_rows
    lane = lax.broadcasted_iota(jnp.int32, (tile, LANES), 1)
    low = lane < HDIM
    pairs = width // LANES
    ones = jnp.ones((tile, LANES), jnp.bfloat16)
    pick = (lax.broadcasted_iota(jnp.int32, (8, LANES), 1) == 0).astype(jnp.float32).astype(jnp.bfloat16)
    key_at = lax.broadcasted_iota(jnp.int32, (1, tile), 1)

    def two(ref, a, b, *at):
        return jnp.concatenate(
            [
                ref[(*at[:-1], pl.ds(pl.multiple_of(a * clip_rows, 16), clip_rows), at[-1])],
                ref[(*at[:-1], pl.ds(pl.multiple_of(b * clip_rows, 16), clip_rows), at[-1])],
            ],
            axis=0,
        )

    for s in range(SAMPLES):
        begin, size = starts[s], starts[s + 1] - starts[s]
        tiles = (size + 1) // 2

        def members(i):
            second = 2 * i + 1 < size
            return (
                order_ref[begin + 2 * i],
                order_ref[begin + 2 * i + second.astype(jnp.int32)],
                second,
            )

        def bias_of(a, b, second):
            label = lax.dot_general(
                pick,
                two(note_ref, a, b, slice(0, LANES)),
                (((1,), (1,)), ((), ())),
                preferred_element_type=jnp.float32,
            )[:1]
            limit = jnp.where(second, tile, clip_rows)
            good = jnp.logical_and(label == s + 1.0, key_at < limit)
            return jnp.where(good, 0.0, far_below)

        def stacked(pair, a, b):
            query = two(qkv_ref, a, b, 0, slice(pair * LANES, (pair + 1) * LANES))
            blank = jnp.zeros_like(query)
            return jnp.concatenate([jnp.where(low, query, blank), jnp.where(low, blank, query)], axis=0)

        def scores_of(pair, query, a, b, bias):
            keys = two(qkv_ref, a, b, 1, slice(pair * LANES, (pair + 1) * LANES))
            return (
                lax.dot_general(query, keys, (((1,), (1,)), ((), ())), preferred_element_type=jnp.float32)
                + bias
            )

        def mix(pair, shifted, a, b):
            cols = slice(pair * LANES, (pair + 1) * LANES)
            values = jnp.concatenate([two(qkv_ref, a, b, 2, cols), ones], axis=1)
            return jnp.dot(shifted.astype(jnp.bfloat16), values, preferred_element_type=jnp.float32)

        def store(pair, a, b, result):
            cols = slice(pair * LANES, (pair + 1) * LANES)
            shares = result[:, :LANES] / result[:, LANES:]
            mixed = jnp.where(low, shares[:tile], shares[tile:])
            for at, clip in ((clip_rows, b), (0, a)):
                for j, mask in enumerate(masks):
                    piece = mixed[at + j * cap : at + (j + 1) * cap]
                    out_ref[jnp.bitwise_xor(place, mask) * clips + clip, :, cols] = piece.astype(jnp.bfloat16)

        def query_tile(i, carry):
            qa, qb, _ = members(i)

            @pl.when(tiles == 1)
            def _():
                ka, kb, second = members(0)
                bias = bias_of(ka, kb, second)
                for pair in range(pairs):
                    scores = scores_of(pair, stacked(pair, qa, qb), ka, kb, bias)
                    top = jnp.max(scores, axis=-1, keepdims=True)
                    store(pair, qa, qb, mix(pair, jnp.exp(scores - top), ka, kb))

            @pl.when(tiles > 1)
            def _():
                for pair in range(pairs):
                    m_ref[pair] = jnp.full((2 * tile, LANES), far_below, jnp.float32)
                    r_ref[pair] = jnp.zeros((2 * tile, 2 * LANES), jnp.float32)

                def key_tile(j, inner):
                    ka, kb, second = members(j)
                    bias = bias_of(ka, kb, second)
                    for pair in range(pairs):
                        scores = scores_of(pair, stacked(pair, qa, qb), ka, kb, bias)
                        old = m_ref[pair][:, :1]
                        top = jnp.maximum(old, jnp.max(scores, axis=-1, keepdims=True))
                        r_ref[pair] = r_ref[pair] * jnp.exp(old - top) + mix(
                            pair, jnp.exp(scores - top), ka, kb
                        )
                        m_ref[pair] = jnp.broadcast_to(top, (2 * tile, LANES))
                    return inner

                lax.fori_loop(0, tiles, key_tile, 0)
                for pair in range(pairs):
                    store(pair, qa, qb, r_ref[pair])

            return carry

        lax.fori_loop(0, tiles, query_tile, 0)


def collect_kernel(frames, heads, count_ref, onehot_ref, recv_ref, out_ref):
    count = scalar_of(count_ref)
    place = lax.axis_index("head")
    slots, tokens = onehot_ref.shape
    frame = place * frames + lax.broadcasted_iota(jnp.int32, (slots, tokens), 1) // (tokens // frames)
    onehot = jnp.where(frame < count, onehot_ref[...], jnp.zeros((), jnp.bfloat16))
    width = recv_ref.shape[1]
    for h in range(heads):
        picked = lax.dot_general(
            onehot,
            recv_ref[h * slots : (h + 1) * slots, :],
            (((0,), (0,)), ((), ())),
            preferred_element_type=jnp.float32,
        )
        out_ref[:, h * width : (h + 1) * width] = picked.astype(jnp.bfloat16)


def shards(latents, frame_counts, routes, samples, conv_weight, embed_weight, qkv_weight):
    frames_dev, rows, cols, depth = latents.shape[1:]
    heads_dev = lax.axis_size("head")
    bags = lax.axis_size("bag")
    area = rows * cols
    tok_dev = frames_dev * area // 4
    cap = 3 * tok_dev // (2 * bags)
    slots = bags * cap
    local_width = qkv_weight.shape[2]
    chans = conv_weight.shape[2]

    tile = latents.reshape(frames_dev * area, depth)
    count = frame_counts
    edge = jax.ShapeDtypeStruct((area, chans), jnp.float32)
    far = pl.pallas_call(
        functools.partial(edge_kernel, rows, cols, frames_dev),
        out_shape=edge,
        in_specs=[ANY, ANY],
        out_specs=VMEM,
        scratch_shapes=[
            pltpu.VMEM((area, depth), jnp.bfloat16),
            pltpu.VMEM((TAPS * TAPS, depth, chans), jnp.bfloat16),
            pltpu.SemaphoreType.DMA((2,)),
        ],
        compiler_params=limit(EDGE_LIMIT),
        cost_estimate=pl.CostEstimate(flops=300000000, bytes_accessed=2000000, transcendentals=0),
        name="edge",
    )(tile, conv_weight)
    across = [(i, i + 1) for i in range(1, heads_dev - 1, 2)]
    far = lax.ppermute(far, "head", across + [(j, i) for i, j in across])

    route_rows = routes[:, 0].reshape(heads_dev, tok_dev)
    row_width = 4 * chans + LANES
    near, acc, onehot = pl.pallas_call(
        functools.partial(own_kernel, bags, cap, rows, cols, frames_dev),
        out_shape=(
            edge,
            jax.ShapeDtypeStruct((frames_dev * area, chans), jnp.float32),
            jax.ShapeDtypeStruct((slots, tok_dev), jnp.bfloat16),
        ),
        in_specs=[VMEM, VMEM, VMEM, VMEM],
        out_specs=(VMEM, VMEM, VMEM),
        compiler_params=limit(16),
        cost_estimate=pl.CostEstimate(flops=1500000000, bytes_accessed=4500000, transcendentals=0),
        name="own",
    )(count, tile, conv_weight, route_rows)
    near = lax.ppermute(near, "head", [(i, i ^ 1) for i in range(heads_dev)])
    outgoing = pl.pallas_call(
        functools.partial(join_kernel, rows, cols, frames_dev),
        out_shape=jax.ShapeDtypeStruct((slots, row_width), jnp.bfloat16),
        in_specs=[VMEM] * 7,
        out_specs=VMEM,
        scratch_shapes=[pltpu.VMEM((frames_dev * area, chans), jnp.float32)],
        compiler_params=limit(16),
        cost_estimate=pl.CostEstimate(flops=300000000, bytes_accessed=3000000, transcendentals=0),
        name="join",
    )(count, samples.reshape(heads_dev, tok_dev), acc, near, far, onehot, embed_weight)

    arrived = lax.all_to_all(
        outgoing.reshape(bags, cap, row_width), "bag", split_axis=0, concat_axis=0, tiled=True
    )
    arrived = arrived.reshape(slots, row_width)
    pieces = {0: arrived}
    bit = heads_dev // 2
    swap = [(i, i ^ bit) for i in range(heads_dev)]
    across = lax.ppermute(arrived, "head", swap)
    folded = pl.pallas_call(
        fold_kernel,
        out_shape=jax.ShapeDtypeStruct((3, 2 * embed_weight.shape[0], local_width), jnp.bfloat16),
        in_specs=[VMEM, VMEM, ANY],
        out_specs=VMEM,
        compiler_params=limit(16),
        cost_estimate=pl.CostEstimate(flops=3300000000, bytes_accessed=14000000, transcendentals=0),
        name="fold",
    )(embed_weight, qkv_weight, arrived)
    def spread(start, bits):
        found = dict(start)
        for lower in bits:
            pairs = [(i, i ^ lower) for i in range(heads_dev)]
            found.update({mask | lower: lax.ppermute(piece, "head", pairs) for mask, piece in found.items()})
        return found

    lower_bits = [1 << i for i in reversed(range(bit.bit_length() - 1))]
    close = spread({0: arrived}, lower_bits)
    near_qkv = pl.pallas_call(
        qkv_kernel,
        out_shape=jax.ShapeDtypeStruct((3, len(close) * slots, local_width), jnp.float32),
        in_specs=[VMEM] * (len(close) + 1),
        out_specs=VMEM,
        compiler_params=limit(16),
        cost_estimate=pl.CostEstimate(flops=1200000000, bytes_accessed=6000000, transcendentals=0),
        name="near_qkv",
    )(*close.values(), folded)
    across, near_qkv = lax.optimization_barrier((across, near_qkv))
    pieces = dict(close)
    pieces.update(spread({bit: across}, lower_bits))
    count_slots = heads_dev * slots
    masks = tuple(pieces)

    pair_rows = 2 * heads_dev * cap
    attended = pl.pallas_call(
        functools.partial(bag_kernel, bags, cap, masks),
        out_shape=jax.ShapeDtypeStruct((heads_dev * bags, cap, local_width), jnp.bfloat16),
        in_specs=[VMEM] * (len(masks) + 2),
        out_specs=VMEM,
        scratch_shapes=[
            pltpu.VMEM((3, count_slots, local_width), jnp.bfloat16),
            pltpu.VMEM((count_slots, LANES), jnp.bfloat16),
            pltpu.VMEM((local_width // LANES, 2 * pair_rows, LANES), jnp.float32),
            pltpu.VMEM((local_width // LANES, 2 * pair_rows, 2 * LANES), jnp.float32),
            pltpu.SMEM((2 * bags,), jnp.int32),
        ],
        compiler_params=limit(28),
        cost_estimate=pl.CostEstimate(flops=3000000000, bytes_accessed=5000000, transcendentals=1200000),
        name="bag",
    )(*pieces.values(), near_qkv, folded)
    received = lax.all_to_all(attended, ("head", "bag"), split_axis=0, concat_axis=0, tiled=True)
    return pl.pallas_call(
        functools.partial(collect_kernel, frames_dev, heads_dev),
        out_shape=jax.ShapeDtypeStruct((tok_dev, heads_dev * local_width), jnp.bfloat16),
        in_specs=[VMEM, VMEM, VMEM],
        out_specs=VMEM,
        compiler_params=limit(16),
        name="collect",
    )(count, onehot, received.reshape(count_slots, local_width))


def solution(mesh):
    placed = (
        P("bag", "head", None, None, None),
        P("bag"),
        P("bag", None),
        P("bag"),
        P(),
        P(),
        P(None, None, "head"),
    )
    return jax.shard_map(
        shards, mesh=mesh, in_specs=placed, out_specs=P(("bag", "head"), None), check_vma=False
    )
```

```python
import functools
import math
import jax
import jax.numpy as jnp
from jax import lax
from jax.experimental import pallas as pl
from jax.experimental.pallas import tpu as pltpu
from jax.sharding import PartitionSpec as P

HDIM = 64
TAPS = 3
SAMPLES = 4
LANES = 128

epsilon = 1e-06
far_below = -1e30

VMEM = pl.BlockSpec(memory_space=pltpu.VMEM)
ANY = pl.BlockSpec(memory_space=pl.ANY)
EDGE_LIMIT = 62


def limit(mib):
    return pltpu.CompilerParams(vmem_limit_bytes=mib << 20)


def slot_of(route_row, bags, cap, stride):
    tokens = route_row.shape[1]
    bag_ids = lax.broadcasted_iota(jnp.int32, (bags, tokens), 0)
    onehot = (bag_ids == route_row).astype(jnp.float32)
    before = (
        lax.broadcasted_iota(jnp.int32, (tokens, tokens), 0)
        < lax.broadcasted_iota(jnp.int32, (tokens, tokens), 1)
    )
    earlier = jnp.dot(
        onehot.astype(jnp.bfloat16),
        before.astype(jnp.float32).astype(jnp.bfloat16),
        preferred_element_type=jnp.float32,
    )
    rank = jnp.sum(earlier * onehot, axis=0, keepdims=True).astype(jnp.int32)
    return route_row * stride + rank


def onehot_of(slot, slots):
    slot_ids = lax.broadcasted_iota(jnp.int32, (slots, slot.shape[1]), 0)
    return (slot_ids == slot).astype(jnp.float32).astype(jnp.bfloat16)


def combine(products, rows, cols):
    chans = products[0].shape[1]
    blank = jnp.zeros((cols, chans), jnp.float32)
    area = rows * cols
    column = lax.broadcasted_iota(jnp.int32, (area, chans), 0) % cols
    total = None
    for e in range(TAPS):
        up, mid, down = products[e], products[TAPS + e], products[2 * TAPS + e]
        merged = (
            mid
            + jnp.concatenate([blank, up[: area - cols]], axis=0)
            + jnp.concatenate([down[cols:], blank], axis=0)
        )
        if e == 0:
            merged = jnp.where(column == 0, 0.0, pltpu.roll(merged, 1, axis=0))
        elif e == 2:
            merged = jnp.where(column == cols - 1, 0.0, pltpu.roll(merged, area - 1, axis=0))
        total = merged if total is None else total + merged
    return total


def plane_products(pieces, w_ref):
    plane = TAPS * TAPS
    chans = w_ref.shape[2]
    stacked = pieces[0][1] if len(pieces) == 1 else jnp.concatenate([x for _, x in pieces], axis=1)
    products = []
    for p in range(0, plane, 2):
        pair = []
        for q in range(p, min(p + 2, plane)):
            taps = [w_ref[plane * t + q] for t, _ in pieces]
            pair.append(taps[0] if len(taps) == 1 else jnp.concatenate(taps, axis=0))
        weight = pair[0] if len(pair) == 1 else jnp.concatenate(pair, axis=1)
        value = jnp.dot(stacked, weight, preferred_element_type=jnp.float32)
        for q in range(len(pair)):
            products.append(value[:, q * chans : (q + 1) * chans])
    return products


def scalar_of(ref):
    return jnp.max(ref[...])


def edge_kernel(rows, cols, frames, x_hbm, w_hbm, near_ref, far_ref, x_ref, w_ref, sems):
    area = rows * cols
    plane = TAPS * TAPS
    jobs = ((frames - 1, 0), (0, 2))
    loads = []
    for i, (f, tap) in enumerate(jobs):
        loads.append(
            (
                pltpu.make_async_copy(
                    x_hbm.at[pl.ds(f * area, area)], x_ref.at[pl.ds(i * area, area)], sems.at[2 * i]
                ),
                pltpu.make_async_copy(
                    w_hbm.at[pl.ds(tap * plane, plane)], w_ref.at[pl.ds(i * plane, plane)], sems.at[2 * i + 1]
                ),
            )
        )
    for pair in loads:
        for load in pair:
            load.start()
    even = lax.axis_index("head") % 2 == 0
    sums = []
    for i in range(2):
        for load in loads[i]:
            load.wait()
        value = x_ref[i * area : (i + 1) * area, :]
        sums.append(combine(plane_products([(i, value)], w_ref), rows, cols))
    up, down = sums
    near_ref[...] = jnp.where(even, up, down)
    far_ref[...] = jnp.where(even, down, up)


def own_kernel(bags, cap, rows, cols, frames, count_ref, x_ref, w_ref, route_ref, acc_ref, onehot_ref):
    count = scalar_of(count_ref)
    place = lax.axis_index("head")
    area = rows * cols
    first = place * frames
    inputs = []
    for f in range(frames):
        value = x_ref[f * area : (f + 1) * area, :]
        inputs.append(jnp.where(first + f < count, value, jnp.zeros_like(value)))
    for f in range(frames):
        pieces = [(t, inputs[f + t - 1]) for t in range(TAPS) if 0 <= f + t - 1 < frames]
        acc_ref[f * area : (f + 1) * area, :] = combine(plane_products(pieces, w_ref), rows, cols)
    route_row = route_ref[pl.ds(place, 1), :]
    onehot_ref[...] = onehot_of(slot_of(route_row, bags, cap, cap), bags * cap)


def join_kernel(
    rows, cols, frames, count_ref, sample_ref, acc_ref, near_ref, far_ref, onehot_ref, e_ref, out_ref, grid_ref
):
    count = scalar_of(count_ref)
    sample = scalar_of(sample_ref)
    area = rows * cols
    place = lax.axis_index("head")
    even = place % 2 == 0
    first = place * frames
    chans = acc_ref.shape[1]
    near, far = near_ref[...], far_ref[...]
    for f in range(frames):
        part = acc_ref[f * area : (f + 1) * area, :]
        if f == 0:
            before = jnp.logical_and(first > 0, first - 1 < count)
            part = part + jnp.where(before, jnp.where(even, far, near), 0.0)
        if f == frames - 1:
            part = part + jnp.where(first + frames < count, jnp.where(even, near, far), 0.0)
        grid_ref[f * area : (f + 1) * area, :] = jnp.where(first + f < count, part, 0.0)
    pieces = [[None] * 2 for _ in range(2)]
    for odd in range(2):
        half = grid_ref[pl.ds(odd, frames * area // 2, stride=2), :]
        half = half.reshape(frames * rows // 2, 2, cols // 2, chans)
        for i in range(2):
            pieces[i][odd] = half[:, i].reshape(frames * area // 4, chans)
    tokens = frames * area // 4
    patches = jnp.concatenate(
        [pieces[0][0], pieces[0][1], pieces[1][0], pieces[1][1]], axis=1
    ).astype(jnp.bfloat16)
    model = e_ref.shape[1]
    col_tile = 256
    total = None
    for n in range(0, model, col_tile):
        part = jnp.dot(patches, e_ref[:, n : n + col_tile], preferred_element_type=jnp.float32)
        squares = part * part
        both = squares[:, :LANES] + squares[:, LANES:]
        total = both if total is None else total + both
    scale = lax.rsqrt(jnp.sum(total, axis=-1, keepdims=True) * (1.0 / model) + epsilon)
    high = scale.astype(jnp.bfloat16).astype(jnp.float32)
    frame = first + lax.broadcasted_iota(jnp.int32, (tokens, LANES), 0) // (area // 4)
    lane = lax.broadcasted_iota(jnp.int32, (tokens, LANES), 1)
    label = jnp.where(frame < count, sample + 1, 0).astype(jnp.float32)
    notes = jnp.where(lane == 0, label, jnp.where(lane == 1, high, jnp.where(lane == 2, scale - high, 0.0)))
    patches = jnp.concatenate([patches, notes.astype(jnp.bfloat16)], axis=1)
    out_ref[...] = jnp.dot(onehot_ref[...], patches, preferred_element_type=jnp.float32).astype(
        jnp.bfloat16
    )


def fold_kernel(e_ref, w_ref, after_ref, fold_ref):
    feats = e_ref.shape[0]
    width = w_ref.shape[2]
    col_tile = 256
    for m in range(3):
        for n in range(0, width, col_tile):
            cols = slice(n, n + col_tile)
            product = jnp.dot(e_ref[...], w_ref[m, :, cols], preferred_element_type=jnp.float32)
            if m == 0:
                product = product * (HDIM ** (-0.5) * math.log2(math.e))
            high = product.astype(jnp.bfloat16)
            fold_ref[m, :feats, cols] = high
            fold_ref[m, feats:, cols] = (product - high.astype(jnp.float32)).astype(jnp.bfloat16)


def qkv_kernel(*refs):
    pieces, fold_ref, out_ref = refs[:-2], refs[-2], refs[-1]
    for m, at, part in qkv_parts(pieces, fold_ref):
        out_ref[m, :, at : at + part.shape[1]] = part


def qkv_parts(pieces, fold_ref):
    feats = pieces[0].shape[1] - LANES
    col_tile = 256
    patch = jnp.concatenate([ref[:, :feats] for ref in pieces], axis=0)
    notes = jnp.concatenate([ref[:, feats:].astype(jnp.float32) for ref in pieces], axis=0)
    scale = jnp.broadcast_to(notes[:, 1:2] + notes[:, 2:3], (notes.shape[0], col_tile))
    twice = jnp.concatenate([patch, patch], axis=1)
    for m in range(3):
        for n in range(0, fold_ref.shape[2], col_tile):
            part = jnp.dot(twice, fold_ref[m, :, n : n + col_tile], preferred_element_type=jnp.float32)
            yield m, n, part * scale


def bag_kernel(clips, cap, masks, *refs):
    count = len(masks)
    pieces, (near_ref, fold_ref, out_ref, qkv_ref, note_ref, m_ref, r_ref, order_ref) = refs[:count], refs[count:]
    place = lax.axis_index("head")
    slots = pieces[0].shape[0]
    feats = pieces[0].shape[1] - LANES
    width = fold_ref.shape[2]
    clip_rows = count * cap
    half = count // 2

    def by_clip(values, c):
        return jnp.concatenate(
            [value[j * slots + c * cap : j * slots + (c + 1) * cap] for value in values for j in range(half)], axis=0
        )

    notes = [
        jnp.concatenate([ref[:, feats:].astype(jnp.float32) for ref in group], axis=0)
        for group in (pieces[:half], pieces[half:])
    ]
    for c in range(clips):
        note = by_clip(notes, c)
        note_ref[c * clip_rows : (c + 1) * clip_rows, :] = note.astype(jnp.bfloat16)
        order_ref[clips + c] = jnp.max(note[:, :1]).astype(jnp.int32)
    starts = [jnp.int32(0)]
    for s in range(SAMPLES):

        def keep_clip(c, at):
            hit = order_ref[clips + c] == s + 1

            @pl.when(hit)
            def _():
                order_ref[at] = c

            return at + hit.astype(jnp.int32)

        starts.append(lax.fori_loop(0, clips, keep_clip, starts[-1]))

    for m, at, part in qkv_parts(pieces[half:], fold_ref):
        cols = slice(at, at + part.shape[1])
        both = (near_ref[m, :, cols], part)
        for c in range(clips):
            qkv_ref[m, c * clip_rows : (c + 1) * clip_rows, cols] = by_clip(both, c).astype(jnp.bfloat16)

    out_ref[...] = jnp.zeros_like(out_ref)
    tile = 2 * clip_rows
    lane = lax.broadcasted_iota(jnp.int32, (tile, LANES), 1)
    low = lane < HDIM
    pairs = width // LANES
    ones = jnp.ones((tile, LANES), jnp.bfloat16)
    unit = lax.broadcasted_iota(jnp.int32, (2 * tile, LANES), 1) == 0
    unit = unit.astype(jnp.float32).astype(jnp.bfloat16)
    key_at = lax.broadcasted_iota(jnp.int32, (tile, LANES), 0)

    def two(ref, a, b, *at):
        return jnp.concatenate(
            [
                ref[(*at[:-1], pl.ds(pl.multiple_of(a * clip_rows, 16), clip_rows), at[-1])],
                ref[(*at[:-1], pl.ds(pl.multiple_of(b * clip_rows, 16), clip_rows), at[-1])],
            ],
            axis=0,
        )

    for s in range(SAMPLES):
        begin, size = starts[s], starts[s + 1] - starts[s]
        tiles = (size + 1) // 2

        def members(i):
            second = 2 * i + 1 < size
            return (
                order_ref[begin + 2 * i],
                order_ref[begin + 2 * i + second.astype(jnp.int32)],
                second,
            )

        def bias_of(a, b, second):
            label = two(note_ref, a, b, slice(0, LANES)).astype(jnp.float32)
            limit = jnp.where(second, tile, clip_rows)
            good = jnp.logical_and(label == s + 1.0, key_at < limit)
            return jnp.where(good, 0.0, far_below).astype(jnp.bfloat16)

        def stacked(pair, a, b):
            query = two(qkv_ref, a, b, 0, slice(pair * LANES, (pair + 1) * LANES))
            blank = jnp.zeros_like(query)
            both = jnp.concatenate([jnp.where(low, query, blank), jnp.where(low, blank, query)], axis=0)
            return jnp.concatenate([both, unit], axis=1)

        def scores_of(pair, query, a, b, bias):
            keys = two(qkv_ref, a, b, 1, slice(pair * LANES, (pair + 1) * LANES))
            keys = jnp.concatenate([keys, bias], axis=1)
            return lax.dot_general(query, keys, (((1,), (1,)), ((), ())), preferred_element_type=jnp.float32)

        def mix(pair, shifted, a, b):
            cols = slice(pair * LANES, (pair + 1) * LANES)
            values = jnp.concatenate([two(qkv_ref, a, b, 2, cols), ones], axis=1)
            return jnp.dot(shifted.astype(jnp.bfloat16), values, preferred_element_type=jnp.float32)

        def store(pair, a, b, result):
            cols = slice(pair * LANES, (pair + 1) * LANES)
            shares = result[:, :LANES] / result[:, LANES:]
            mixed = jnp.where(low, shares[:tile], shares[tile:])
            for at, clip in ((clip_rows, b), (0, a)):
                for j, mask in enumerate(masks):
                    piece = mixed[at + j * cap : at + (j + 1) * cap]
                    out_ref[jnp.bitwise_xor(place, mask) * clips + clip, :, cols] = piece.astype(jnp.bfloat16)

        def query_tile(i, carry):
            qa, qb, _ = members(i)

            @pl.when(tiles == 1)
            def _():
                ka, kb, second = members(0)
                bias = bias_of(ka, kb, second)
                for pair in range(pairs):
                    scores = scores_of(pair, stacked(pair, qa, qb), ka, kb, bias)
                    top = jnp.max(scores, axis=-1, keepdims=True)
                    store(pair, qa, qb, mix(pair, jnp.exp2(scores - top), ka, kb))

            @pl.when(tiles > 1)
            def _():
                for pair in range(pairs):
                    m_ref[pair] = jnp.full((2 * tile, LANES), far_below, jnp.float32)
                    r_ref[pair] = jnp.zeros((2 * tile, 2 * LANES), jnp.float32)

                def key_tile(j, inner):
                    ka, kb, second = members(j)
                    bias = bias_of(ka, kb, second)
                    for pair in range(pairs):
                        scores = scores_of(pair, stacked(pair, qa, qb), ka, kb, bias)
                        old = m_ref[pair][:, :1]
                        top = jnp.maximum(old, jnp.max(scores, axis=-1, keepdims=True))
                        r_ref[pair] = r_ref[pair] * jnp.exp2(old - top) + mix(
                            pair, jnp.exp2(scores - top), ka, kb
                        )
                        m_ref[pair] = jnp.broadcast_to(top, (2 * tile, LANES))
                    return inner

                lax.fori_loop(0, tiles, key_tile, 0)
                for pair in range(pairs):
                    store(pair, qa, qb, r_ref[pair])

            return carry

        lax.fori_loop(0, tiles, query_tile, 0)


def collect_kernel(frames, heads, count_ref, onehot_ref, recv_ref, out_ref):
    count = scalar_of(count_ref)
    place = lax.axis_index("head")
    slots, tokens = onehot_ref.shape
    frame = place * frames + lax.broadcasted_iota(jnp.int32, (slots, tokens), 1) // (tokens // frames)
    onehot = jnp.where(frame < count, onehot_ref[...], jnp.zeros((), jnp.bfloat16))
    width = recv_ref.shape[1]
    for h in range(heads):
        picked = lax.dot_general(
            onehot,
            recv_ref[h * slots : (h + 1) * slots, :],
            (((0,), (0,)), ((), ())),
            preferred_element_type=jnp.float32,
        )
        out_ref[:, h * width : (h + 1) * width] = picked.astype(jnp.bfloat16)


def shards(latents, frame_counts, routes, samples, conv_weight, embed_weight, qkv_weight):
    frames_dev, rows, cols, depth = latents.shape[1:]
    heads_dev = lax.axis_size("head")
    bags = lax.axis_size("bag")
    area = rows * cols
    tok_dev = frames_dev * area // 4
    cap = 3 * tok_dev // (2 * bags)
    slots = bags * cap
    local_width = qkv_weight.shape[2]
    chans = conv_weight.shape[2]

    tile = latents.reshape(frames_dev * area, depth)
    count = frame_counts
    edge = jax.ShapeDtypeStruct((area, chans), jnp.float32)
    near, far = pl.pallas_call(
        functools.partial(edge_kernel, rows, cols, frames_dev),
        out_shape=(edge, edge),
        in_specs=[ANY, ANY],
        out_specs=(VMEM, VMEM),
        scratch_shapes=[
            pltpu.VMEM((2 * area, depth), jnp.bfloat16),
            pltpu.VMEM((2 * TAPS * TAPS, depth, chans), jnp.bfloat16),
            pltpu.SemaphoreType.DMA((4,)),
        ],
        compiler_params=limit(EDGE_LIMIT),
        cost_estimate=pl.CostEstimate(flops=600000000, bytes_accessed=4500000, transcendentals=0),
        name="edge",
    )(tile, conv_weight)
    across = [(i, i + 1) for i in range(1, heads_dev - 1, 2)]
    far = lax.ppermute(far, "head", across + [(j, i) for i, j in across])
    near = lax.ppermute(near, "head", [(i, i ^ 1) for i in range(heads_dev)])

    route_rows = routes[:, 0].reshape(heads_dev, tok_dev)
    row_width = 4 * chans + LANES
    acc, onehot = pl.pallas_call(
        functools.partial(own_kernel, bags, cap, rows, cols, frames_dev),
        out_shape=(
            jax.ShapeDtypeStruct((frames_dev * area, chans), jnp.float32),
            jax.ShapeDtypeStruct((slots, tok_dev), jnp.bfloat16),
        ),
        in_specs=[VMEM, VMEM, VMEM, VMEM],
        out_specs=(VMEM, VMEM),
        compiler_params=limit(16),
        cost_estimate=pl.CostEstimate(flops=1200000000, bytes_accessed=4500000, transcendentals=0),
        name="own",
    )(count, tile, conv_weight, route_rows)
    outgoing = pl.pallas_call(
        functools.partial(join_kernel, rows, cols, frames_dev),
        out_shape=jax.ShapeDtypeStruct((slots, row_width), jnp.bfloat16),
        in_specs=[VMEM] * 7,
        out_specs=VMEM,
        scratch_shapes=[pltpu.VMEM((frames_dev * area, chans), jnp.float32)],
        compiler_params=limit(16),
        cost_estimate=pl.CostEstimate(flops=300000000, bytes_accessed=3000000, transcendentals=0),
        name="join",
    )(count, samples.reshape(heads_dev, tok_dev), acc, near, far, onehot, embed_weight)

    arrived = lax.all_to_all(
        outgoing.reshape(bags, cap, row_width), "bag", split_axis=0, concat_axis=0, tiled=True
    )
    arrived = arrived.reshape(slots, row_width)
    pieces = {0: arrived}
    bit = heads_dev // 2
    swap = [(i, i ^ bit) for i in range(heads_dev)]
    across = lax.ppermute(arrived, "head", swap)
    folded = pl.pallas_call(
        fold_kernel,
        out_shape=jax.ShapeDtypeStruct((3, 2 * embed_weight.shape[0], local_width), jnp.bfloat16),
        in_specs=[VMEM, VMEM, ANY],
        out_specs=VMEM,
        compiler_params=limit(16),
        cost_estimate=pl.CostEstimate(flops=3300000000, bytes_accessed=14000000, transcendentals=0),
        name="fold",
    )(embed_weight, qkv_weight, arrived)
    def spread(start, bits):
        found = dict(start)
        for lower in bits:
            pairs = [(i, i ^ lower) for i in range(heads_dev)]
            found.update({mask | lower: lax.ppermute(piece, "head", pairs) for mask, piece in found.items()})
        return found

    lower_bits = [1 << i for i in reversed(range(bit.bit_length() - 1))]
    close = spread({0: arrived}, lower_bits)
    near_qkv = pl.pallas_call(
        qkv_kernel,
        out_shape=jax.ShapeDtypeStruct((3, len(close) * slots, local_width), jnp.float32),
        in_specs=[VMEM] * (len(close) + 1),
        out_specs=VMEM,
        compiler_params=limit(16),
        cost_estimate=pl.CostEstimate(flops=1200000000, bytes_accessed=6000000, transcendentals=0),
        name="near_qkv",
    )(*close.values(), folded)
    across, near_qkv = lax.optimization_barrier((across, near_qkv))
    pieces = dict(close)
    pieces.update(spread({bit: across}, lower_bits))
    count_slots = heads_dev * slots
    masks = tuple(pieces)

    pair_rows = 2 * heads_dev * cap
    attended = pl.pallas_call(
        functools.partial(bag_kernel, bags, cap, masks),
        out_shape=jax.ShapeDtypeStruct((heads_dev * bags, cap, local_width), jnp.bfloat16),
        in_specs=[VMEM] * (len(masks) + 2),
        out_specs=VMEM,
        scratch_shapes=[
            pltpu.VMEM((3, count_slots, local_width), jnp.bfloat16),
            pltpu.VMEM((count_slots, LANES), jnp.bfloat16),
            pltpu.VMEM((local_width // LANES, 2 * pair_rows, LANES), jnp.float32),
            pltpu.VMEM((local_width // LANES, 2 * pair_rows, 2 * LANES), jnp.float32),
            pltpu.SMEM((2 * bags,), jnp.int32),
        ],
        compiler_params=limit(28),
        cost_estimate=pl.CostEstimate(flops=3000000000, bytes_accessed=5000000, transcendentals=1200000),
        name="bag",
    )(*pieces.values(), near_qkv, folded)
    received = lax.all_to_all(attended, ("head", "bag"), split_axis=0, concat_axis=0, tiled=True)
    return pl.pallas_call(
        functools.partial(collect_kernel, frames_dev, heads_dev),
        out_shape=jax.ShapeDtypeStruct((tok_dev, heads_dev * local_width), jnp.bfloat16),
        in_specs=[VMEM, VMEM, VMEM],
        out_specs=VMEM,
        compiler_params=limit(16),
        name="collect",
    )(count, onehot, received.reshape(count_slots, local_width))


def solution(mesh):
    placed = (
        P("bag", "head", None, None, None),
        P("bag"),
        P("bag", None),
        P("bag"),
        P(),
        P(),
        P(None, None, "head"),
    )
    return jax.shard_map(
        shards, mesh=mesh, in_specs=placed, out_specs=P(("bag", "head"), None), check_vma=False
    )
```

```python
import functools
import math
import jax
import jax.numpy as jnp
from jax import lax
from jax.experimental import pallas as pl
from jax.experimental.pallas import tpu as pltpu
from jax.sharding import PartitionSpec as P

HDIM = 64
TAPS = 3
SAMPLES = 4
LANES = 128

epsilon = 1e-06
far_below = -1e30

VMEM = pl.BlockSpec(memory_space=pltpu.VMEM)
ANY = pl.BlockSpec(memory_space=pl.ANY)
EDGE_LIMIT = 60


def limit(mib):
    return pltpu.CompilerParams(vmem_limit_bytes=mib << 20)


def slot_of(route_row, bags, cap, stride):
    tokens = route_row.shape[1]
    bag_ids = lax.broadcasted_iota(jnp.int32, (bags, tokens), 0)
    onehot = (bag_ids == route_row).astype(jnp.float32)
    before = (
        lax.broadcasted_iota(jnp.int32, (tokens, tokens), 0)
        < lax.broadcasted_iota(jnp.int32, (tokens, tokens), 1)
    )
    earlier = jnp.dot(
        onehot.astype(jnp.bfloat16),
        before.astype(jnp.float32).astype(jnp.bfloat16),
        preferred_element_type=jnp.float32,
    )
    rank = jnp.sum(earlier * onehot, axis=0, keepdims=True).astype(jnp.int32)
    return route_row * stride + rank


def onehot_of(slot, slots):
    slot_ids = lax.broadcasted_iota(jnp.int32, (slots, slot.shape[1]), 0)
    return (slot_ids == slot).astype(jnp.float32).astype(jnp.bfloat16)


def combine(products, rows, cols):
    chans = products[0].shape[1]
    blank = jnp.zeros((cols, chans), jnp.float32)
    area = rows * cols
    column = lax.broadcasted_iota(jnp.int32, (area, chans), 0) % cols
    total = None
    for e in range(TAPS):
        up, mid, down = products[e], products[TAPS + e], products[2 * TAPS + e]
        merged = (
            mid
            + jnp.concatenate([blank, up[: area - cols]], axis=0)
            + jnp.concatenate([down[cols:], blank], axis=0)
        )
        if e == 0:
            merged = jnp.where(column == 0, 0.0, pltpu.roll(merged, 1, axis=0))
        elif e == 2:
            merged = jnp.where(column == cols - 1, 0.0, pltpu.roll(merged, area - 1, axis=0))
        total = merged if total is None else total + merged
    return total


def plane_products(pieces, w_ref):
    plane = TAPS * TAPS
    chans = w_ref.shape[2]
    stacked = pieces[0][1] if len(pieces) == 1 else jnp.concatenate([x for _, x in pieces], axis=1)
    products = []
    for p in range(0, plane, 2):
        pair = []
        for q in range(p, min(p + 2, plane)):
            taps = [w_ref[plane * t + q] for t, _ in pieces]
            pair.append(taps[0] if len(taps) == 1 else jnp.concatenate(taps, axis=0))
        weight = pair[0] if len(pair) == 1 else jnp.concatenate(pair, axis=1)
        value = jnp.dot(stacked, weight, preferred_element_type=jnp.float32)
        for q in range(len(pair)):
            products.append(value[:, q * chans : (q + 1) * chans])
    return products


def scalar_of(ref):
    return jnp.max(ref[...])


def edge_kernel(rows, cols, frames, x_hbm, w_hbm, near_ref, far_ref, x_ref, w_ref, sems):
    area = rows * cols
    plane = TAPS * TAPS
    jobs = ((frames - 1, 0), (0, 2))
    loads = []
    for i, (f, tap) in enumerate(jobs):
        group = [
            pltpu.make_async_copy(
                x_hbm.at[pl.ds(f * area, area)], x_ref.at[pl.ds(i * area, area)], sems.at[i, TAPS]
            )
        ]
        for row in range(TAPS):
            group.append(
                pltpu.make_async_copy(
                    w_hbm.at[pl.ds(tap * plane + row * TAPS, TAPS)],
                    w_ref.at[pl.ds(i * plane + row * TAPS, TAPS)],
                    sems.at[i, row],
                )
            )
        loads.append(group)
    for group in loads:
        for load in group:
            load.start()
    even = lax.axis_index("head") % 2 == 0
    sums = []
    for i in range(2):
        for load in loads[i]:
            load.wait()
        value = x_ref[i * area : (i + 1) * area, :]
        sums.append(combine(plane_products([(i, value)], w_ref), rows, cols))
    up, down = sums
    near_ref[...] = jnp.where(even, up, down)
    far_ref[...] = jnp.where(even, down, up)


def own_kernel(bags, cap, rows, cols, frames, count_ref, x_ref, w_ref, route_ref, acc_ref, onehot_ref):
    count = scalar_of(count_ref)
    place = lax.axis_index("head")
    area = rows * cols
    first = place * frames
    inputs = []
    for f in range(frames):
        value = x_ref[f * area : (f + 1) * area, :]
        inputs.append(jnp.where(first + f < count, value, jnp.zeros_like(value)))
    for f in range(frames):
        pieces = [(t, inputs[f + t - 1]) for t in range(TAPS) if 0 <= f + t - 1 < frames]
        acc_ref[f * area : (f + 1) * area, :] = combine(plane_products(pieces, w_ref), rows, cols)
    route_row = route_ref[pl.ds(place, 1), :]
    onehot_ref[...] = onehot_of(slot_of(route_row, bags, cap, cap), bags * cap)


def join_kernel(
    rows, cols, frames, count_ref, sample_ref, acc_ref, near_ref, far_ref, onehot_ref, e_ref, out_ref, grid_ref
):
    count = scalar_of(count_ref)
    sample = scalar_of(sample_ref)
    area = rows * cols
    place = lax.axis_index("head")
    even = place % 2 == 0
    first = place * frames
    chans = acc_ref.shape[1]
    near, far = near_ref[...], far_ref[...]
    for f in range(frames):
        part = acc_ref[f * area : (f + 1) * area, :]
        if f == 0:
            before = jnp.logical_and(first > 0, first - 1 < count)
            part = part + jnp.where(before, jnp.where(even, far, near), 0.0)
        if f == frames - 1:
            part = part + jnp.where(first + frames < count, jnp.where(even, near, far), 0.0)
        grid_ref[f * area : (f + 1) * area, :] = jnp.where(first + f < count, part, 0.0)
    pieces = [[None] * 2 for _ in range(2)]
    for odd in range(2):
        half = grid_ref[pl.ds(odd, frames * area // 2, stride=2), :]
        half = half.reshape(frames * rows // 2, 2, cols // 2, chans)
        for i in range(2):
            pieces[i][odd] = half[:, i].reshape(frames * area // 4, chans)
    tokens = frames * area // 4
    patches = jnp.concatenate(
        [pieces[0][0], pieces[0][1], pieces[1][0], pieces[1][1]], axis=1
    ).astype(jnp.bfloat16)
    model = e_ref.shape[1]
    col_tile = 256
    total = None
    for n in range(0, model, col_tile):
        part = jnp.dot(patches, e_ref[:, n : n + col_tile], preferred_element_type=jnp.float32)
        squares = part * part
        both = squares[:, :LANES] + squares[:, LANES:]
        total = both if total is None else total + both
    scale = lax.rsqrt(jnp.sum(total, axis=-1, keepdims=True) * (1.0 / model) + epsilon)
    high = scale.astype(jnp.bfloat16).astype(jnp.float32)
    frame = first + lax.broadcasted_iota(jnp.int32, (tokens, LANES), 0) // (area // 4)
    lane = lax.broadcasted_iota(jnp.int32, (tokens, LANES), 1)
    label = jnp.where(frame < count, sample + 1, 0).astype(jnp.float32)
    notes = jnp.where(lane == 0, label, jnp.where(lane == 1, high, jnp.where(lane == 2, scale - high, 0.0)))
    patches = jnp.concatenate([patches, notes.astype(jnp.bfloat16)], axis=1)
    out_ref[...] = jnp.dot(onehot_ref[...], patches, preferred_element_type=jnp.float32).astype(
        jnp.bfloat16
    )


def fold_kernel(e_ref, w_ref, after_ref, fold_ref):
    feats = e_ref.shape[0]
    width = w_ref.shape[2]
    col_tile = 256
    for m in range(3):
        for n in range(0, width, col_tile):
            cols = slice(n, n + col_tile)
            product = jnp.dot(e_ref[...], w_ref[m, :, cols], preferred_element_type=jnp.float32)
            if m == 0:
                product = product * (HDIM ** (-0.5) * math.log2(math.e))
            high = product.astype(jnp.bfloat16)
            fold_ref[m, :feats, cols] = high
            fold_ref[m, feats:, cols] = (product - high.astype(jnp.float32)).astype(jnp.bfloat16)


def qkv_kernel(*refs):
    pieces, fold_ref, out_ref = refs[:-2], refs[-2], refs[-1]
    for m, at, part in qkv_parts(pieces, fold_ref):
        out_ref[m, :, at : at + part.shape[1]] = part


def qkv_parts(pieces, fold_ref):
    feats = pieces[0].shape[1] - LANES
    col_tile = 256
    patch = jnp.concatenate([ref[:, :feats] for ref in pieces], axis=0)
    notes = jnp.concatenate([ref[:, feats:].astype(jnp.float32) for ref in pieces], axis=0)
    scale = jnp.broadcast_to(notes[:, 1:2] + notes[:, 2:3], (notes.shape[0], col_tile))
    twice = jnp.concatenate([patch, patch], axis=1)
    for m in range(3):
        for n in range(0, fold_ref.shape[2], col_tile):
            part = jnp.dot(twice, fold_ref[m, :, n : n + col_tile], preferred_element_type=jnp.float32)
            yield m, n, part * scale


def bag_kernel(clips, cap, masks, groups, *refs):
    count = len(masks)
    pieces, rest = refs[:count], refs[count:]
    early, rest = rest[: len(groups)], rest[len(groups) :]
    fold_ref, out_ref, qkv_ref, note_ref, m_ref, r_ref, order_ref = rest
    place = lax.axis_index("head")
    slots = pieces[0].shape[0]
    feats = pieces[0].shape[1] - LANES
    width = fold_ref.shape[2]
    clip_rows = count * cap
    done = sum(groups)

    def by_clip(values, c):
        return jnp.concatenate(
            [
                value[j * slots + c * cap : j * slots + (c + 1) * cap]
                for value in values
                for j in range(value.shape[0] // slots)
            ],
            axis=0,
        )

    notes = [ref[:, feats:].astype(jnp.float32) for ref in pieces]
    for c in range(clips):
        note = by_clip(notes, c)
        note_ref[c * clip_rows : (c + 1) * clip_rows, :] = note.astype(jnp.bfloat16)
        order_ref[clips + c] = jnp.max(note[:, :1]).astype(jnp.int32)
    starts = [jnp.int32(0)]
    for s in range(SAMPLES):

        def keep_clip(c, at):
            hit = order_ref[clips + c] == s + 1

            @pl.when(hit)
            def _():
                order_ref[at] = c

            return at + hit.astype(jnp.int32)

        starts.append(lax.fori_loop(0, clips, keep_clip, starts[-1]))

    for m, at, part in qkv_parts(pieces[done:], fold_ref):
        cols = slice(at, at + part.shape[1])
        parts = [ref[m, :, cols] for ref in early] + [part]
        for c in range(clips):
            qkv_ref[m, c * clip_rows : (c + 1) * clip_rows, cols] = by_clip(parts, c).astype(jnp.bfloat16)

    out_ref[...] = jnp.zeros_like(out_ref)
    tile = 2 * clip_rows
    lane = lax.broadcasted_iota(jnp.int32, (tile, LANES), 1)
    low = lane < HDIM
    pairs = width // LANES
    ones = jnp.ones((tile, LANES), jnp.bfloat16)
    pick = (lax.broadcasted_iota(jnp.int32, (8, LANES), 1) == 0).astype(jnp.float32).astype(jnp.bfloat16)
    key_at = lax.broadcasted_iota(jnp.int32, (1, tile), 1)

    def two(ref, a, b, *at):
        return jnp.concatenate(
            [
                ref[(*at[:-1], pl.ds(pl.multiple_of(a * clip_rows, 16), clip_rows), at[-1])],
                ref[(*at[:-1], pl.ds(pl.multiple_of(b * clip_rows, 16), clip_rows), at[-1])],
            ],
            axis=0,
        )

    for s in range(SAMPLES):
        begin, size = starts[s], starts[s + 1] - starts[s]
        tiles = (size + 1) // 2

        def members(i):
            second = 2 * i + 1 < size
            return (
                order_ref[begin + 2 * i],
                order_ref[begin + 2 * i + second.astype(jnp.int32)],
                second,
            )

        def bias_of(a, b, second):
            label = lax.dot_general(
                pick,
                two(note_ref, a, b, slice(0, LANES)),
                (((1,), (1,)), ((), ())),
                preferred_element_type=jnp.float32,
            )[:1]
            limit = jnp.where(second, tile, clip_rows)
            good = jnp.logical_and(label == s + 1.0, key_at < limit)
            return jnp.where(good, 0.0, far_below)

        def stacked(pair, a, b):
            query = two(qkv_ref, a, b, 0, slice(pair * LANES, (pair + 1) * LANES))
            blank = jnp.zeros_like(query)
            return jnp.concatenate([jnp.where(low, query, blank), jnp.where(low, blank, query)], axis=0)

        def scores_of(pair, query, a, b, bias):
            keys = two(qkv_ref, a, b, 1, slice(pair * LANES, (pair + 1) * LANES))
            return (
                lax.dot_general(query, keys, (((1,), (1,)), ((), ())), preferred_element_type=jnp.float32)
                + bias
            )

        def mix(pair, shifted, a, b):
            cols = slice(pair * LANES, (pair + 1) * LANES)
            values = jnp.concatenate([two(qkv_ref, a, b, 2, cols), ones], axis=1)
            return jnp.dot(shifted.astype(jnp.bfloat16), values, preferred_element_type=jnp.float32)

        def store(pair, a, b, result):
            cols = slice(pair * LANES, (pair + 1) * LANES)
            shares = result[:, :LANES] / result[:, LANES:]
            mixed = jnp.where(low, shares[:tile], shares[tile:])
            for at, clip in ((clip_rows, b), (0, a)):
                for j, mask in enumerate(masks):
                    piece = mixed[at + j * cap : at + (j + 1) * cap]
                    out_ref[jnp.bitwise_xor(place, mask) * clips + clip, :, cols] = piece.astype(jnp.bfloat16)

        def query_tile(i, carry):
            qa, qb, _ = members(i)

            @pl.when(tiles == 1)
            def _():
                ka, kb, second = members(0)
                bias = bias_of(ka, kb, second)
                for pair in range(pairs):
                    scores = scores_of(pair, stacked(pair, qa, qb), ka, kb, bias)
                    top = jnp.max(scores, axis=-1, keepdims=True)
                    store(pair, qa, qb, mix(pair, jnp.exp2(scores - top), ka, kb))

            @pl.when(tiles > 1)
            def _():
                for pair in range(pairs):
                    m_ref[pair] = jnp.full((2 * tile, LANES), far_below, jnp.float32)
                    r_ref[pair] = jnp.zeros((2 * tile, 2 * LANES), jnp.float32)

                def key_tile(j, inner):
                    ka, kb, second = members(j)
                    bias = bias_of(ka, kb, second)
                    for pair in range(pairs):
                        scores = scores_of(pair, stacked(pair, qa, qb), ka, kb, bias)
                        old = m_ref[pair][:, :1]
                        top = jnp.maximum(old, jnp.max(scores, axis=-1, keepdims=True))
                        r_ref[pair] = r_ref[pair] * jnp.exp2(old - top) + mix(
                            pair, jnp.exp2(scores - top), ka, kb
                        )
                        m_ref[pair] = jnp.broadcast_to(top, (2 * tile, LANES))
                    return inner

                lax.fori_loop(0, tiles, key_tile, 0)
                for pair in range(pairs):
                    store(pair, qa, qb, r_ref[pair])

            return carry

        lax.fori_loop(0, tiles, query_tile, 0)


def collect_kernel(frames, heads, count_ref, onehot_ref, recv_ref, out_ref):
    count = scalar_of(count_ref)
    place = lax.axis_index("head")
    slots, tokens = onehot_ref.shape
    frame = place * frames + lax.broadcasted_iota(jnp.int32, (slots, tokens), 1) // (tokens // frames)
    onehot = jnp.where(frame < count, onehot_ref[...], jnp.zeros((), jnp.bfloat16))
    width = recv_ref.shape[1]
    for h in range(heads):
        picked = lax.dot_general(
            onehot,
            recv_ref[h * slots : (h + 1) * slots, :],
            (((0,), (0,)), ((), ())),
            preferred_element_type=jnp.float32,
        )
        out_ref[:, h * width : (h + 1) * width] = picked.astype(jnp.bfloat16)


def shards(latents, frame_counts, routes, samples, conv_weight, embed_weight, qkv_weight):
    frames_dev, rows, cols, depth = latents.shape[1:]
    heads_dev = lax.axis_size("head")
    bags = lax.axis_size("bag")
    area = rows * cols
    tok_dev = frames_dev * area // 4
    cap = 3 * tok_dev // (2 * bags)
    slots = bags * cap
    local_width = qkv_weight.shape[2]
    chans = conv_weight.shape[2]

    tile = latents.reshape(frames_dev * area, depth)
    count = frame_counts
    edge = jax.ShapeDtypeStruct((area, chans), jnp.float32)
    near, far = pl.pallas_call(
        functools.partial(edge_kernel, rows, cols, frames_dev),
        out_shape=(edge, edge),
        in_specs=[ANY, ANY],
        out_specs=(VMEM, VMEM),
        scratch_shapes=[
            pltpu.VMEM((2 * area, depth), jnp.bfloat16),
            pltpu.VMEM((2 * TAPS * TAPS, depth, chans), jnp.bfloat16),
            pltpu.SemaphoreType.DMA((2, TAPS + 1)),
        ],
        compiler_params=limit(EDGE_LIMIT),
        cost_estimate=pl.CostEstimate(flops=600000000, bytes_accessed=4500000, transcendentals=0),
        name="edge",
    )(tile, conv_weight)
    across = [(i, i + 1) for i in range(1, heads_dev - 1, 2)]
    far = lax.ppermute(far, "head", across + [(j, i) for i, j in across])
    near = lax.ppermute(near, "head", [(i, i ^ 1) for i in range(heads_dev)])

    route_rows = routes[:, 0].reshape(heads_dev, tok_dev)
    row_width = 4 * chans + LANES
    acc, onehot = pl.pallas_call(
        functools.partial(own_kernel, bags, cap, rows, cols, frames_dev),
        out_shape=(
            jax.ShapeDtypeStruct((frames_dev * area, chans), jnp.float32),
            jax.ShapeDtypeStruct((slots, tok_dev), jnp.bfloat16),
        ),
        in_specs=[VMEM, VMEM, VMEM, VMEM],
        out_specs=(VMEM, VMEM),
        compiler_params=limit(16),
        cost_estimate=pl.CostEstimate(flops=1200000000, bytes_accessed=4500000, transcendentals=0),
        name="own",
    )(count, tile, conv_weight, route_rows)
    outgoing = pl.pallas_call(
        functools.partial(join_kernel, rows, cols, frames_dev),
        out_shape=jax.ShapeDtypeStruct((slots, row_width), jnp.bfloat16),
        in_specs=[VMEM] * 7,
        out_specs=VMEM,
        scratch_shapes=[pltpu.VMEM((frames_dev * area, chans), jnp.float32)],
        compiler_params=limit(16),
        cost_estimate=pl.CostEstimate(flops=300000000, bytes_accessed=3000000, transcendentals=0),
        name="join",
    )(count, samples.reshape(heads_dev, tok_dev), acc, near, far, onehot, embed_weight)

    arrived = lax.all_to_all(
        outgoing.reshape(bags, cap, row_width), "bag", split_axis=0, concat_axis=0, tiled=True
    )
    arrived = arrived.reshape(slots, row_width)
    pieces = {0: arrived}
    bit = heads_dev // 2
    swap = [(i, i ^ bit) for i in range(heads_dev)]
    across = lax.ppermute(arrived, "head", swap)
    folded = pl.pallas_call(
        fold_kernel,
        out_shape=jax.ShapeDtypeStruct((3, 2 * embed_weight.shape[0], local_width), jnp.bfloat16),
        in_specs=[VMEM, VMEM, ANY],
        out_specs=VMEM,
        compiler_params=limit(16),
        cost_estimate=pl.CostEstimate(flops=3300000000, bytes_accessed=14000000, transcendentals=0),
        name="fold",
    )(embed_weight, qkv_weight, arrived)
    def spread(start, bits):
        found = dict(start)
        for lower in bits:
            pairs = [(i, i ^ lower) for i in range(heads_dev)]
            found.update({mask | lower: lax.ppermute(piece, "head", pairs) for mask, piece in found.items()})
        return found

    lower_bits = [1 << i for i in reversed(range(bit.bit_length() - 1))]
    close = spread({0: arrived}, lower_bits)

    def project(group, name):
        return pl.pallas_call(
            qkv_kernel,
            out_shape=jax.ShapeDtypeStruct((3, len(group) * slots, local_width), jnp.float32),
            in_specs=[VMEM] * (len(group) + 1),
            out_specs=VMEM,
            compiler_params=limit(16),
            cost_estimate=pl.CostEstimate(
                flops=600000000 * len(group), bytes_accessed=3000000 * len(group), transcendentals=0
            ),
            name=name,
        )(*group, folded)

    near_qkv = project(list(close.values()), "near_qkv")
    across, near_qkv = lax.optimization_barrier((across, near_qkv))
    pieces = dict(close)
    pieces.update(spread({bit: across}, lower_bits))
    across_qkv = project([across], "across_qkv")
    groups = (len(close), 1)
    count_slots = heads_dev * slots
    masks = tuple(pieces)

    pair_rows = 2 * heads_dev * cap
    attended = pl.pallas_call(
        functools.partial(bag_kernel, bags, cap, masks, groups),
        out_shape=jax.ShapeDtypeStruct((heads_dev * bags, cap, local_width), jnp.bfloat16),
        in_specs=[VMEM] * (len(masks) + 3),
        out_specs=VMEM,
        scratch_shapes=[
            pltpu.VMEM((3, count_slots, local_width), jnp.bfloat16),
            pltpu.VMEM((count_slots, LANES), jnp.bfloat16),
            pltpu.VMEM((local_width // LANES, 2 * pair_rows, LANES), jnp.float32),
            pltpu.VMEM((local_width // LANES, 2 * pair_rows, 2 * LANES), jnp.float32),
            pltpu.SMEM((2 * bags,), jnp.int32),
        ],
        compiler_params=limit(28),
        cost_estimate=pl.CostEstimate(flops=3000000000, bytes_accessed=5000000, transcendentals=1200000),
        name="bag",
    )(*pieces.values(), near_qkv, across_qkv, folded)
    received = lax.all_to_all(attended, ("head", "bag"), split_axis=0, concat_axis=0, tiled=True)
    return pl.pallas_call(
        functools.partial(collect_kernel, frames_dev, heads_dev),
        out_shape=jax.ShapeDtypeStruct((tok_dev, heads_dev * local_width), jnp.bfloat16),
        in_specs=[VMEM, VMEM, VMEM],
        out_specs=VMEM,
        compiler_params=limit(16),
        name="collect",
    )(count, onehot, received.reshape(count_slots, local_width))


def solution(mesh):
    placed = (
        P("bag", "head", None, None, None),
        P("bag"),
        P("bag", None),
        P("bag"),
        P(),
        P(),
        P(None, None, "head"),
    )
    return jax.shard_map(
        shards, mesh=mesh, in_specs=placed, out_specs=P(("bag", "head"), None), check_vma=False
    )
```

```python
import functools
import math
import jax
import jax.numpy as jnp
from jax import lax
from jax.experimental import pallas as pl
from jax.experimental.pallas import tpu as pltpu
from jax.sharding import PartitionSpec as P

HDIM = 64
TAPS = 3
SAMPLES = 4
LANES = 128

epsilon = 1e-06
far_below = -1e30

VMEM = pl.BlockSpec(memory_space=pltpu.VMEM)
ANY = pl.BlockSpec(memory_space=pl.ANY)
EDGE_LIMIT = 60


def limit(mib):
    return pltpu.CompilerParams(vmem_limit_bytes=mib << 20)


def slot_of(route_row, bags, cap, stride):
    tokens = route_row.shape[1]
    bag_ids = lax.broadcasted_iota(jnp.int32, (bags, tokens), 0)
    onehot = (bag_ids == route_row).astype(jnp.float32)
    before = (
        lax.broadcasted_iota(jnp.int32, (tokens, tokens), 0)
        < lax.broadcasted_iota(jnp.int32, (tokens, tokens), 1)
    )
    earlier = jnp.dot(
        onehot.astype(jnp.bfloat16),
        before.astype(jnp.float32).astype(jnp.bfloat16),
        preferred_element_type=jnp.float32,
    )
    rank = jnp.sum(earlier * onehot, axis=0, keepdims=True).astype(jnp.int32)
    return route_row * stride + rank


def onehot_of(slot, slots):
    slot_ids = lax.broadcasted_iota(jnp.int32, (slots, slot.shape[1]), 0)
    return (slot_ids == slot).astype(jnp.float32).astype(jnp.bfloat16)


def combine(products, rows, cols):
    chans = products[0].shape[1]
    blank = jnp.zeros((cols, chans), jnp.float32)
    area = rows * cols
    column = lax.broadcasted_iota(jnp.int32, (area, chans), 0) % cols
    total = None
    for e in range(TAPS):
        up, mid, down = products[e], products[TAPS + e], products[2 * TAPS + e]
        merged = (
            mid
            + jnp.concatenate([blank, up[: area - cols]], axis=0)
            + jnp.concatenate([down[cols:], blank], axis=0)
        )
        if e == 0:
            merged = jnp.where(column == 0, 0.0, pltpu.roll(merged, 1, axis=0))
        elif e == 2:
            merged = jnp.where(column == cols - 1, 0.0, pltpu.roll(merged, area - 1, axis=0))
        total = merged if total is None else total + merged
    return total


def plane_products(pieces, w_ref):
    plane = TAPS * TAPS
    chans = w_ref.shape[2]
    stacked = pieces[0][1] if len(pieces) == 1 else jnp.concatenate([x for _, x in pieces], axis=1)
    products = []
    for p in range(0, plane, 2):
        pair = []
        for q in range(p, min(p + 2, plane)):
            taps = [w_ref[plane * t + q] for t, _ in pieces]
            pair.append(taps[0] if len(taps) == 1 else jnp.concatenate(taps, axis=0))
        weight = pair[0] if len(pair) == 1 else jnp.concatenate(pair, axis=1)
        value = jnp.dot(stacked, weight, preferred_element_type=jnp.float32)
        for q in range(len(pair)):
            products.append(value[:, q * chans : (q + 1) * chans])
    return products


def scalar_of(ref):
    return jnp.max(ref[...])


def edge_kernel(rows, cols, frames, x_hbm, w_hbm, near_ref, far_ref, x_ref, w_ref, sems):
    area = rows * cols
    plane = TAPS * TAPS
    jobs = ((frames - 1, 0), (0, 2))
    loads = []
    for i, (f, tap) in enumerate(jobs):
        group = [
            pltpu.make_async_copy(
                x_hbm.at[pl.ds(f * area, area)], x_ref.at[pl.ds(i * area, area)], sems.at[i, TAPS]
            )
        ]
        for row in range(TAPS):
            group.append(
                pltpu.make_async_copy(
                    w_hbm.at[pl.ds(tap * plane + row * TAPS, TAPS)],
                    w_ref.at[pl.ds(i * plane + row * TAPS, TAPS)],
                    sems.at[i, row],
                )
            )
        loads.append(group)
    for group in loads:
        for load in group:
            load.start()
    even = lax.axis_index("head") % 2 == 0
    sums = []
    for i in range(2):
        for load in loads[i]:
            load.wait()
        value = x_ref[i * area : (i + 1) * area, :]
        sums.append(combine(plane_products([(i, value)], w_ref), rows, cols))
    up, down = sums
    near_ref[...] = jnp.where(even, up, down)
    far_ref[...] = jnp.where(even, down, up)


def own_kernel(bags, cap, rows, cols, frames, count_ref, x_ref, w_ref, route_ref, acc_ref, onehot_ref):
    count = scalar_of(count_ref)
    place = lax.axis_index("head")
    area = rows * cols
    first = place * frames
    inputs = []
    for f in range(frames):
        value = x_ref[f * area : (f + 1) * area, :]
        inputs.append(jnp.where(first + f < count, value, jnp.zeros_like(value)))
    for f in range(frames):
        pieces = [(t, inputs[f + t - 1]) for t in range(TAPS) if 0 <= f + t - 1 < frames]
        acc_ref[f * area : (f + 1) * area, :] = combine(plane_products(pieces, w_ref), rows, cols)
    route_row = route_ref[pl.ds(place, 1), :]
    onehot_ref[...] = onehot_of(slot_of(route_row, bags, cap, cap), bags * cap)


def join_kernel(
    rows, cols, frames, count_ref, sample_ref, acc_ref, near_ref, far_ref, onehot_ref, e_ref, out_ref, grid_ref
):
    count = scalar_of(count_ref)
    sample = scalar_of(sample_ref)
    area = rows * cols
    place = lax.axis_index("head")
    even = place % 2 == 0
    first = place * frames
    chans = acc_ref.shape[1]
    near, far = near_ref[...], far_ref[...]
    for f in range(frames):
        part = acc_ref[f * area : (f + 1) * area, :]
        if f == 0:
            before = jnp.logical_and(first > 0, first - 1 < count)
            part = part + jnp.where(before, jnp.where(even, far, near), 0.0)
        if f == frames - 1:
            part = part + jnp.where(first + frames < count, jnp.where(even, near, far), 0.0)
        grid_ref[f * area : (f + 1) * area, :] = jnp.where(first + f < count, part, 0.0)
    pieces = [[None] * 2 for _ in range(2)]
    for odd in range(2):
        half = grid_ref[pl.ds(odd, frames * area // 2, stride=2), :]
        half = half.reshape(frames * rows // 2, 2, cols // 2, chans)
        for i in range(2):
            pieces[i][odd] = half[:, i].reshape(frames * area // 4, chans)
    tokens = frames * area // 4
    patches = jnp.concatenate(
        [pieces[0][0], pieces[0][1], pieces[1][0], pieces[1][1]], axis=1
    ).astype(jnp.bfloat16)
    model = e_ref.shape[1]
    col_tile = 256
    total = None
    for n in range(0, model, col_tile):
        part = jnp.dot(patches, e_ref[:, n : n + col_tile], preferred_element_type=jnp.float32)
        squares = part * part
        both = squares[:, :LANES] + squares[:, LANES:]
        total = both if total is None else total + both
    scale = lax.rsqrt(jnp.sum(total, axis=-1, keepdims=True) * (1.0 / model) + epsilon)
    high = scale.astype(jnp.bfloat16).astype(jnp.float32)
    frame = first + lax.broadcasted_iota(jnp.int32, (tokens, LANES), 0) // (area // 4)
    lane = lax.broadcasted_iota(jnp.int32, (tokens, LANES), 1)
    label = jnp.where(frame < count, sample + 1, 0).astype(jnp.float32)
    notes = jnp.where(lane == 0, label, jnp.where(lane == 1, high, jnp.where(lane == 2, scale - high, 0.0)))
    patches = jnp.concatenate([patches, notes.astype(jnp.bfloat16)], axis=1)
    out_ref[...] = jnp.dot(onehot_ref[...], patches, preferred_element_type=jnp.float32).astype(
        jnp.bfloat16
    )


def fold_kernel(e_ref, w_ref, after_ref, fold_ref):
    feats = e_ref.shape[0]
    width = w_ref.shape[2]
    col_tile = 256
    for m in range(3):
        for n in range(0, width, col_tile):
            cols = slice(n, n + col_tile)
            product = jnp.dot(e_ref[...], w_ref[m, :, cols], preferred_element_type=jnp.float32)
            if m == 0:
                product = product * (HDIM ** (-0.5) * math.log2(math.e))
            high = product.astype(jnp.bfloat16)
            fold_ref[m, :feats, cols] = high
            fold_ref[m, feats:, cols] = (product - high.astype(jnp.float32)).astype(jnp.bfloat16)


def qkv_kernel(*refs):
    pieces, fold_ref, out_ref = refs[:-2], refs[-2], refs[-1]
    for m, at, part in qkv_parts(pieces, fold_ref):
        out_ref[m, :, at : at + part.shape[1]] = part


def qkv_parts(pieces, fold_ref):
    feats = pieces[0].shape[1] - LANES
    col_tile = 256
    patch = jnp.concatenate([ref[:, :feats] for ref in pieces], axis=0)
    notes = jnp.concatenate([ref[:, feats:].astype(jnp.float32) for ref in pieces], axis=0)
    scale = jnp.broadcast_to(notes[:, 1:2] + notes[:, 2:3], (notes.shape[0], col_tile))
    twice = jnp.concatenate([patch, patch], axis=1)
    for m in range(3):
        for n in range(0, fold_ref.shape[2], col_tile):
            part = jnp.dot(twice, fold_ref[m, :, n : n + col_tile], preferred_element_type=jnp.float32)
            yield m, n, part * scale


def bag_kernel(clips, cap, masks, groups, *refs):
    count = len(masks)
    pieces, rest = refs[:count], refs[count:]
    early, rest = rest[: len(groups)], rest[len(groups) :]
    fold_ref, out_ref, qkv_ref, note_ref, m_ref, r_ref, order_ref = rest
    place = lax.axis_index("head")
    slots = pieces[0].shape[0]
    feats = pieces[0].shape[1] - LANES
    width = fold_ref.shape[2]
    clip_rows = count * cap
    done = sum(groups)

    def by_clip(values, c):
        return jnp.concatenate(
            [
                value[j * slots + c * cap : j * slots + (c + 1) * cap]
                for value in values
                for j in range(value.shape[0] // slots)
            ],
            axis=0,
        )

    notes = [ref[:, feats:].astype(jnp.float32) for ref in pieces]
    for c in range(clips):
        note = by_clip(notes, c)
        note_ref[c * clip_rows : (c + 1) * clip_rows, :] = note.astype(jnp.bfloat16)
        order_ref[clips + c] = jnp.max(note[:, :1]).astype(jnp.int32)
    starts = [jnp.int32(0)]
    for s in range(SAMPLES):

        def keep_clip(c, at):
            hit = order_ref[clips + c] == s + 1

            @pl.when(hit)
            def _():
                order_ref[at] = c

            return at + hit.astype(jnp.int32)

        starts.append(lax.fori_loop(0, clips, keep_clip, starts[-1]))

    for m, at, part in qkv_parts(pieces[done:], fold_ref):
        cols = slice(at, at + part.shape[1])
        parts = [ref[m, :, cols] for ref in early] + [part]
        for c in range(clips):
            qkv_ref[m, c * clip_rows : (c + 1) * clip_rows, cols] = by_clip(parts, c).astype(jnp.bfloat16)

    out_ref[...] = jnp.zeros_like(out_ref)
    tile = 2 * clip_rows
    lane = lax.broadcasted_iota(jnp.int32, (tile, LANES), 1)
    low = lane < HDIM
    pairs = width // LANES
    ones = jnp.ones((tile, LANES), jnp.bfloat16)
    pick = (lax.broadcasted_iota(jnp.int32, (8, LANES), 1) == 0).astype(jnp.float32).astype(jnp.bfloat16)
    key_at = lax.broadcasted_iota(jnp.int32, (1, tile), 1)

    def two(ref, a, b, *at):
        return jnp.concatenate(
            [
                ref[(*at[:-1], pl.ds(pl.multiple_of(a * clip_rows, 16), clip_rows), at[-1])],
                ref[(*at[:-1], pl.ds(pl.multiple_of(b * clip_rows, 16), clip_rows), at[-1])],
            ],
            axis=0,
        )

    for s in range(SAMPLES):
        begin, size = starts[s], starts[s + 1] - starts[s]
        tiles = (size + 1) // 2

        def members(i):
            second = 2 * i + 1 < size
            return (
                order_ref[begin + 2 * i],
                order_ref[begin + 2 * i + second.astype(jnp.int32)],
                second,
            )

        def bias_of(a, b, second):
            label = lax.dot_general(
                pick,
                two(note_ref, a, b, slice(0, LANES)),
                (((1,), (1,)), ((), ())),
                preferred_element_type=jnp.float32,
            )[:1]
            limit = jnp.where(second, tile, clip_rows)
            good = jnp.logical_and(label == s + 1.0, key_at < limit)
            return jnp.where(good, 0.0, far_below)

        def stacked(pair, a, b):
            query = two(qkv_ref, a, b, 0, slice(pair * LANES, (pair + 1) * LANES))
            blank = jnp.zeros_like(query)
            return jnp.concatenate([jnp.where(low, query, blank), jnp.where(low, blank, query)], axis=0)

        def scores_of(pair, query, a, b, bias):
            keys = two(qkv_ref, a, b, 1, slice(pair * LANES, (pair + 1) * LANES))
            return (
                lax.dot_general(query, keys, (((1,), (1,)), ((), ())), preferred_element_type=jnp.float32)
                + bias
            )

        def mix(pair, shifted, a, b):
            values = two(qkv_ref, a, b, 2, slice(pair * LANES, (pair + 1) * LANES))
            weights = shifted.astype(jnp.bfloat16)
            sides = (jnp.where(low, values, ones), jnp.where(low, ones, values))
            return jnp.concatenate(
                [
                    jnp.dot(weights[i * tile : (i + 1) * tile], side, preferred_element_type=jnp.float32)
                    for i, side in enumerate(sides)
                ],
                axis=0,
            )

        def store(pair, a, b, result):
            cols = slice(pair * LANES, (pair + 1) * LANES)
            sums = pltpu.roll(jnp.where(low, result[tile:], result[:tile]), HDIM, axis=1)
            mixed = jnp.where(low, result[:tile], result[tile:]) / sums
            for at, clip in ((clip_rows, b), (0, a)):
                for j, mask in enumerate(masks):
                    piece = mixed[at + j * cap : at + (j + 1) * cap]
                    out_ref[jnp.bitwise_xor(place, mask) * clips + clip, :, cols] = piece.astype(jnp.bfloat16)

        def query_tile(i, carry):
            qa, qb, _ = members(i)

            @pl.when(tiles == 1)
            def _():
                ka, kb, second = members(0)
                bias = bias_of(ka, kb, second)
                for pair in range(pairs):
                    scores = scores_of(pair, stacked(pair, qa, qb), ka, kb, bias)
                    top = jnp.max(scores, axis=-1, keepdims=True)
                    store(pair, qa, qb, mix(pair, jnp.exp2(scores - top), ka, kb))

            @pl.when(tiles > 1)
            def _():
                for pair in range(pairs):
                    m_ref[pair] = jnp.full((2 * tile, LANES), far_below, jnp.float32)
                    r_ref[pair] = jnp.zeros((2 * tile, LANES), jnp.float32)

                def key_tile(j, inner):
                    ka, kb, second = members(j)
                    bias = bias_of(ka, kb, second)
                    for pair in range(pairs):
                        scores = scores_of(pair, stacked(pair, qa, qb), ka, kb, bias)
                        old = m_ref[pair][:, :1]
                        top = jnp.maximum(old, jnp.max(scores, axis=-1, keepdims=True))
                        r_ref[pair] = r_ref[pair] * jnp.exp2(old - top) + mix(
                            pair, jnp.exp2(scores - top), ka, kb
                        )
                        m_ref[pair] = jnp.broadcast_to(top, (2 * tile, LANES))
                    return inner

                lax.fori_loop(0, tiles, key_tile, 0)
                for pair in range(pairs):
                    store(pair, qa, qb, r_ref[pair])

            return carry

        lax.fori_loop(0, tiles, query_tile, 0)


def collect_kernel(frames, heads, count_ref, onehot_ref, recv_ref, out_ref):
    count = scalar_of(count_ref)
    place = lax.axis_index("head")
    slots, tokens = onehot_ref.shape
    frame = place * frames + lax.broadcasted_iota(jnp.int32, (slots, tokens), 1) // (tokens // frames)
    onehot = jnp.where(frame < count, onehot_ref[...], jnp.zeros((), jnp.bfloat16))
    width = recv_ref.shape[1]
    for h in range(heads):
        picked = lax.dot_general(
            onehot,
            recv_ref[h * slots : (h + 1) * slots, :],
            (((0,), (0,)), ((), ())),
            preferred_element_type=jnp.float32,
        )
        out_ref[:, h * width : (h + 1) * width] = picked.astype(jnp.bfloat16)


def shards(latents, frame_counts, routes, samples, conv_weight, embed_weight, qkv_weight):
    frames_dev, rows, cols, depth = latents.shape[1:]
    heads_dev = lax.axis_size("head")
    bags = lax.axis_size("bag")
    area = rows * cols
    tok_dev = frames_dev * area // 4
    cap = 3 * tok_dev // (2 * bags)
    slots = bags * cap
    local_width = qkv_weight.shape[2]
    chans = conv_weight.shape[2]

    tile = latents.reshape(frames_dev * area, depth)
    count = frame_counts
    edge = jax.ShapeDtypeStruct((area, chans), jnp.float32)
    near, far = pl.pallas_call(
        functools.partial(edge_kernel, rows, cols, frames_dev),
        out_shape=(edge, edge),
        in_specs=[ANY, ANY],
        out_specs=(VMEM, VMEM),
        scratch_shapes=[
            pltpu.VMEM((2 * area, depth), jnp.bfloat16),
            pltpu.VMEM((2 * TAPS * TAPS, depth, chans), jnp.bfloat16),
            pltpu.SemaphoreType.DMA((2, TAPS + 1)),
        ],
        compiler_params=limit(EDGE_LIMIT),
        cost_estimate=pl.CostEstimate(flops=600000000, bytes_accessed=4500000, transcendentals=0),
        name="edge",
    )(tile, conv_weight)
    across = [(i, i + 1) for i in range(1, heads_dev - 1, 2)]
    far = lax.ppermute(far, "head", across + [(j, i) for i, j in across])
    near = lax.ppermute(near, "head", [(i, i ^ 1) for i in range(heads_dev)])

    route_rows = routes[:, 0].reshape(heads_dev, tok_dev)
    row_width = 4 * chans + LANES
    acc, onehot = pl.pallas_call(
        functools.partial(own_kernel, bags, cap, rows, cols, frames_dev),
        out_shape=(
            jax.ShapeDtypeStruct((frames_dev * area, chans), jnp.float32),
            jax.ShapeDtypeStruct((slots, tok_dev), jnp.bfloat16),
        ),
        in_specs=[VMEM, VMEM, VMEM, VMEM],
        out_specs=(VMEM, VMEM),
        compiler_params=limit(16),
        cost_estimate=pl.CostEstimate(flops=1200000000, bytes_accessed=4500000, transcendentals=0),
        name="own",
    )(count, tile, conv_weight, route_rows)
    outgoing = pl.pallas_call(
        functools.partial(join_kernel, rows, cols, frames_dev),
        out_shape=jax.ShapeDtypeStruct((slots, row_width), jnp.bfloat16),
        in_specs=[VMEM] * 7,
        out_specs=VMEM,
        scratch_shapes=[pltpu.VMEM((frames_dev * area, chans), jnp.float32)],
        compiler_params=limit(16),
        cost_estimate=pl.CostEstimate(flops=300000000, bytes_accessed=3000000, transcendentals=0),
        name="join",
    )(count, samples.reshape(heads_dev, tok_dev), acc, near, far, onehot, embed_weight)

    arrived = lax.all_to_all(
        outgoing.reshape(bags, cap, row_width), "bag", split_axis=0, concat_axis=0, tiled=True
    )
    arrived = arrived.reshape(slots, row_width)
    pieces = {0: arrived}
    bit = heads_dev // 2
    swap = [(i, i ^ bit) for i in range(heads_dev)]
    across = lax.ppermute(arrived, "head", swap)
    folded = pl.pallas_call(
        fold_kernel,
        out_shape=jax.ShapeDtypeStruct((3, 2 * embed_weight.shape[0], local_width), jnp.bfloat16),
        in_specs=[VMEM, VMEM, ANY],
        out_specs=VMEM,
        compiler_params=limit(16),
        cost_estimate=pl.CostEstimate(flops=3300000000, bytes_accessed=14000000, transcendentals=0),
        name="fold",
    )(embed_weight, qkv_weight, arrived)
    def spread(start, bits):
        found = dict(start)
        for lower in bits:
            pairs = [(i, i ^ lower) for i in range(heads_dev)]
            found.update({mask | lower: lax.ppermute(piece, "head", pairs) for mask, piece in found.items()})
        return found

    lower_bits = [1 << i for i in reversed(range(bit.bit_length() - 1))]
    close = spread({0: arrived}, lower_bits)

    def project(group, name):
        return pl.pallas_call(
            qkv_kernel,
            out_shape=jax.ShapeDtypeStruct((3, len(group) * slots, local_width), jnp.float32),
            in_specs=[VMEM] * (len(group) + 1),
            out_specs=VMEM,
            compiler_params=limit(16),
            cost_estimate=pl.CostEstimate(
                flops=600000000 * len(group), bytes_accessed=3000000 * len(group), transcendentals=0
            ),
            name=name,
        )(*group, folded)

    near_qkv = project(list(close.values()), "near_qkv")
    across, near_qkv = lax.optimization_barrier((across, near_qkv))
    pieces = dict(close)
    pieces.update(spread({bit: across}, lower_bits))
    across_qkv = project([across], "across_qkv")
    groups = (len(close), 1)
    count_slots = heads_dev * slots
    masks = tuple(pieces)

    pair_rows = 2 * heads_dev * cap
    attended = pl.pallas_call(
        functools.partial(bag_kernel, bags, cap, masks, groups),
        out_shape=jax.ShapeDtypeStruct((heads_dev * bags, cap, local_width), jnp.bfloat16),
        in_specs=[VMEM] * (len(masks) + 3),
        out_specs=VMEM,
        scratch_shapes=[
            pltpu.VMEM((3, count_slots, local_width), jnp.bfloat16),
            pltpu.VMEM((count_slots, LANES), jnp.bfloat16),
            pltpu.VMEM((local_width // LANES, 2 * pair_rows, LANES), jnp.float32),
            pltpu.VMEM((local_width // LANES, 2 * pair_rows, LANES), jnp.float32),
            pltpu.SMEM((2 * bags,), jnp.int32),
        ],
        compiler_params=limit(28),
        cost_estimate=pl.CostEstimate(flops=3000000000, bytes_accessed=5000000, transcendentals=1200000),
        name="bag",
    )(*pieces.values(), near_qkv, across_qkv, folded)
    received = lax.all_to_all(attended, ("head", "bag"), split_axis=0, concat_axis=0, tiled=True)
    return pl.pallas_call(
        functools.partial(collect_kernel, frames_dev, heads_dev),
        out_shape=jax.ShapeDtypeStruct((tok_dev, heads_dev * local_width), jnp.bfloat16),
        in_specs=[VMEM, VMEM, VMEM],
        out_specs=VMEM,
        compiler_params=limit(16),
        name="collect",
    )(count, onehot, received.reshape(count_slots, local_width))


def solution(mesh):
    placed = (
        P("bag", "head", None, None, None),
        P("bag"),
        P("bag", None),
        P("bag"),
        P(),
        P(),
        P(None, None, "head"),
    )
    return jax.shard_map(
        shards, mesh=mesh, in_specs=placed, out_specs=P(("bag", "head"), None), check_vma=False
    )
```

```python
import functools
import math
import jax
import jax.numpy as jnp
from jax import lax
from jax.experimental import pallas as pl
from jax.experimental.pallas import tpu as pltpu
from jax.sharding import PartitionSpec as P

HDIM = 64
TAPS = 3
SAMPLES = 4
LANES = 128

epsilon = 1e-06
far_below = -1e30

VMEM = pl.BlockSpec(memory_space=pltpu.VMEM)
ANY = pl.BlockSpec(memory_space=pl.ANY)
EDGE_LIMIT = 60


def limit(mib):
    return pltpu.CompilerParams(vmem_limit_bytes=mib << 20)


def slot_of(route_row, bags, cap, stride):
    tokens = route_row.shape[1]
    bag_ids = lax.broadcasted_iota(jnp.int32, (bags, tokens), 0)
    onehot = (bag_ids == route_row).astype(jnp.float32)
    before = (
        lax.broadcasted_iota(jnp.int32, (tokens, tokens), 0)
        < lax.broadcasted_iota(jnp.int32, (tokens, tokens), 1)
    )
    earlier = jnp.dot(
        onehot.astype(jnp.bfloat16),
        before.astype(jnp.float32).astype(jnp.bfloat16),
        preferred_element_type=jnp.float32,
    )
    rank = jnp.sum(earlier * onehot, axis=0, keepdims=True).astype(jnp.int32)
    return route_row * stride + rank


def onehot_of(slot, slots):
    slot_ids = lax.broadcasted_iota(jnp.int32, (slots, slot.shape[1]), 0)
    return (slot_ids == slot).astype(jnp.float32).astype(jnp.bfloat16)


def combine(products, rows, cols):
    chans = products[0].shape[1]
    blank = jnp.zeros((cols, chans), jnp.float32)
    area = rows * cols
    column = lax.broadcasted_iota(jnp.int32, (area, chans), 0) % cols
    total = None
    for e in range(TAPS):
        up, mid, down = products[e], products[TAPS + e], products[2 * TAPS + e]
        merged = (
            mid
            + jnp.concatenate([blank, up[: area - cols]], axis=0)
            + jnp.concatenate([down[cols:], blank], axis=0)
        )
        if e == 0:
            merged = jnp.where(column == 0, 0.0, pltpu.roll(merged, 1, axis=0))
        elif e == 2:
            merged = jnp.where(column == cols - 1, 0.0, pltpu.roll(merged, area - 1, axis=0))
        total = merged if total is None else total + merged
    return total


def plane_products(pieces, w_ref):
    plane = TAPS * TAPS
    chans = w_ref.shape[2]
    stacked = pieces[0][1] if len(pieces) == 1 else jnp.concatenate([x for _, x in pieces], axis=1)
    products = []
    for p in range(0, plane, 2):
        pair = []
        for q in range(p, min(p + 2, plane)):
            taps = [w_ref[plane * t + q] for t, _ in pieces]
            pair.append(taps[0] if len(taps) == 1 else jnp.concatenate(taps, axis=0))
        weight = pair[0] if len(pair) == 1 else jnp.concatenate(pair, axis=1)
        value = jnp.dot(stacked, weight, preferred_element_type=jnp.float32)
        for q in range(len(pair)):
            products.append(value[:, q * chans : (q + 1) * chans])
    return products


def scalar_of(ref):
    return jnp.max(ref[...])


def edge_kernel(rows, cols, frames, x_hbm, w_hbm, near_ref, far_ref, x_ref, w_ref, sems):
    area = rows * cols
    plane = TAPS * TAPS
    jobs = ((frames - 1, 0), (0, 2))
    loads = []
    for i, (f, tap) in enumerate(jobs):
        group = [
            pltpu.make_async_copy(
                x_hbm.at[pl.ds(f * area, area)], x_ref.at[pl.ds(i * area, area)], sems.at[i, TAPS]
            )
        ]
        for row in range(TAPS):
            group.append(
                pltpu.make_async_copy(
                    w_hbm.at[pl.ds(tap * plane + row * TAPS, TAPS)],
                    w_ref.at[pl.ds(i * plane + row * TAPS, TAPS)],
                    sems.at[i, row],
                )
            )
        loads.append(group)
    for group in loads:
        for load in group:
            load.start()
    even = lax.axis_index("head") % 2 == 0
    sums = []
    for i in range(2):
        for load in loads[i]:
            load.wait()
        value = x_ref[i * area : (i + 1) * area, :]
        sums.append(combine(plane_products([(i, value)], w_ref), rows, cols))
    up, down = sums
    near_ref[...] = jnp.where(even, up, down)
    far_ref[...] = jnp.where(even, down, up)


def own_kernel(bags, cap, rows, cols, frames, count_ref, x_ref, w_ref, route_ref, acc_ref, onehot_ref):
    count = scalar_of(count_ref)
    place = lax.axis_index("head")
    area = rows * cols
    first = place * frames
    inputs = []
    for f in range(frames):
        value = x_ref[f * area : (f + 1) * area, :]
        inputs.append(jnp.where(first + f < count, value, jnp.zeros_like(value)))
    for f in range(frames):
        pieces = [(t, inputs[f + t - 1]) for t in range(TAPS) if 0 <= f + t - 1 < frames]
        acc_ref[f * area : (f + 1) * area, :] = combine(plane_products(pieces, w_ref), rows, cols)
    route_row = route_ref[pl.ds(place, 1), :]
    onehot_ref[...] = onehot_of(slot_of(route_row, bags, cap, cap), bags * cap)


def join_kernel(
    rows, cols, frames, count_ref, sample_ref, acc_ref, near_ref, far_ref, onehot_ref, e_ref, out_ref, grid_ref
):
    count = scalar_of(count_ref)
    sample = scalar_of(sample_ref)
    area = rows * cols
    place = lax.axis_index("head")
    even = place % 2 == 0
    first = place * frames
    chans = acc_ref.shape[1]
    near, far = near_ref[...], far_ref[...]
    for f in range(frames):
        part = acc_ref[f * area : (f + 1) * area, :]
        if f == 0:
            before = jnp.logical_and(first > 0, first - 1 < count)
            part = part + jnp.where(before, jnp.where(even, far, near), 0.0)
        if f == frames - 1:
            part = part + jnp.where(first + frames < count, jnp.where(even, near, far), 0.0)
        grid_ref[f * area : (f + 1) * area, :] = jnp.where(first + f < count, part, 0.0)
    pieces = [[None] * 2 for _ in range(2)]
    for odd in range(2):
        half = grid_ref[pl.ds(odd, frames * area // 2, stride=2), :]
        half = half.reshape(frames * rows // 2, 2, cols // 2, chans)
        for i in range(2):
            pieces[i][odd] = half[:, i].reshape(frames * area // 4, chans)
    tokens = frames * area // 4
    patches = jnp.concatenate(
        [pieces[0][0], pieces[0][1], pieces[1][0], pieces[1][1]], axis=1
    ).astype(jnp.bfloat16)
    model = e_ref.shape[1]
    col_tile = 256
    total = None
    for n in range(0, model, col_tile):
        part = jnp.dot(patches, e_ref[:, n : n + col_tile], preferred_element_type=jnp.float32)
        squares = part * part
        both = squares[:, :LANES] + squares[:, LANES:]
        total = both if total is None else total + both
    scale = lax.rsqrt(jnp.sum(total, axis=-1, keepdims=True) * (1.0 / model) + epsilon)
    high = scale.astype(jnp.bfloat16).astype(jnp.float32)
    frame = first + lax.broadcasted_iota(jnp.int32, (tokens, LANES), 0) // (area // 4)
    lane = lax.broadcasted_iota(jnp.int32, (tokens, LANES), 1)
    label = jnp.where(frame < count, sample + 1, 0).astype(jnp.float32)
    notes = jnp.where(lane == 0, label, jnp.where(lane == 1, high, jnp.where(lane == 2, scale - high, 0.0)))
    patches = jnp.concatenate([patches, notes.astype(jnp.bfloat16)], axis=1)
    out_ref[...] = jnp.dot(onehot_ref[...], patches, preferred_element_type=jnp.float32).astype(
        jnp.bfloat16
    )


def fold_kernel(e_ref, w_ref, after_ref, fold_ref):
    feats = e_ref.shape[0]
    width = w_ref.shape[2]
    col_tile = 256
    for m in range(3):
        for n in range(0, width, col_tile):
            cols = slice(n, n + col_tile)
            product = jnp.dot(e_ref[...], w_ref[m, :, cols], preferred_element_type=jnp.float32)
            if m == 0:
                product = product * (HDIM ** (-0.5) * math.log2(math.e))
            high = product.astype(jnp.bfloat16)
            fold_ref[m, :feats, cols] = high
            fold_ref[m, feats:, cols] = (product - high.astype(jnp.float32)).astype(jnp.bfloat16)


def qkv_kernel(*refs):
    pieces, fold_ref, out_ref = refs[:-2], refs[-2], refs[-1]
    for m, at, part in qkv_parts(pieces, fold_ref):
        out_ref[m, :, at : at + part.shape[1]] = part


def qkv_parts(pieces, fold_ref):
    feats = pieces[0].shape[1] - LANES
    col_tile = 256
    patch = jnp.concatenate([ref[:, :feats] for ref in pieces], axis=0)
    notes = jnp.concatenate([ref[:, feats:].astype(jnp.float32) for ref in pieces], axis=0)
    scale = jnp.broadcast_to(notes[:, 1:2] + notes[:, 2:3], (notes.shape[0], col_tile))
    twice = jnp.concatenate([patch, patch], axis=1)
    for m in range(3):
        for n in range(0, fold_ref.shape[2], col_tile):
            part = jnp.dot(twice, fold_ref[m, :, n : n + col_tile], preferred_element_type=jnp.float32)
            yield m, n, part * scale


def bag_kernel(clips, cap, masks, groups, *refs):
    count = len(masks)
    pieces, rest = refs[:count], refs[count:]
    early, rest = rest[: len(groups)], rest[len(groups) :]
    fold_ref, out_ref, qkv_ref, note_ref, m_ref, r_ref, order_ref = rest
    place = lax.axis_index("head")
    slots = pieces[0].shape[0]
    feats = pieces[0].shape[1] - LANES
    width = fold_ref.shape[2]
    clip_rows = count * cap
    done = sum(groups)

    def by_clip(values, c):
        return jnp.concatenate(
            [
                value[j * slots + c * cap : j * slots + (c + 1) * cap]
                for value in values
                for j in range(value.shape[0] // slots)
            ],
            axis=0,
        )

    notes = [ref[:, feats:].astype(jnp.float32) for ref in pieces]
    for c in range(clips):
        note = by_clip(notes, c)
        note_ref[c * clip_rows : (c + 1) * clip_rows, :] = note.astype(jnp.bfloat16)
        order_ref[clips + c] = jnp.max(note[:, :1]).astype(jnp.int32)
    starts = [jnp.int32(0)]
    for s in range(SAMPLES):

        def keep_clip(c, at):
            hit = order_ref[clips + c] == s + 1

            @pl.when(hit)
            def _():
                order_ref[at] = c

            return at + hit.astype(jnp.int32)

        starts.append(lax.fori_loop(0, clips, keep_clip, starts[-1]))

    for m, at, part in qkv_parts(pieces[done:], fold_ref):
        cols = slice(at, at + part.shape[1])
        parts = [ref[m, :, cols] for ref in early] + [part]
        for c in range(clips):
            qkv_ref[m, c * clip_rows : (c + 1) * clip_rows, cols] = by_clip(parts, c).astype(jnp.bfloat16)

    for c in range(clips):

        @pl.when(order_ref[clips + c] == 0)
        def _():
            for j in range(count):
                out_ref[j * clips + c] = jnp.zeros(out_ref.shape[1:], out_ref.dtype)

    tile = 2 * clip_rows
    lane = lax.broadcasted_iota(jnp.int32, (tile, LANES), 1)
    low = lane < HDIM
    pairs = width // LANES
    ones = jnp.ones((tile, LANES), jnp.bfloat16)
    pick = (lax.broadcasted_iota(jnp.int32, (8, LANES), 1) == 0).astype(jnp.float32).astype(jnp.bfloat16)
    key_at = lax.broadcasted_iota(jnp.int32, (1, tile), 1)

    def two(ref, a, b, *at):
        return jnp.concatenate(
            [
                ref[(*at[:-1], pl.ds(pl.multiple_of(a * clip_rows, 16), clip_rows), at[-1])],
                ref[(*at[:-1], pl.ds(pl.multiple_of(b * clip_rows, 16), clip_rows), at[-1])],
            ],
            axis=0,
        )

    for s in range(SAMPLES):
        begin, size = starts[s], starts[s + 1] - starts[s]
        tiles = (size + 1) // 2

        def members(i):
            second = 2 * i + 1 < size
            return (
                order_ref[begin + 2 * i],
                order_ref[begin + 2 * i + second.astype(jnp.int32)],
                second,
            )

        def bias_of(a, b, second):
            label = lax.dot_general(
                pick,
                two(note_ref, a, b, slice(0, LANES)),
                (((1,), (1,)), ((), ())),
                preferred_element_type=jnp.float32,
            )[:1]
            limit = jnp.where(second, tile, clip_rows)
            good = jnp.logical_and(label == s + 1.0, key_at < limit)
            return jnp.where(good, 0.0, far_below)

        def stacked(pair, a, b):
            query = two(qkv_ref, a, b, 0, slice(pair * LANES, (pair + 1) * LANES))
            blank = jnp.zeros_like(query)
            return jnp.concatenate([jnp.where(low, query, blank), jnp.where(low, blank, query)], axis=0)

        def scores_of(pair, query, a, b, bias):
            keys = two(qkv_ref, a, b, 1, slice(pair * LANES, (pair + 1) * LANES))
            return (
                lax.dot_general(query, keys, (((1,), (1,)), ((), ())), preferred_element_type=jnp.float32)
                + bias
            )

        def mix(pair, shifted, a, b):
            cols = slice(pair * LANES, (pair + 1) * LANES)
            values = jnp.concatenate([two(qkv_ref, a, b, 2, cols), ones], axis=1)
            return jnp.dot(shifted.astype(jnp.bfloat16), values, preferred_element_type=jnp.float32)

        def store(pair, a, b, result):
            cols = slice(pair * LANES, (pair + 1) * LANES)
            shares = result[:, :LANES] / result[:, LANES:]
            mixed = jnp.where(low, shares[:tile], shares[tile:])
            for at, clip in ((clip_rows, b), (0, a)):
                for j, mask in enumerate(masks):
                    piece = mixed[at + j * cap : at + (j + 1) * cap]
                    out_ref[jnp.bitwise_xor(place, mask) * clips + clip, :, cols] = piece.astype(jnp.bfloat16)

        def query_tile(i, carry):
            qa, qb, _ = members(i)

            @pl.when(tiles == 1)
            def _():
                ka, kb, second = members(0)
                bias = bias_of(ka, kb, second)
                for pair in range(pairs):
                    scores = scores_of(pair, stacked(pair, qa, qb), ka, kb, bias)
                    top = jnp.max(scores, axis=-1, keepdims=True)
                    store(pair, qa, qb, mix(pair, jnp.exp2(scores - top), ka, kb))

            @pl.when(tiles > 1)
            def _():
                for pair in range(pairs):
                    m_ref[pair] = jnp.full((2 * tile, LANES), far_below, jnp.float32)
                    r_ref[pair] = jnp.zeros((2 * tile, 2 * LANES), jnp.float32)

                def key_tile(j, inner):
                    ka, kb, second = members(j)
                    bias = bias_of(ka, kb, second)
                    for pair in range(pairs):
                        scores = scores_of(pair, stacked(pair, qa, qb), ka, kb, bias)
                        old = m_ref[pair][:, :1]
                        top = jnp.maximum(old, jnp.max(scores, axis=-1, keepdims=True))
                        r_ref[pair] = r_ref[pair] * jnp.exp2(old - top) + mix(
                            pair, jnp.exp2(scores - top), ka, kb
                        )
                        m_ref[pair] = jnp.broadcast_to(top, (2 * tile, LANES))
                    return inner

                lax.fori_loop(0, tiles, key_tile, 0)
                for pair in range(pairs):
                    store(pair, qa, qb, r_ref[pair])

            return carry

        lax.fori_loop(0, tiles, query_tile, 0)


def collect_kernel(frames, heads, count_ref, onehot_ref, recv_ref, out_ref):
    count = scalar_of(count_ref)
    place = lax.axis_index("head")
    slots, tokens = onehot_ref.shape
    frame = place * frames + lax.broadcasted_iota(jnp.int32, (slots, tokens), 1) // (tokens // frames)
    onehot = jnp.where(frame < count, onehot_ref[...], jnp.zeros((), jnp.bfloat16))
    width = recv_ref.shape[1]
    for h in range(heads):
        picked = lax.dot_general(
            onehot,
            recv_ref[h * slots : (h + 1) * slots, :],
            (((0,), (0,)), ((), ())),
            preferred_element_type=jnp.float32,
        )
        out_ref[:, h * width : (h + 1) * width] = picked.astype(jnp.bfloat16)


def shards(latents, frame_counts, routes, samples, conv_weight, embed_weight, qkv_weight):
    frames_dev, rows, cols, depth = latents.shape[1:]
    heads_dev = lax.axis_size("head")
    bags = lax.axis_size("bag")
    area = rows * cols
    tok_dev = frames_dev * area // 4
    cap = 3 * tok_dev // (2 * bags)
    slots = bags * cap
    local_width = qkv_weight.shape[2]
    chans = conv_weight.shape[2]

    tile = latents.reshape(frames_dev * area, depth)
    count = frame_counts
    edge = jax.ShapeDtypeStruct((area, chans), jnp.float32)
    near, far = pl.pallas_call(
        functools.partial(edge_kernel, rows, cols, frames_dev),
        out_shape=(edge, edge),
        in_specs=[ANY, ANY],
        out_specs=(VMEM, VMEM),
        scratch_shapes=[
            pltpu.VMEM((2 * area, depth), jnp.bfloat16),
            pltpu.VMEM((2 * TAPS * TAPS, depth, chans), jnp.bfloat16),
            pltpu.SemaphoreType.DMA((2, TAPS + 1)),
        ],
        compiler_params=limit(EDGE_LIMIT),
        cost_estimate=pl.CostEstimate(flops=600000000, bytes_accessed=4500000, transcendentals=0),
        name="edge",
    )(tile, conv_weight)
    across = [(i, i + 1) for i in range(1, heads_dev - 1, 2)]
    far = lax.ppermute(far, "head", across + [(j, i) for i, j in across])
    near = lax.ppermute(near, "head", [(i, i ^ 1) for i in range(heads_dev)])

    route_rows = routes[:, 0].reshape(heads_dev, tok_dev)
    row_width = 4 * chans + LANES
    acc, onehot = pl.pallas_call(
        functools.partial(own_kernel, bags, cap, rows, cols, frames_dev),
        out_shape=(
            jax.ShapeDtypeStruct((frames_dev * area, chans), jnp.float32),
            jax.ShapeDtypeStruct((slots, tok_dev), jnp.bfloat16),
        ),
        in_specs=[VMEM, VMEM, VMEM, VMEM],
        out_specs=(VMEM, VMEM),
        compiler_params=limit(16),
        cost_estimate=pl.CostEstimate(flops=4000000000, bytes_accessed=4500000, transcendentals=0),
        name="own",
    )(count, tile, conv_weight, route_rows)
    outgoing = pl.pallas_call(
        functools.partial(join_kernel, rows, cols, frames_dev),
        out_shape=jax.ShapeDtypeStruct((slots, row_width), jnp.bfloat16),
        in_specs=[VMEM] * 7,
        out_specs=VMEM,
        scratch_shapes=[pltpu.VMEM((frames_dev * area, chans), jnp.float32)],
        compiler_params=limit(16),
        cost_estimate=pl.CostEstimate(flops=300000000, bytes_accessed=3000000, transcendentals=0),
        name="join",
    )(count, samples.reshape(heads_dev, tok_dev), acc, near, far, onehot, embed_weight)

    arrived = lax.all_to_all(
        outgoing.reshape(bags, cap, row_width), "bag", split_axis=0, concat_axis=0, tiled=True
    )
    arrived = arrived.reshape(slots, row_width)
    pieces = {0: arrived}
    bit = heads_dev // 2
    swap = [(i, i ^ bit) for i in range(heads_dev)]
    across = lax.ppermute(arrived, "head", swap)
    folded = pl.pallas_call(
        fold_kernel,
        out_shape=jax.ShapeDtypeStruct((3, 2 * embed_weight.shape[0], local_width), jnp.bfloat16),
        in_specs=[VMEM, VMEM, ANY],
        out_specs=VMEM,
        compiler_params=limit(16),
        cost_estimate=pl.CostEstimate(flops=3300000000, bytes_accessed=14000000, transcendentals=0),
        name="fold",
    )(embed_weight, qkv_weight, arrived)
    def spread(start, bits):
        found = dict(start)
        for lower in bits:
            pairs = [(i, i ^ lower) for i in range(heads_dev)]
            found.update({mask | lower: lax.ppermute(piece, "head", pairs) for mask, piece in found.items()})
        return found

    lower_bits = [1 << i for i in reversed(range(bit.bit_length() - 1))]
    close = spread({0: arrived}, lower_bits)

    def project(group, name):
        return pl.pallas_call(
            qkv_kernel,
            out_shape=jax.ShapeDtypeStruct((3, len(group) * slots, local_width), jnp.float32),
            in_specs=[VMEM] * (len(group) + 1),
            out_specs=VMEM,
            compiler_params=limit(16),
            cost_estimate=pl.CostEstimate(
                flops=600000000 * len(group), bytes_accessed=3000000 * len(group), transcendentals=0
            ),
            name=name,
        )(*group, folded)

    near_qkv = project(list(close.values()), "near_qkv")
    across, near_qkv = lax.optimization_barrier((across, near_qkv))
    pieces = dict(close)
    pieces.update(spread({bit: across}, lower_bits))
    across_qkv = project([across], "across_qkv")
    groups = (len(close), 1)
    count_slots = heads_dev * slots
    masks = tuple(pieces)

    pair_rows = 2 * heads_dev * cap
    attended = pl.pallas_call(
        functools.partial(bag_kernel, bags, cap, masks, groups),
        out_shape=jax.ShapeDtypeStruct((heads_dev * bags, cap, local_width), jnp.bfloat16),
        in_specs=[VMEM] * (len(masks) + 3),
        out_specs=VMEM,
        scratch_shapes=[
            pltpu.VMEM((3, count_slots, local_width), jnp.bfloat16),
            pltpu.VMEM((count_slots, LANES), jnp.bfloat16),
            pltpu.VMEM((local_width // LANES, 2 * pair_rows, LANES), jnp.float32),
            pltpu.VMEM((local_width // LANES, 2 * pair_rows, 2 * LANES), jnp.float32),
            pltpu.SMEM((2 * bags,), jnp.int32),
        ],
        compiler_params=limit(28),
        cost_estimate=pl.CostEstimate(flops=3000000000, bytes_accessed=5000000, transcendentals=1200000),
        name="bag",
    )(*pieces.values(), near_qkv, across_qkv, folded)
    received = lax.all_to_all(attended, ("head", "bag"), split_axis=0, concat_axis=0, tiled=True)
    return pl.pallas_call(
        functools.partial(collect_kernel, frames_dev, heads_dev),
        out_shape=jax.ShapeDtypeStruct((tok_dev, heads_dev * local_width), jnp.bfloat16),
        in_specs=[VMEM, VMEM, VMEM],
        out_specs=VMEM,
        compiler_params=limit(16),
        name="collect",
    )(count, onehot, received.reshape(count_slots, local_width))


def solution(mesh):
    placed = (
        P("bag", "head", None, None, None),
        P("bag"),
        P("bag", None),
        P("bag"),
        P(),
        P(),
        P(None, None, "head"),
    )
    return jax.shard_map(
        shards, mesh=mesh, in_specs=placed, out_specs=P(("bag", "head"), None), check_vma=False
    )
```

```python
import functools
import math
import jax
import jax.numpy as jnp
from jax import lax
from jax.experimental import pallas as pl
from jax.experimental.pallas import tpu as pltpu
from jax.sharding import PartitionSpec as P


HDIM = 64
TAPS = 3
SAMPLES = 4
LANES = 128

epsilon = 1e-06
far_below = -1e30

VMEM = pl.BlockSpec(memory_space=pltpu.VMEM)
ANY = pl.BlockSpec(memory_space=pl.ANY)
EDGE_LIMIT = 60


def limit(mib):
    return pltpu.CompilerParams(vmem_limit_bytes=mib << 20)


def slot_of(route_row, bags, stride):
    tokens = route_row.shape[1]
    bag_ids = lax.broadcasted_iota(jnp.int32, (bags, tokens), 0)
    onehot = (bag_ids == route_row).astype(jnp.float32)
    before = (
        lax.broadcasted_iota(jnp.int32, (tokens, tokens), 0)
        < lax.broadcasted_iota(jnp.int32, (tokens, tokens), 1)
    )
    earlier = jnp.dot(
        onehot.astype(jnp.bfloat16),
        before.astype(jnp.float32).astype(jnp.bfloat16),
        preferred_element_type=jnp.float32,
    )
    rank = jnp.sum(earlier * onehot, axis=0, keepdims=True).astype(jnp.int32)
    return route_row * stride + rank


def onehot_of(slot, slots):
    slot_ids = lax.broadcasted_iota(jnp.int32, (slots, slot.shape[1]), 0)
    return (slot_ids == slot).astype(jnp.float32).astype(jnp.bfloat16)


def combine(products, rows, cols):
    chans = products[0].shape[1]
    blank = jnp.zeros((cols, chans), jnp.float32)
    area = rows * cols
    column = lax.broadcasted_iota(jnp.int32, (area, chans), 0) % cols
    total = None
    for e in range(TAPS):
        up, mid, down = products[e], products[TAPS + e], products[2 * TAPS + e]
        merged = (
            mid
            + jnp.concatenate([blank, up[: area - cols]], axis=0)
            + jnp.concatenate([down[cols:], blank], axis=0)
        )
        if e == 0:
            merged = jnp.where(column == 0, 0.0, pltpu.roll(merged, 1, axis=0))
        elif e == 2:
            merged = jnp.where(column == cols - 1, 0.0, pltpu.roll(merged, area - 1, axis=0))
        total = merged if total is None else total + merged
    return total


def plane_products(pieces, w_ref):
    plane = TAPS * TAPS
    chans = w_ref.shape[2]
    stacked = pieces[0][1] if len(pieces) == 1 else jnp.concatenate([x for _, x in pieces], axis=1)
    products = []
    for p in range(0, plane, 2):
        pair = []
        for q in range(p, min(p + 2, plane)):
            taps = [w_ref[plane * t + q] for t, _ in pieces]
            pair.append(taps[0] if len(taps) == 1 else jnp.concatenate(taps, axis=0))
        weight = pair[0] if len(pair) == 1 else jnp.concatenate(pair, axis=1)
        value = jnp.dot(stacked, weight, preferred_element_type=jnp.float32)
        for q in range(len(pair)):
            products.append(value[:, q * chans : (q + 1) * chans])
    return products


def scalar_of(ref):
    return jnp.max(ref[...])


def edge_kernel(rows, cols, frames, x_hbm, w_hbm, near_ref, far_ref, x_ref, w_ref, sems):
    area = rows * cols
    plane = TAPS * TAPS
    jobs = ((frames - 1, 0), (0, 2))
    loads = []
    for i, (f, tap) in enumerate(jobs):
        group = [
            pltpu.make_async_copy(
                x_hbm.at[pl.ds(f * area, area)], x_ref.at[pl.ds(i * area, area)], sems.at[i, TAPS]
            )
        ]
        for row in range(TAPS):
            group.append(
                pltpu.make_async_copy(
                    w_hbm.at[pl.ds(tap * plane + row * TAPS, TAPS)],
                    w_ref.at[pl.ds(i * plane + row * TAPS, TAPS)],
                    sems.at[i, row],
                )
            )
        loads.append(group)
    for group in loads:
        for load in group:
            load.start()
    even = lax.axis_index("head") % 2 == 0
    sums = []
    for i in range(2):
        for load in loads[i]:
            load.wait()
        value = x_ref[i * area : (i + 1) * area, :]
        sums.append(combine(plane_products([(i, value)], w_ref), rows, cols))
    up, down = sums
    near_ref[...] = jnp.where(even, up, down)
    far_ref[...] = jnp.where(even, down, up)


def own_kernel(bags, cap, rows, cols, frames, count_ref, x_ref, w_ref, route_ref, acc_ref, onehot_ref):
    count = scalar_of(count_ref)
    place = lax.axis_index("head")
    area = rows * cols
    first = place * frames
    inputs = []
    for f in range(frames):
        value = x_ref[f * area : (f + 1) * area, :]
        inputs.append(jnp.where(first + f < count, value, jnp.zeros_like(value)))
    for f in range(frames):
        pieces = [(t, inputs[f + t - 1]) for t in range(TAPS) if 0 <= f + t - 1 < frames]
        acc_ref[f * area : (f + 1) * area, :] = combine(plane_products(pieces, w_ref), rows, cols)
    route_row = route_ref[pl.ds(place, 1), :]
    onehot_ref[...] = onehot_of(slot_of(route_row, bags, cap), bags * cap)


def join_kernel(
    rows, cols, frames, count_ref, sample_ref, acc_ref, near_ref, far_ref, onehot_ref, e_ref, out_ref, grid_ref
):
    count = scalar_of(count_ref)
    sample = scalar_of(sample_ref)
    area = rows * cols
    place = lax.axis_index("head")
    even = place % 2 == 0
    first = place * frames
    chans = acc_ref.shape[1]
    near, far = near_ref[...], far_ref[...]
    for f in range(frames):
        part = acc_ref[f * area : (f + 1) * area, :]
        if f == 0:
            before = jnp.logical_and(first > 0, first - 1 < count)
            part = part + jnp.where(before, jnp.where(even, far, near), 0.0)
        if f == frames - 1:
            part = part + jnp.where(first + frames < count, jnp.where(even, near, far), 0.0)
        grid_ref[f * area : (f + 1) * area, :] = jnp.where(first + f < count, part, 0.0)
    pieces = [[None] * 2 for _ in range(2)]
    for odd in range(2):
        half = grid_ref[pl.ds(odd, frames * area // 2, stride=2), :]
        half = half.reshape(frames * rows // 2, 2, cols // 2, chans)
        for i in range(2):
            pieces[i][odd] = half[:, i].reshape(frames * area // 4, chans)
    tokens = frames * area // 4
    patches = jnp.concatenate(
        [pieces[0][0], pieces[0][1], pieces[1][0], pieces[1][1]], axis=1
    ).astype(jnp.bfloat16)
    model = e_ref.shape[1]
    col_tile = 256
    total = None
    for n in range(0, model, col_tile):
        part = jnp.dot(patches, e_ref[:, n : n + col_tile], preferred_element_type=jnp.float32)
        squares = part * part
        both = squares[:, :LANES] + squares[:, LANES:]
        total = both if total is None else total + both
    scale = lax.rsqrt(jnp.sum(total, axis=-1, keepdims=True) * (1.0 / model) + epsilon)
    high = scale.astype(jnp.bfloat16).astype(jnp.float32)
    frame = first + lax.broadcasted_iota(jnp.int32, (tokens, LANES), 0) // (area // 4)
    lane = lax.broadcasted_iota(jnp.int32, (tokens, LANES), 1)
    label = jnp.where(frame < count, sample + 1, 0).astype(jnp.float32)
    notes = jnp.where(lane == 0, label, jnp.where(lane == 1, high, jnp.where(lane == 2, scale - high, 0.0)))
    patches = jnp.concatenate([patches, notes.astype(jnp.bfloat16)], axis=1)
    out_ref[...] = jnp.dot(onehot_ref[...], patches, preferred_element_type=jnp.float32).astype(
        jnp.bfloat16
    )


def fold_kernel(e_ref, w_ref, after_ref, fold_ref):
    feats = e_ref.shape[0]
    width = w_ref.shape[2]
    col_tile = 256
    for m in range(3):
        for n in range(0, width, col_tile):
            cols = slice(n, n + col_tile)
            product = jnp.dot(e_ref[...], w_ref[m, :, cols], preferred_element_type=jnp.float32)
            if m == 0:
                product = product * (HDIM ** (-0.5) * math.log2(math.e))
            high = product.astype(jnp.bfloat16)
            fold_ref[m, :feats, cols] = high
            fold_ref[m, feats:, cols] = (product - high.astype(jnp.float32)).astype(jnp.bfloat16)


def qkv_kernel(*refs):
    pieces, fold_ref, out_ref = refs[:-2], refs[-2], refs[-1]
    for m, at, part in qkv_parts(pieces, fold_ref):
        out_ref[m, :, at : at + part.shape[1]] = part


def qkv_parts(pieces, fold_ref):
    feats = pieces[0].shape[1] - LANES
    col_tile = 256
    patch = jnp.concatenate([ref[:, :feats] for ref in pieces], axis=0)
    notes = jnp.concatenate([ref[:, feats:].astype(jnp.float32) for ref in pieces], axis=0)
    scale = jnp.broadcast_to(notes[:, 1:2] + notes[:, 2:3], (notes.shape[0], col_tile))
    twice = jnp.concatenate([patch, patch], axis=1)
    for m in range(3):
        for n in range(0, fold_ref.shape[2], col_tile):
            part = jnp.dot(twice, fold_ref[m, :, n : n + col_tile], preferred_element_type=jnp.float32)
            yield m, n, part * scale


def bag_kernel(clips, cap, masks, groups, *refs):
    count = len(masks)
    pieces, rest = refs[:count], refs[count:]
    early, rest = rest[: len(groups)], rest[len(groups) :]
    fold_ref, out_ref, qkv_ref, note_ref, m_ref, r_ref, order_ref = rest
    place = lax.axis_index("head")
    slots = pieces[0].shape[0]
    feats = pieces[0].shape[1] - LANES
    width = fold_ref.shape[2]
    clip_rows = count * cap
    done = sum(groups)

    def by_clip(values, c):
        return jnp.concatenate(
            [
                value[j * slots + c * cap : j * slots + (c + 1) * cap]
                for value in values
                for j in range(value.shape[0] // slots)
            ],
            axis=0,
        )

    notes = [ref[:, feats:].astype(jnp.float32) for ref in pieces]
    for c in range(clips):
        note = by_clip(notes, c)
        note_ref[c * clip_rows : (c + 1) * clip_rows, :] = note.astype(jnp.bfloat16)
        order_ref[clips + c] = jnp.max(note[:, :1]).astype(jnp.int32)
    starts = [jnp.int32(0)]
    for s in range(SAMPLES):

        def keep_clip(c, at):
            hit = order_ref[clips + c] == s + 1

            @pl.when(hit)
            def _():
                order_ref[at] = c

            return at + hit.astype(jnp.int32)

        starts.append(lax.fori_loop(0, clips, keep_clip, starts[-1]))

    for m, at, part in qkv_parts(pieces[done:], fold_ref):
        cols = slice(at, at + part.shape[1])
        parts = [ref[m, :, cols] for ref in early] + [part]
        for c in range(clips):
            qkv_ref[m, c * clip_rows : (c + 1) * clip_rows, cols] = by_clip(parts, c).astype(jnp.bfloat16)

    out_ref[...] = jnp.zeros_like(out_ref)
    tile = 2 * clip_rows
    lane = lax.broadcasted_iota(jnp.int32, (tile, LANES), 1)
    low = lane < HDIM
    pairs = width // LANES
    ones = jnp.ones((tile, LANES), jnp.bfloat16)
    pick = (lax.broadcasted_iota(jnp.int32, (8, LANES), 1) == 0).astype(jnp.float32).astype(jnp.bfloat16)
    key_at = lax.broadcasted_iota(jnp.int32, (1, tile), 1)

    def two(ref, a, b, *at):
        return jnp.concatenate(
            [
                ref[(*at[:-1], pl.ds(pl.multiple_of(a * clip_rows, 16), clip_rows), at[-1])],
                ref[(*at[:-1], pl.ds(pl.multiple_of(b * clip_rows, 16), clip_rows), at[-1])],
            ],
            axis=0,
        )

    for s in range(SAMPLES):
        begin, size = starts[s], starts[s + 1] - starts[s]
        tiles = (size + 1) // 2

        def members(i):
            second = 2 * i + 1 < size
            return (
                order_ref[begin + 2 * i],
                order_ref[begin + 2 * i + second.astype(jnp.int32)],
                second,
            )

        def bias_of(a, b, second):
            label = lax.dot_general(
                pick,
                two(note_ref, a, b, slice(0, LANES)),
                (((1,), (1,)), ((), ())),
                preferred_element_type=jnp.float32,
            )[:1]
            limit = jnp.where(second, tile, clip_rows)
            good = jnp.logical_and(label == s + 1.0, key_at < limit)
            return jnp.where(good, 0.0, far_below)

        def stacked(pair, a, b):
            query = two(qkv_ref, a, b, 0, slice(pair * LANES, (pair + 1) * LANES))
            blank = jnp.zeros_like(query)
            return jnp.concatenate([jnp.where(low, query, blank), jnp.where(low, blank, query)], axis=0)

        def scores_of(pair, query, a, b, bias):
            keys = two(qkv_ref, a, b, 1, slice(pair * LANES, (pair + 1) * LANES))
            return (
                lax.dot_general(query, keys, (((1,), (1,)), ((), ())), preferred_element_type=jnp.float32)
                + bias
            )

        def mix(pair, shifted, a, b):
            cols = slice(pair * LANES, (pair + 1) * LANES)
            values = jnp.concatenate([two(qkv_ref, a, b, 2, cols), ones], axis=1)
            return jnp.dot(shifted.astype(jnp.bfloat16), values, preferred_element_type=jnp.float32)

        def store(pair, a, b, result):
            cols = slice(pair * LANES, (pair + 1) * LANES)
            shares = result[:, :LANES] / result[:, LANES:]
            mixed = jnp.where(low, shares[:tile], shares[tile:])
            for at, clip in ((clip_rows, b), (0, a)):
                for j, mask in enumerate(masks):
                    piece = mixed[at + j * cap : at + (j + 1) * cap]
                    out_ref[jnp.bitwise_xor(place, mask) * clips + clip, :, cols] = piece.astype(jnp.bfloat16)

        def query_tile(i, carry):
            qa, qb, _ = members(i)

            @pl.when(tiles == 1)
            def _():
                ka, kb, second = members(0)
                bias = bias_of(ka, kb, second)
                for pair in range(pairs):
                    scores = scores_of(pair, stacked(pair, qa, qb), ka, kb, bias)
                    top = jnp.max(scores, axis=-1, keepdims=True)
                    store(pair, qa, qb, mix(pair, jnp.exp2(scores - top), ka, kb))

            @pl.when(tiles > 1)
            def _():
                for pair in range(pairs):
                    m_ref[pair] = jnp.full((2 * tile, LANES), far_below, jnp.float32)
                    r_ref[pair] = jnp.zeros((2 * tile, 2 * LANES), jnp.float32)

                def key_tile(j, inner):
                    ka, kb, second = members(j)
                    bias = bias_of(ka, kb, second)
                    for pair in range(pairs):
                        scores = scores_of(pair, stacked(pair, qa, qb), ka, kb, bias)
                        old = m_ref[pair][:, :1]
                        top = jnp.maximum(old, jnp.max(scores, axis=-1, keepdims=True))
                        r_ref[pair] = r_ref[pair] * jnp.exp2(old - top) + mix(
                            pair, jnp.exp2(scores - top), ka, kb
                        )
                        m_ref[pair] = jnp.broadcast_to(top, (2 * tile, LANES))
                    return inner

                lax.fori_loop(0, tiles, key_tile, 0)
                for pair in range(pairs):
                    store(pair, qa, qb, r_ref[pair])

            return carry

        lax.fori_loop(0, tiles, query_tile, 0)


def collect_kernel(frames, heads, count_ref, onehot_ref, recv_ref, out_ref):
    count = scalar_of(count_ref)
    place = lax.axis_index("head")
    slots, tokens = onehot_ref.shape
    frame = place * frames + lax.broadcasted_iota(jnp.int32, (slots, tokens), 1) // (tokens // frames)
    onehot = jnp.where(frame < count, onehot_ref[...], jnp.zeros((), jnp.bfloat16))
    width = recv_ref.shape[1]
    for h in range(heads):
        picked = lax.dot_general(
            onehot,
            recv_ref[h * slots : (h + 1) * slots, :],
            (((0,), (0,)), ((), ())),
            preferred_element_type=jnp.float32,
        )
        out_ref[:, h * width : (h + 1) * width] = picked.astype(jnp.bfloat16)


def shards(latents, frame_counts, routes, samples, conv_weight, embed_weight, qkv_weight):
    frames_dev, rows, cols, depth = latents.shape[1:]
    heads_dev = lax.axis_size("head")
    bags = lax.axis_size("bag")
    area = rows * cols
    tok_dev = frames_dev * area // 4
    cap = 3 * tok_dev // (2 * bags)
    slots = bags * cap
    local_width = qkv_weight.shape[2]
    chans = conv_weight.shape[2]

    tile = latents.reshape(frames_dev * area, depth)
    count = frame_counts
    edge = jax.ShapeDtypeStruct((area, chans), jnp.float32)
    near, far = pl.pallas_call(
        functools.partial(edge_kernel, rows, cols, frames_dev),
        out_shape=(edge, edge),
        in_specs=[ANY, ANY],
        out_specs=(VMEM, VMEM),
        scratch_shapes=[
            pltpu.VMEM((2 * area, depth), jnp.bfloat16),
            pltpu.VMEM((2 * TAPS * TAPS, depth, chans), jnp.bfloat16),
            pltpu.SemaphoreType.DMA((2, TAPS + 1)),
        ],
        compiler_params=limit(EDGE_LIMIT),
        cost_estimate=pl.CostEstimate(flops=600000000, bytes_accessed=4500000, transcendentals=0),
        name="edge",
    )(tile, conv_weight)
    across = [(i, i + 1) for i in range(1, heads_dev - 1, 2)]
    far = lax.ppermute(far, "head", across + [(j, i) for i, j in across])
    near = lax.ppermute(near, "head", [(i, i ^ 1) for i in range(heads_dev)])

    route_rows = routes[:, 0].reshape(heads_dev, tok_dev)
    row_width = 4 * chans + LANES
    acc, onehot = pl.pallas_call(
        functools.partial(own_kernel, bags, cap, rows, cols, frames_dev),
        out_shape=(
            jax.ShapeDtypeStruct((frames_dev * area, chans), jnp.float32),
            jax.ShapeDtypeStruct((slots, tok_dev), jnp.bfloat16),
        ),
        in_specs=[VMEM, VMEM, VMEM, VMEM],
        out_specs=(VMEM, VMEM),
        compiler_params=limit(16),
        cost_estimate=pl.CostEstimate(flops=4000000000, bytes_accessed=4500000, transcendentals=0),
        name="own",
    )(count, tile, conv_weight, route_rows)
    outgoing = pl.pallas_call(
        functools.partial(join_kernel, rows, cols, frames_dev),
        out_shape=jax.ShapeDtypeStruct((slots, row_width), jnp.bfloat16),
        in_specs=[VMEM] * 7,
        out_specs=VMEM,
        scratch_shapes=[pltpu.VMEM((frames_dev * area, chans), jnp.float32)],
        compiler_params=limit(16),
        cost_estimate=pl.CostEstimate(flops=300000000, bytes_accessed=3000000, transcendentals=0),
        name="join",
    )(count, samples.reshape(heads_dev, tok_dev), acc, near, far, onehot, embed_weight)

    arrived = lax.all_to_all(
        outgoing.reshape(bags, cap, row_width), "bag", split_axis=0, concat_axis=0, tiled=True
    )
    arrived = arrived.reshape(slots, row_width)
    pieces = {0: arrived}
    bit = heads_dev // 2
    swap = [(i, i ^ bit) for i in range(heads_dev)]
    across = lax.ppermute(arrived, "head", swap)
    folded = pl.pallas_call(
        fold_kernel,
        out_shape=jax.ShapeDtypeStruct((3, 2 * embed_weight.shape[0], local_width), jnp.bfloat16),
        in_specs=[VMEM, VMEM, ANY],
        out_specs=VMEM,
        compiler_params=limit(16),
        cost_estimate=pl.CostEstimate(flops=3300000000, bytes_accessed=14000000, transcendentals=0),
        name="fold",
    )(embed_weight, qkv_weight, arrived)

    def spread(start, bits):
        found = dict(start)
        for lower in bits:
            pairs = [(i, i ^ lower) for i in range(heads_dev)]
            found.update({mask | lower: lax.ppermute(piece, "head", pairs) for mask, piece in found.items()})
        return found

    lower_bits = [1 << i for i in reversed(range(bit.bit_length() - 1))]
    close = spread({0: arrived}, lower_bits)

    def project(group):
        return pl.pallas_call(
            qkv_kernel,
            out_shape=jax.ShapeDtypeStruct((3, len(group) * slots, local_width), jnp.float32),
            in_specs=[VMEM] * (len(group) + 1),
            out_specs=VMEM,
            compiler_params=limit(16),
            cost_estimate=pl.CostEstimate(
                flops=600000000 * len(group), bytes_accessed=3000000 * len(group), transcendentals=0
            ),
        )(*group, folded)

    near_qkv = project(list(close.values()))
    across, near_qkv = lax.optimization_barrier((across, near_qkv))
    pieces = dict(close)
    pieces.update(spread({bit: across}, lower_bits))
    across_qkv = project([across])
    groups = (len(close), 1)
    count_slots = heads_dev * slots
    masks = tuple(pieces)

    pair_rows = 2 * heads_dev * cap
    attended = pl.pallas_call(
        functools.partial(bag_kernel, bags, cap, masks, groups),
        out_shape=jax.ShapeDtypeStruct((heads_dev * bags, cap, local_width), jnp.bfloat16),
        in_specs=[VMEM] * (len(masks) + 3),
        out_specs=VMEM,
        scratch_shapes=[
            pltpu.VMEM((3, count_slots, local_width), jnp.bfloat16),
            pltpu.VMEM((count_slots, LANES), jnp.bfloat16),
            pltpu.VMEM((local_width // LANES, 2 * pair_rows, LANES), jnp.float32),
            pltpu.VMEM((local_width // LANES, 2 * pair_rows, 2 * LANES), jnp.float32),
            pltpu.SMEM((2 * bags,), jnp.int32),
        ],
        compiler_params=limit(28),
        cost_estimate=pl.CostEstimate(flops=3000000000, bytes_accessed=5000000, transcendentals=1200000),
        name="bag",
    )(*pieces.values(), near_qkv, across_qkv, folded)
    received = lax.all_to_all(attended, ("head", "bag"), split_axis=0, concat_axis=0, tiled=True)
    return pl.pallas_call(
        functools.partial(collect_kernel, frames_dev, heads_dev),
        out_shape=jax.ShapeDtypeStruct((tok_dev, heads_dev * local_width), jnp.bfloat16),
        in_specs=[VMEM, VMEM, VMEM],
        out_specs=VMEM,
        compiler_params=limit(16),
        name="collect",
    )(count, onehot, received.reshape(count_slots, local_width))


def solution(mesh):
    placed = (
        P("bag", "head", None, None, None),
        P("bag"),
        P("bag", None),
        P("bag"),
        P(),
        P(),
        P(None, None, "head"),
    )

    return jax.shard_map(shards, mesh=mesh, in_specs=placed, out_specs=P(("bag", "head"), None), check_vma=False)
```

```python
import functools
import math
import jax
import jax.numpy as jnp
from jax import lax
from jax.experimental import pallas as pl
from jax.experimental.pallas import tpu as pltpu
from jax.sharding import PartitionSpec as P

HDIM = 64
TAPS = 3
SAMPLES = 4
LANES = 128

epsilon = 1e-06
far_below = -1e30

VMEM = pl.BlockSpec(memory_space=pltpu.VMEM)
ANY = pl.BlockSpec(memory_space=pl.ANY)
EDGE_LIMIT = 60


def limit(mib):
    return pltpu.CompilerParams(vmem_limit_bytes=mib << 20)


def slot_of(route_row, bags, cap, stride):
    tokens = route_row.shape[1]
    bag_ids = lax.broadcasted_iota(jnp.int32, (bags, tokens), 0)
    onehot = (bag_ids == route_row).astype(jnp.float32)
    before = (
        lax.broadcasted_iota(jnp.int32, (tokens, tokens), 0)
        < lax.broadcasted_iota(jnp.int32, (tokens, tokens), 1)
    )
    earlier = jnp.dot(
        onehot.astype(jnp.bfloat16),
        before.astype(jnp.float32).astype(jnp.bfloat16),
        preferred_element_type=jnp.float32,
    )
    rank = jnp.sum(earlier * onehot, axis=0, keepdims=True).astype(jnp.int32)
    return route_row * stride + rank


def onehot_of(slot, slots):
    slot_ids = lax.broadcasted_iota(jnp.int32, (slots, slot.shape[1]), 0)
    return (slot_ids == slot).astype(jnp.float32).astype(jnp.bfloat16)


def combine(products, rows, cols):
    chans = products[0].shape[1]
    blank = jnp.zeros((cols, chans), jnp.float32)
    area = rows * cols
    column = lax.broadcasted_iota(jnp.int32, (area, chans), 0) % cols
    total = None
    for e in range(TAPS):
        up, mid, down = products[e], products[TAPS + e], products[2 * TAPS + e]
        merged = (
            mid
            + jnp.concatenate([blank, up[: area - cols]], axis=0)
            + jnp.concatenate([down[cols:], blank], axis=0)
        )
        if e == 0:
            merged = jnp.where(column == 0, 0.0, pltpu.roll(merged, 1, axis=0))
        elif e == 2:
            merged = jnp.where(column == cols - 1, 0.0, pltpu.roll(merged, area - 1, axis=0))
        total = merged if total is None else total + merged
    return total


def plane_products(pieces, w_ref):
    plane = TAPS * TAPS
    chans = w_ref.shape[2]
    stacked = pieces[0][1] if len(pieces) == 1 else jnp.concatenate([x for _, x in pieces], axis=1)
    products = []
    for p in range(0, plane, 2):
        pair = []
        for q in range(p, min(p + 2, plane)):
            taps = [w_ref[plane * t + q] for t, _ in pieces]
            pair.append(taps[0] if len(taps) == 1 else jnp.concatenate(taps, axis=0))
        weight = pair[0] if len(pair) == 1 else jnp.concatenate(pair, axis=1)
        value = jnp.dot(stacked, weight, preferred_element_type=jnp.float32)
        for q in range(len(pair)):
            products.append(value[:, q * chans : (q + 1) * chans])
    return products


def scalar_of(ref):
    return jnp.max(ref[...])


def edge_kernel(rows, cols, frames, x_hbm, w_hbm, near_ref, far_ref, x_ref, w_ref, sems):
    area = rows * cols
    plane = TAPS * TAPS
    jobs = ((frames - 1, 0), (0, 2))
    loads = []
    for i, (f, tap) in enumerate(jobs):
        group = [
            pltpu.make_async_copy(
                x_hbm.at[pl.ds(f * area, area)], x_ref.at[pl.ds(i * area, area)], sems.at[i, TAPS]
            )
        ]
        for row in range(TAPS):
            group.append(
                pltpu.make_async_copy(
                    w_hbm.at[pl.ds(tap * plane + row * TAPS, TAPS)],
                    w_ref.at[pl.ds(i * plane + row * TAPS, TAPS)],
                    sems.at[i, row],
                )
            )
        loads.append(group)
    for group in loads:
        for load in group:
            load.start()
    even = lax.axis_index("head") % 2 == 0
    sums = []
    for i in range(2):
        for load in loads[i]:
            load.wait()
        value = x_ref[i * area : (i + 1) * area, :]
        sums.append(combine(plane_products([(i, value)], w_ref), rows, cols))
    up, down = sums
    near_ref[...] = jnp.where(even, up, down)
    far_ref[...] = jnp.where(even, down, up)


def own_kernel(bags, cap, rows, cols, frames, count_ref, x_ref, w_ref, route_ref, acc_ref, onehot_ref):
    count = scalar_of(count_ref)
    place = lax.axis_index("head")
    area = rows * cols
    first = place * frames
    inputs = []
    for f in range(frames):
        value = x_ref[f * area : (f + 1) * area, :]
        inputs.append(jnp.where(first + f < count, value, jnp.zeros_like(value)))
    for f in range(frames):
        pieces = [(t, inputs[f + t - 1]) for t in range(TAPS) if 0 <= f + t - 1 < frames]
        acc_ref[f * area : (f + 1) * area, :] = combine(plane_products(pieces, w_ref), rows, cols)
    route_row = route_ref[pl.ds(place, 1), :]
    onehot_ref[...] = onehot_of(slot_of(route_row, bags, cap, cap), bags * cap)


def join_kernel(
    rows, cols, frames, count_ref, sample_ref, acc_ref, near_ref, far_ref, onehot_ref, e_ref, out_ref, grid_ref
):
    count = scalar_of(count_ref)
    sample = scalar_of(sample_ref)
    area = rows * cols
    place = lax.axis_index("head")
    even = place % 2 == 0
    first = place * frames
    chans = acc_ref.shape[1]
    near, far = near_ref[...], far_ref[...]
    for f in range(frames):
        part = acc_ref[f * area : (f + 1) * area, :]
        if f == 0:
            before = jnp.logical_and(first > 0, first - 1 < count)
            part = part + jnp.where(before, jnp.where(even, far, near), 0.0)
        if f == frames - 1:
            part = part + jnp.where(first + frames < count, jnp.where(even, near, far), 0.0)
        grid_ref[f * area : (f + 1) * area, :] = jnp.where(first + f < count, part, 0.0)
    pieces = [[None] * 2 for _ in range(2)]
    for odd in range(2):
        half = grid_ref[pl.ds(odd, frames * area // 2, stride=2), :]
        half = half.reshape(frames * rows // 2, 2, cols // 2, chans)
        for i in range(2):
            pieces[i][odd] = half[:, i].reshape(frames * area // 4, chans)
    tokens = frames * area // 4
    patches = jnp.concatenate(
        [pieces[0][0], pieces[0][1], pieces[1][0], pieces[1][1]], axis=1
    ).astype(jnp.bfloat16)
    model = e_ref.shape[1]
    col_tile = 256
    total = None
    for n in range(0, model, col_tile):
        part = jnp.dot(patches, e_ref[:, n : n + col_tile], preferred_element_type=jnp.float32)
        squares = part * part
        both = squares[:, :LANES] + squares[:, LANES:]
        total = both if total is None else total + both
    scale = lax.rsqrt(jnp.sum(total, axis=-1, keepdims=True) * (1.0 / model) + epsilon)
    high = scale.astype(jnp.bfloat16).astype(jnp.float32)
    frame = first + lax.broadcasted_iota(jnp.int32, (tokens, LANES), 0) // (area // 4)
    lane = lax.broadcasted_iota(jnp.int32, (tokens, LANES), 1)
    label = jnp.where(frame < count, sample + 1, 0).astype(jnp.float32)
    notes = jnp.where(lane == 0, label, jnp.where(lane == 1, high, jnp.where(lane == 2, scale - high, 0.0)))
    patches = jnp.concatenate([patches, notes.astype(jnp.bfloat16)], axis=1)
    out_ref[...] = jnp.dot(onehot_ref[...], patches, preferred_element_type=jnp.float32).astype(
        jnp.bfloat16
    )


def fold_kernel(e_ref, w_ref, after_ref, fold_ref):
    feats = e_ref.shape[0]
    width = w_ref.shape[2]
    col_tile = 256
    for m in range(3):
        for n in range(0, width, col_tile):
            cols = slice(n, n + col_tile)
            product = jnp.dot(e_ref[...], w_ref[m, :, cols], preferred_element_type=jnp.float32)
            if m == 0:
                product = product * (HDIM ** (-0.5) * math.log2(math.e))
            high = product.astype(jnp.bfloat16)
            fold_ref[m, :feats, cols] = high
            fold_ref[m, feats:, cols] = (product - high.astype(jnp.float32)).astype(jnp.bfloat16)


def qkv_kernel(*refs):
    pieces, fold_ref, out_ref = refs[:-2], refs[-2], refs[-1]
    for m, at, part in qkv_parts(pieces, fold_ref):
        out_ref[m, :, at : at + part.shape[1]] = part


def qkv_parts(pieces, fold_ref):
    feats = pieces[0].shape[1] - LANES
    col_tile = 256
    patch = jnp.concatenate([ref[:, :feats] for ref in pieces], axis=0)
    notes = jnp.concatenate([ref[:, feats:].astype(jnp.float32) for ref in pieces], axis=0)
    scale = jnp.broadcast_to(notes[:, 1:2] + notes[:, 2:3], (notes.shape[0], col_tile))
    twice = jnp.concatenate([patch, patch], axis=1)
    for m in range(3):
        for n in range(0, fold_ref.shape[2], col_tile):
            part = jnp.dot(twice, fold_ref[m, :, n : n + col_tile], preferred_element_type=jnp.float32)
            yield m, n, part * scale


def bag_kernel(clips, cap, masks, groups, *refs):
    count = len(masks)
    pieces, rest = refs[:count], refs[count:]
    early, rest = rest[: len(groups)], rest[len(groups) :]
    fold_ref, out_ref, qkv_ref, note_ref, m_ref, r_ref, order_ref = rest
    place = lax.axis_index("head")
    slots = pieces[0].shape[0]
    feats = pieces[0].shape[1] - LANES
    width = fold_ref.shape[2]
    clip_rows = count * cap
    done = sum(groups)

    def by_clip(values, c):
        return jnp.concatenate(
            [
                value[j * slots + c * cap : j * slots + (c + 1) * cap]
                for value in values
                for j in range(value.shape[0] // slots)
            ],
            axis=0,
        )

    notes = [ref[:, feats:].astype(jnp.float32) for ref in pieces]
    for c in range(clips):
        note = by_clip(notes, c)
        note_ref[c * clip_rows : (c + 1) * clip_rows, :] = note.astype(jnp.bfloat16)
        order_ref[clips + c] = jnp.max(note[:, :1]).astype(jnp.int32)
    starts = [jnp.int32(0)]
    for s in range(SAMPLES):

        def keep_clip(c, at):
            hit = order_ref[clips + c] == s + 1

            @pl.when(hit)
            def _():
                order_ref[at] = c

            return at + hit.astype(jnp.int32)

        starts.append(lax.fori_loop(0, clips, keep_clip, starts[-1]))

    for m, at, part in qkv_parts(pieces[done:], fold_ref):
        cols = slice(at, at + part.shape[1])
        parts = [ref[m, :, cols] for ref in early] + [part]
        for c in range(clips):
            qkv_ref[m, c * clip_rows : (c + 1) * clip_rows, cols] = by_clip(parts, c).astype(jnp.bfloat16)

    out_ref[...] = jnp.zeros_like(out_ref)
    tile = 2 * clip_rows
    lane = lax.broadcasted_iota(jnp.int32, (tile, LANES), 1)
    low = lane < HDIM
    pairs = width // LANES
    ones = jnp.ones((tile, LANES), jnp.bfloat16)
    pick = (lax.broadcasted_iota(jnp.int32, (8, LANES), 1) == 0).astype(jnp.float32).astype(jnp.bfloat16)
    key_at = lax.broadcasted_iota(jnp.int32, (1, tile), 1)

    def two(ref, a, b, *at):
        return jnp.concatenate(
            [
                ref[(*at[:-1], pl.ds(pl.multiple_of(a * clip_rows, 16), clip_rows), at[-1])],
                ref[(*at[:-1], pl.ds(pl.multiple_of(b * clip_rows, 16), clip_rows), at[-1])],
            ],
            axis=0,
        )

    for s in range(SAMPLES):
        begin, size = starts[s], starts[s + 1] - starts[s]
        tiles = (size + 1) // 2

        def members(i):
            second = 2 * i + 1 < size
            return (
                order_ref[begin + 2 * i],
                order_ref[begin + 2 * i + second.astype(jnp.int32)],
                second,
            )

        def bias_of(a, b, second):
            label = lax.dot_general(
                pick,
                two(note_ref, a, b, slice(0, LANES)),
                (((1,), (1,)), ((), ())),
                preferred_element_type=jnp.float32,
            )[:1]
            limit = jnp.where(second, tile, clip_rows)
            good = jnp.logical_and(label == s + 1.0, key_at < limit)
            return jnp.where(good, 0.0, far_below)

        def stacked(pair, a, b):
            query = two(qkv_ref, a, b, 0, slice(pair * LANES, (pair + 1) * LANES))
            blank = jnp.zeros_like(query)
            return jnp.concatenate([jnp.where(low, query, blank), jnp.where(low, blank, query)], axis=0)

        def scores_of(pair, query, a, b, bias):
            keys = two(qkv_ref, a, b, 1, slice(pair * LANES, (pair + 1) * LANES))
            return (
                lax.dot_general(query, keys, (((1,), (1,)), ((), ())), preferred_element_type=jnp.float32)
                + bias
            )

        def mix(pair, shifted, a, b):
            cols = slice(pair * LANES, (pair + 1) * LANES)
            values = jnp.concatenate([two(qkv_ref, a, b, 2, cols), ones], axis=1)
            return jnp.dot(shifted.astype(jnp.bfloat16), values, preferred_element_type=jnp.float32)

        def store(pair, a, b, result):
            cols = slice(pair * LANES, (pair + 1) * LANES)
            shares = result[:, :LANES] / result[:, LANES:]
            mixed = jnp.where(low, shares[:tile], shares[tile:])
            for at, clip in ((clip_rows, b), (0, a)):
                for j, mask in enumerate(masks):
                    piece = mixed[at + j * cap : at + (j + 1) * cap]
                    out_ref[jnp.bitwise_xor(place, mask) * clips + clip, :, cols] = piece.astype(jnp.bfloat16)

        def query_tile(i, carry):
            qa, qb, _ = members(i)

            @pl.when(tiles == 1)
            def _():
                ka, kb, second = members(0)
                bias = bias_of(ka, kb, second)
                for pair in range(pairs):
                    scores = scores_of(pair, stacked(pair, qa, qb), ka, kb, bias)
                    top = jnp.max(scores, axis=-1, keepdims=True)
                    store(pair, qa, qb, mix(pair, jnp.exp2(scores - top), ka, kb))

            @pl.when(tiles > 1)
            def _():
                for pair in range(pairs):
                    m_ref[pair] = jnp.full((2 * tile, LANES), far_below, jnp.float32)
                    r_ref[pair] = jnp.zeros((2 * tile, 2 * LANES), jnp.float32)

                def key_tile(j, inner):
                    ka, kb, second = members(j)
                    bias = bias_of(ka, kb, second)
                    for pair in range(pairs):
                        scores = scores_of(pair, stacked(pair, qa, qb), ka, kb, bias)
                        old = m_ref[pair][:, :1]
                        top = jnp.maximum(old, jnp.max(scores, axis=-1, keepdims=True))
                        r_ref[pair] = r_ref[pair] * jnp.exp2(old - top) + mix(
                            pair, jnp.exp2(scores - top), ka, kb
                        )
                        m_ref[pair] = jnp.broadcast_to(top, (2 * tile, LANES))
                    return inner

                lax.fori_loop(0, tiles, key_tile, 0)
                for pair in range(pairs):
                    store(pair, qa, qb, r_ref[pair])

            return carry

        lax.fori_loop(0, tiles, query_tile, 0)


def collect_kernel(frames, heads, count_ref, onehot_ref, recv_ref, out_ref):
    count = scalar_of(count_ref)
    place = lax.axis_index("head")
    slots, tokens = onehot_ref.shape
    frame = place * frames + lax.broadcasted_iota(jnp.int32, (slots, tokens), 1) // (tokens // frames)
    onehot = jnp.where(frame < count, onehot_ref[...].astype(jnp.float32), 0.0).T.astype(jnp.bfloat16)
    width = recv_ref.shape[1]
    for h in range(heads):
        picked = jnp.dot(
            onehot, recv_ref[h * slots : (h + 1) * slots, :], preferred_element_type=jnp.float32
        )
        out_ref[:, h * width : (h + 1) * width] = picked.astype(jnp.bfloat16)


def shards(latents, frame_counts, routes, samples, conv_weight, embed_weight, qkv_weight):
    frames_dev, rows, cols, depth = latents.shape[1:]
    heads_dev = lax.axis_size("head")
    bags = lax.axis_size("bag")
    area = rows * cols
    tok_dev = frames_dev * area // 4
    cap = 3 * tok_dev // (2 * bags)
    slots = bags * cap
    local_width = qkv_weight.shape[2]
    chans = conv_weight.shape[2]

    tile = latents.reshape(frames_dev * area, depth)
    count = frame_counts
    edge = jax.ShapeDtypeStruct((area, chans), jnp.float32)
    near, far = pl.pallas_call(
        functools.partial(edge_kernel, rows, cols, frames_dev),
        out_shape=(edge, edge),
        in_specs=[ANY, ANY],
        out_specs=(VMEM, VMEM),
        scratch_shapes=[
            pltpu.VMEM((2 * area, depth), jnp.bfloat16),
            pltpu.VMEM((2 * TAPS * TAPS, depth, chans), jnp.bfloat16),
            pltpu.SemaphoreType.DMA((2, TAPS + 1)),
        ],
        compiler_params=limit(EDGE_LIMIT),
        cost_estimate=pl.CostEstimate(flops=600000000, bytes_accessed=4500000, transcendentals=0),
        name="edge",
    )(tile, conv_weight)
    across = [(i, i + 1) for i in range(1, heads_dev - 1, 2)]
    far = lax.ppermute(far, "head", across + [(j, i) for i, j in across])
    near = lax.ppermute(near, "head", [(i, i ^ 1) for i in range(heads_dev)])

    route_rows = routes[:, 0].reshape(heads_dev, tok_dev)
    row_width = 4 * chans + LANES
    acc, onehot = pl.pallas_call(
        functools.partial(own_kernel, bags, cap, rows, cols, frames_dev),
        out_shape=(
            jax.ShapeDtypeStruct((frames_dev * area, chans), jnp.float32),
            jax.ShapeDtypeStruct((slots, tok_dev), jnp.bfloat16),
        ),
        in_specs=[VMEM, VMEM, VMEM, VMEM],
        out_specs=(VMEM, VMEM),
        compiler_params=limit(16),
        cost_estimate=pl.CostEstimate(flops=4000000000, bytes_accessed=4500000, transcendentals=0),
        name="own",
    )(count, tile, conv_weight, route_rows)
    outgoing = pl.pallas_call(
        functools.partial(join_kernel, rows, cols, frames_dev),
        out_shape=jax.ShapeDtypeStruct((slots, row_width), jnp.bfloat16),
        in_specs=[VMEM] * 7,
        out_specs=VMEM,
        scratch_shapes=[pltpu.VMEM((frames_dev * area, chans), jnp.float32)],
        compiler_params=limit(16),
        cost_estimate=pl.CostEstimate(flops=300000000, bytes_accessed=3000000, transcendentals=0),
        name="join",
    )(count, samples.reshape(heads_dev, tok_dev), acc, near, far, onehot, embed_weight)

    arrived = lax.all_to_all(
        outgoing.reshape(bags, cap, row_width), "bag", split_axis=0, concat_axis=0, tiled=True
    )
    arrived = arrived.reshape(slots, row_width)
    pieces = {0: arrived}
    bit = heads_dev // 2
    swap = [(i, i ^ bit) for i in range(heads_dev)]
    across = lax.ppermute(arrived, "head", swap)
    folded = pl.pallas_call(
        fold_kernel,
        out_shape=jax.ShapeDtypeStruct((3, 2 * embed_weight.shape[0], local_width), jnp.bfloat16),
        in_specs=[VMEM, VMEM, ANY],
        out_specs=VMEM,
        compiler_params=limit(16),
        cost_estimate=pl.CostEstimate(flops=3300000000, bytes_accessed=14000000, transcendentals=0),
        name="fold",
    )(embed_weight, qkv_weight, arrived)
    def spread(start, bits):
        found = dict(start)
        for lower in bits:
            pairs = [(i, i ^ lower) for i in range(heads_dev)]
            found.update({mask | lower: lax.ppermute(piece, "head", pairs) for mask, piece in found.items()})
        return found

    lower_bits = [1 << i for i in reversed(range(bit.bit_length() - 1))]
    close = spread({0: arrived}, lower_bits)

    def project(group, name):
        return pl.pallas_call(
            qkv_kernel,
            out_shape=jax.ShapeDtypeStruct((3, len(group) * slots, local_width), jnp.float32),
            in_specs=[VMEM] * (len(group) + 1),
            out_specs=VMEM,
            compiler_params=limit(16),
            cost_estimate=pl.CostEstimate(
                flops=600000000 * len(group), bytes_accessed=3000000 * len(group), transcendentals=0
            ),
            name=name,
        )(*group, folded)

    near_qkv = project(list(close.values()), "near_qkv")
    across, near_qkv = lax.optimization_barrier((across, near_qkv))
    pieces = dict(close)
    pieces.update(spread({bit: across}, lower_bits))
    across_qkv = project([across], "across_qkv")
    groups = (len(close), 1)
    count_slots = heads_dev * slots
    masks = tuple(pieces)

    pair_rows = 2 * heads_dev * cap
    attended = pl.pallas_call(
        functools.partial(bag_kernel, bags, cap, masks, groups),
        out_shape=jax.ShapeDtypeStruct((heads_dev * bags, cap, local_width), jnp.bfloat16),
        in_specs=[VMEM] * (len(masks) + 3),
        out_specs=VMEM,
        scratch_shapes=[
            pltpu.VMEM((3, count_slots, local_width), jnp.bfloat16),
            pltpu.VMEM((count_slots, LANES), jnp.bfloat16),
            pltpu.VMEM((local_width // LANES, 2 * pair_rows, LANES), jnp.float32),
            pltpu.VMEM((local_width // LANES, 2 * pair_rows, 2 * LANES), jnp.float32),
            pltpu.SMEM((2 * bags,), jnp.int32),
        ],
        compiler_params=limit(28),
        cost_estimate=pl.CostEstimate(flops=3000000000, bytes_accessed=5000000, transcendentals=1200000),
        name="bag",
    )(*pieces.values(), near_qkv, across_qkv, folded)
    received = lax.all_to_all(attended, ("head", "bag"), split_axis=0, concat_axis=0, tiled=True)
    return pl.pallas_call(
        functools.partial(collect_kernel, frames_dev, heads_dev),
        out_shape=jax.ShapeDtypeStruct((tok_dev, heads_dev * local_width), jnp.bfloat16),
        in_specs=[VMEM, VMEM, VMEM],
        out_specs=VMEM,
        compiler_params=limit(16),
        name="collect",
    )(count, onehot, received.reshape(count_slots, local_width))


def solution(mesh):
    placed = (
        P("bag", "head", None, None, None),
        P("bag"),
        P("bag", None),
        P("bag"),
        P(),
        P(),
        P(None, None, "head"),
    )
    return jax.shard_map(
        shards, mesh=mesh, in_specs=placed, out_specs=P(("bag", "head"), None), check_vma=False
    )
```

```python
import functools
import math
import jax
import jax.numpy as jnp
from jax import lax
from jax.experimental import pallas as pl
from jax.experimental.pallas import tpu as pltpu
from jax.sharding import PartitionSpec as P

HDIM = 64
TAPS = 3
SAMPLES = 4
LANES = 128

epsilon = 1e-06
far_below = -1e30

VMEM = pl.BlockSpec(memory_space=pltpu.VMEM)
ANY = pl.BlockSpec(memory_space=pl.ANY)
EDGE_LIMIT = 60


def limit(mib):
    return pltpu.CompilerParams(vmem_limit_bytes=mib << 20)


def slot_of(route_row, bags, cap, stride):
    tokens = route_row.shape[1]
    bag_ids = lax.broadcasted_iota(jnp.int32, (bags, tokens), 0)
    onehot = (bag_ids == route_row).astype(jnp.float32)
    before = (
        lax.broadcasted_iota(jnp.int32, (tokens, tokens), 0)
        < lax.broadcasted_iota(jnp.int32, (tokens, tokens), 1)
    )
    earlier = jnp.dot(
        onehot.astype(jnp.bfloat16),
        before.astype(jnp.float32).astype(jnp.bfloat16),
        preferred_element_type=jnp.float32,
    )
    rank = jnp.sum(earlier * onehot, axis=0, keepdims=True).astype(jnp.int32)
    return route_row * stride + rank


def onehot_of(slot, slots):
    slot_ids = lax.broadcasted_iota(jnp.int32, (slots, slot.shape[1]), 0)
    return (slot_ids == slot).astype(jnp.float32).astype(jnp.bfloat16)


def combine(products, rows, cols):
    chans = products[0].shape[1]
    blank = jnp.zeros((cols, chans), jnp.float32)
    area = rows * cols
    column = lax.broadcasted_iota(jnp.int32, (area, chans), 0) % cols
    total = None
    for e in range(TAPS):
        up, mid, down = products[e], products[TAPS + e], products[2 * TAPS + e]
        merged = (
            mid
            + jnp.concatenate([blank, up[: area - cols]], axis=0)
            + jnp.concatenate([down[cols:], blank], axis=0)
        )
        if e == 0:
            merged = jnp.where(column == 0, 0.0, pltpu.roll(merged, 1, axis=0))
        elif e == 2:
            merged = jnp.where(column == cols - 1, 0.0, pltpu.roll(merged, area - 1, axis=0))
        total = merged if total is None else total + merged
    return total


def plane_products(pieces, w_ref):
    plane = TAPS * TAPS
    chans = w_ref.shape[2]
    stacked = pieces[0][1] if len(pieces) == 1 else jnp.concatenate([x for _, x in pieces], axis=1)
    products = []
    for p in range(0, plane, 2):
        pair = []
        for q in range(p, min(p + 2, plane)):
            taps = [w_ref[plane * t + q] for t, _ in pieces]
            pair.append(taps[0] if len(taps) == 1 else jnp.concatenate(taps, axis=0))
        weight = pair[0] if len(pair) == 1 else jnp.concatenate(pair, axis=1)
        value = jnp.dot(stacked, weight, preferred_element_type=jnp.float32)
        for q in range(len(pair)):
            products.append(value[:, q * chans : (q + 1) * chans])
    return products


def scalar_of(ref):
    return jnp.max(ref[...])


def edge_kernel(rows, cols, frames, x_hbm, w_hbm, near_ref, far_ref, x_ref, w_ref, sems):
    area = rows * cols
    plane = TAPS * TAPS
    jobs = ((frames - 1, 0), (0, 2))
    loads = []
    for i, (f, tap) in enumerate(jobs):
        group = [
            pltpu.make_async_copy(
                x_hbm.at[pl.ds(f * area, area)], x_ref.at[pl.ds(i * area, area)], sems.at[i, TAPS]
            )
        ]
        for row in range(TAPS):
            group.append(
                pltpu.make_async_copy(
                    w_hbm.at[pl.ds(tap * plane + row * TAPS, TAPS)],
                    w_ref.at[pl.ds(i * plane + row * TAPS, TAPS)],
                    sems.at[i, row],
                )
            )
        loads.append(group)
    for group in loads:
        for load in group:
            load.start()
    even = lax.axis_index("head") % 2 == 0
    sums = []
    for i in range(2):
        for load in loads[i]:
            load.wait()
        value = x_ref[i * area : (i + 1) * area, :]
        sums.append(combine(plane_products([(i, value)], w_ref), rows, cols))
    up, down = sums
    near_ref[...] = jnp.where(even, up, down)
    far_ref[...] = jnp.where(even, down, up)


def own_kernel(bags, cap, rows, cols, frames, count_ref, x_ref, w_ref, route_ref, acc_ref, onehot_ref):
    count = scalar_of(count_ref)
    place = lax.axis_index("head")
    area = rows * cols
    first = place * frames
    inputs = []
    for f in range(frames):
        value = x_ref[f * area : (f + 1) * area, :]
        inputs.append(jnp.where(first + f < count, value, jnp.zeros_like(value)))
    for f in range(frames):
        pieces = [(t, inputs[f + t - 1]) for t in range(TAPS) if 0 <= f + t - 1 < frames]
        acc_ref[f * area : (f + 1) * area, :] = combine(plane_products(pieces, w_ref), rows, cols)
    route_row = route_ref[pl.ds(place, 1), :]
    onehot_ref[...] = onehot_of(slot_of(route_row, bags, cap, cap), bags * cap)


def join_kernel(
    rows, cols, frames, count_ref, sample_ref, acc_ref, near_ref, far_ref, onehot_ref, e_ref, out_ref, grid_ref
):
    count = scalar_of(count_ref)
    sample = scalar_of(sample_ref)
    area = rows * cols
    place = lax.axis_index("head")
    even = place % 2 == 0
    first = place * frames
    chans = acc_ref.shape[1]
    near, far = near_ref[...], far_ref[...]
    for f in range(frames):
        part = acc_ref[f * area : (f + 1) * area, :]
        if f == 0:
            before = jnp.logical_and(first > 0, first - 1 < count)
            part = part + jnp.where(before, jnp.where(even, far, near), 0.0)
        if f == frames - 1:
            part = part + jnp.where(first + frames < count, jnp.where(even, near, far), 0.0)
        grid_ref[f * area : (f + 1) * area, :] = jnp.where(first + f < count, part, 0.0)
    pieces = [[None] * 2 for _ in range(2)]
    for odd in range(2):
        half = grid_ref[pl.ds(odd, frames * area // 2, stride=2), :]
        half = half.reshape(frames * rows // 2, 2, cols // 2, chans)
        for i in range(2):
            pieces[i][odd] = half[:, i].reshape(frames * area // 4, chans)
    tokens = frames * area // 4
    patches = jnp.concatenate(
        [pieces[0][0], pieces[0][1], pieces[1][0], pieces[1][1]], axis=1
    ).astype(jnp.bfloat16)
    model = e_ref.shape[1]
    col_tile = 256
    total = None
    for n in range(0, model, col_tile):
        part = jnp.dot(patches, e_ref[:, n : n + col_tile], preferred_element_type=jnp.float32)
        squares = part * part
        both = squares[:, :LANES] + squares[:, LANES:]
        total = both if total is None else total + both
    scale = lax.rsqrt(jnp.sum(total, axis=-1, keepdims=True) * (1.0 / model) + epsilon)
    high = scale.astype(jnp.bfloat16).astype(jnp.float32)
    frame = first + lax.broadcasted_iota(jnp.int32, (tokens, LANES), 0) // (area // 4)
    lane = lax.broadcasted_iota(jnp.int32, (tokens, LANES), 1)
    label = jnp.where(frame < count, sample + 1, 0).astype(jnp.float32)
    notes = jnp.where(lane == 0, label, jnp.where(lane == 1, high, jnp.where(lane == 2, scale - high, 0.0)))
    patches = jnp.concatenate([patches, notes.astype(jnp.bfloat16)], axis=1)
    out_ref[...] = jnp.dot(onehot_ref[...], patches, preferred_element_type=jnp.float32).astype(
        jnp.bfloat16
    )


def fold_kernel(e_ref, w_ref, after_ref, fold_ref):
    feats = e_ref.shape[0]
    width = w_ref.shape[2]
    col_tile = 256
    for m in range(3):
        for n in range(0, width, col_tile):
            cols = slice(n, n + col_tile)
            product = jnp.dot(e_ref[...], w_ref[m, :, cols], preferred_element_type=jnp.float32)
            if m == 0:
                product = product * (HDIM ** (-0.5) * math.log2(math.e))
            high = product.astype(jnp.bfloat16)
            fold_ref[m, :feats, cols] = high
            fold_ref[m, feats:, cols] = (product - high.astype(jnp.float32)).astype(jnp.bfloat16)


def qkv_kernel(*refs):
    pieces, fold_ref, out_ref = refs[:-2], refs[-2], refs[-1]
    for m, at, part in qkv_parts(pieces, fold_ref):
        out_ref[m, :, at : at + part.shape[1]] = part


def qkv_parts(pieces, fold_ref):
    feats = pieces[0].shape[1] - LANES
    col_tile = 256
    patch = jnp.concatenate([ref[:, :feats] for ref in pieces], axis=0)
    notes = jnp.concatenate([ref[:, feats:].astype(jnp.float32) for ref in pieces], axis=0)
    scale = jnp.broadcast_to(notes[:, 1:2] + notes[:, 2:3], (notes.shape[0], col_tile))
    twice = jnp.concatenate([patch, patch], axis=1)
    for m in range(3):
        for n in range(0, fold_ref.shape[2], col_tile):
            part = jnp.dot(twice, fold_ref[m, :, n : n + col_tile], preferred_element_type=jnp.float32)
            yield m, n, part * scale


def bag_kernel(clips, cap, masks, groups, *refs):
    count = len(masks)
    pieces, rest = refs[:count], refs[count:]
    early, rest = rest[: len(groups)], rest[len(groups) :]
    fold_ref, out_ref, qkv_ref, note_ref, m_ref, r_ref, order_ref = rest
    place = lax.axis_index("head")
    slots = pieces[0].shape[0]
    feats = pieces[0].shape[1] - LANES
    width = fold_ref.shape[2]
    clip_rows = count * cap
    done = sum(groups)

    def by_clip(values, c):
        return jnp.concatenate(
            [
                value[j * slots + c * cap : j * slots + (c + 1) * cap]
                for value in values
                for j in range(value.shape[0] // slots)
            ],
            axis=0,
        )

    notes = [ref[:, feats:].astype(jnp.float32) for ref in pieces]
    for c in range(clips):
        note = by_clip(notes, c)
        note_ref[c * clip_rows : (c + 1) * clip_rows, :] = note.astype(jnp.bfloat16)
        order_ref[clips + c] = jnp.max(note[:, :1]).astype(jnp.int32)
    starts = [jnp.int32(0)]
    for s in range(SAMPLES):

        def keep_clip(c, at):
            hit = order_ref[clips + c] == s + 1

            @pl.when(hit)
            def _():
                order_ref[at] = c

            return at + hit.astype(jnp.int32)

        starts.append(lax.fori_loop(0, clips, keep_clip, starts[-1]))

    for m, at, part in qkv_parts(pieces[done:], fold_ref):
        cols = slice(at, at + part.shape[1])
        parts = [ref[m, :, cols] for ref in early] + [part]
        for c in range(clips):
            qkv_ref[m, c * clip_rows : (c + 1) * clip_rows, cols] = by_clip(parts, c).astype(jnp.bfloat16)

    out_ref[...] = jnp.zeros_like(out_ref)
    tile = 2 * clip_rows
    lane = lax.broadcasted_iota(jnp.int32, (tile, LANES), 1)
    low = lane < HDIM
    pairs = width // LANES
    ones = jnp.ones((tile, LANES), jnp.bfloat16)
    pick = (lax.broadcasted_iota(jnp.int32, (8, LANES), 1) == 0).astype(jnp.float32).astype(jnp.bfloat16)
    key_at = lax.broadcasted_iota(jnp.int32, (1, tile), 1)

    def two(ref, a, b, *at):
        return jnp.concatenate(
            [
                ref[(*at[:-1], pl.ds(pl.multiple_of(a * clip_rows, 16), clip_rows), at[-1])],
                ref[(*at[:-1], pl.ds(pl.multiple_of(b * clip_rows, 16), clip_rows), at[-1])],
            ],
            axis=0,
        )

    for s in range(SAMPLES):
        begin, size = starts[s], starts[s + 1] - starts[s]
        tiles = (size + 1) // 2

        def members(i):
            second = 2 * i + 1 < size
            return (
                order_ref[begin + 2 * i],
                order_ref[begin + 2 * i + second.astype(jnp.int32)],
                second,
            )

        def bias_of(a, b, second):
            label = lax.dot_general(
                pick,
                two(note_ref, a, b, slice(0, LANES)),
                (((1,), (1,)), ((), ())),
                preferred_element_type=jnp.float32,
            )[:1]
            limit = jnp.where(second, tile, clip_rows)
            good = jnp.logical_and(label == s + 1.0, key_at < limit)
            return jnp.where(good, 0.0, far_below)

        def stacked(pair, a, b):
            query = two(qkv_ref, a, b, 0, slice(pair * LANES, (pair + 1) * LANES))
            blank = jnp.zeros_like(query)
            return jnp.concatenate([jnp.where(low, query, blank), jnp.where(low, blank, query)], axis=0)

        def scores_of(pair, query, a, b, bias):
            keys = two(qkv_ref, a, b, 1, slice(pair * LANES, (pair + 1) * LANES))
            return (
                lax.dot_general(query, keys, (((1,), (1,)), ((), ())), preferred_element_type=jnp.float32)
                + bias
            )

        def mix(pair, shifted, a, b):
            cols = slice(pair * LANES, (pair + 1) * LANES)
            values = jnp.concatenate([two(qkv_ref, a, b, 2, cols), ones], axis=1)
            return jnp.dot(shifted.astype(jnp.bfloat16), values, preferred_element_type=jnp.float32)

        def store(pair, a, b, result):
            cols = slice(pair * LANES, (pair + 1) * LANES)
            shares = result[:, :LANES] / result[:, LANES:]
            mixed = jnp.where(low, shares[:tile], shares[tile:])
            for at, clip in ((clip_rows, b), (0, a)):
                for j, mask in enumerate(masks):
                    piece = mixed[at + j * cap : at + (j + 1) * cap]
                    out_ref[jnp.bitwise_xor(place, mask) * clips + clip, :, cols] = piece.astype(jnp.bfloat16)

        def query_tile(i, carry):
            qa, qb, _ = members(i)

            @pl.when(tiles == 1)
            def _():
                ka, kb, second = members(0)
                bias = bias_of(ka, kb, second)
                for pair in range(pairs):
                    scores = scores_of(pair, stacked(pair, qa, qb), ka, kb, bias)
                    top = jnp.max(scores, axis=-1, keepdims=True)
                    store(pair, qa, qb, mix(pair, jnp.exp2(scores - top), ka, kb))

            @pl.when(tiles > 1)
            def _():
                for pair in range(pairs):
                    m_ref[pair] = jnp.full((2 * tile, LANES), far_below, jnp.float32)
                    r_ref[pair] = jnp.zeros((2 * tile, 2 * LANES), jnp.float32)

                def key_tile(j, inner):
                    ka, kb, second = members(j)
                    bias = bias_of(ka, kb, second)
                    for pair in range(pairs):
                        scores = scores_of(pair, stacked(pair, qa, qb), ka, kb, bias)
                        old = m_ref[pair][:, :1]
                        top = jnp.maximum(old, jnp.max(scores, axis=-1, keepdims=True))
                        r_ref[pair] = r_ref[pair] * jnp.exp2(old - top) + mix(
                            pair, jnp.exp2(scores - top), ka, kb
                        )
                        m_ref[pair] = jnp.broadcast_to(top, (2 * tile, LANES))
                    return inner

                lax.fori_loop(0, tiles, key_tile, 0)
                for pair in range(pairs):
                    store(pair, qa, qb, r_ref[pair])

            return carry

        lax.fori_loop(0, tiles, query_tile, 0)


def collect_kernel(frames, heads, count_ref, onehot_ref, recv_ref, out_ref):
    count = scalar_of(count_ref)
    place = lax.axis_index("head")
    slots, tokens = onehot_ref.shape
    frame = place * frames + lax.broadcasted_iota(jnp.int32, (slots, tokens), 1) // (tokens // frames)
    onehot = jnp.where(frame < count, onehot_ref[...].astype(jnp.float32), 0.0).T.astype(jnp.bfloat16)
    width = recv_ref.shape[1]
    for h in range(heads):
        picked = jnp.dot(
            onehot, recv_ref[h * slots : (h + 1) * slots, :], preferred_element_type=jnp.float32
        )
        out_ref[:, h * width : (h + 1) * width] = picked.astype(jnp.bfloat16)


def shards(latents, frame_counts, routes, samples, conv_weight, embed_weight, qkv_weight):
    frames_dev, rows, cols, depth = latents.shape[1:]
    heads_dev = lax.axis_size("head")
    bags = lax.axis_size("bag")
    area = rows * cols
    tok_dev = frames_dev * area // 4
    cap = 3 * tok_dev // (2 * bags)
    slots = bags * cap
    local_width = qkv_weight.shape[2]
    chans = conv_weight.shape[2]

    tile = latents.reshape(frames_dev * area, depth)
    count = frame_counts
    edge = jax.ShapeDtypeStruct((area, chans), jnp.float32)
    near, far = pl.pallas_call(
        functools.partial(edge_kernel, rows, cols, frames_dev),
        out_shape=(edge, edge),
        in_specs=[ANY, ANY],
        out_specs=(VMEM, VMEM),
        scratch_shapes=[
            pltpu.VMEM((2 * area, depth), jnp.bfloat16),
            pltpu.VMEM((2 * TAPS * TAPS, depth, chans), jnp.bfloat16),
            pltpu.SemaphoreType.DMA((2, TAPS + 1)),
        ],
        compiler_params=limit(EDGE_LIMIT),
        cost_estimate=pl.CostEstimate(flops=600000000, bytes_accessed=4500000, transcendentals=0),
        name="edge",
    )(tile, conv_weight)
    across = [(i, i + 1) for i in range(1, heads_dev - 1, 2)]
    far = lax.ppermute(far, "head", across + [(j, i) for i, j in across])
    near = lax.ppermute(near, "head", [(i, i ^ 1) for i in range(heads_dev)])

    route_rows = routes[:, 0].reshape(heads_dev, tok_dev)
    row_width = 4 * chans + LANES
    acc, onehot = pl.pallas_call(
        functools.partial(own_kernel, bags, cap, rows, cols, frames_dev),
        out_shape=(
            jax.ShapeDtypeStruct((frames_dev * area, chans), jnp.float32),
            jax.ShapeDtypeStruct((slots, tok_dev), jnp.bfloat16),
        ),
        in_specs=[VMEM, VMEM, VMEM, VMEM],
        out_specs=(VMEM, VMEM),
        compiler_params=limit(16),
        cost_estimate=pl.CostEstimate(flops=4000000000, bytes_accessed=4500000, transcendentals=0),
        name="own",
    )(count, tile, conv_weight, route_rows)
    outgoing = pl.pallas_call(
        functools.partial(join_kernel, rows, cols, frames_dev),
        out_shape=jax.ShapeDtypeStruct((slots, row_width), jnp.bfloat16),
        in_specs=[VMEM] * 7,
        out_specs=VMEM,
        scratch_shapes=[pltpu.VMEM((frames_dev * area + 8, chans), jnp.float32)],
        compiler_params=limit(16),
        cost_estimate=pl.CostEstimate(flops=300000000, bytes_accessed=3000000, transcendentals=0),
        name="join",
    )(count, samples.reshape(heads_dev, tok_dev), acc, near, far, onehot, embed_weight)

    arrived = lax.all_to_all(
        outgoing.reshape(bags, cap, row_width), "bag", split_axis=0, concat_axis=0, tiled=True
    )
    arrived = arrived.reshape(slots, row_width)
    pieces = {0: arrived}
    bit = heads_dev // 2
    swap = [(i, i ^ bit) for i in range(heads_dev)]
    across = lax.ppermute(arrived, "head", swap)
    folded = pl.pallas_call(
        fold_kernel,
        out_shape=jax.ShapeDtypeStruct((3, 2 * embed_weight.shape[0], local_width), jnp.bfloat16),
        in_specs=[VMEM, VMEM, ANY],
        out_specs=VMEM,
        compiler_params=limit(16),
        cost_estimate=pl.CostEstimate(flops=3300000000, bytes_accessed=14000000, transcendentals=0),
        name="fold",
    )(embed_weight, qkv_weight, arrived)
    def spread(start, bits):
        found = dict(start)
        for lower in bits:
            pairs = [(i, i ^ lower) for i in range(heads_dev)]
            found.update({mask | lower: lax.ppermute(piece, "head", pairs) for mask, piece in found.items()})
        return found

    lower_bits = [1 << i for i in reversed(range(bit.bit_length() - 1))]
    close = spread({0: arrived}, lower_bits)

    def project(group, name):
        return pl.pallas_call(
            qkv_kernel,
            out_shape=jax.ShapeDtypeStruct((3, len(group) * slots, local_width), jnp.float32),
            in_specs=[VMEM] * (len(group) + 1),
            out_specs=VMEM,
            compiler_params=limit(16),
            cost_estimate=pl.CostEstimate(
                flops=600000000 * len(group), bytes_accessed=3000000 * len(group), transcendentals=0
            ),
            name=name,
        )(*group, folded)

    near_qkv = project(list(close.values()), "near_qkv")
    across, near_qkv = lax.optimization_barrier((across, near_qkv))
    pieces = dict(close)
    pieces.update(spread({bit: across}, lower_bits))
    across_qkv = project([across], "across_qkv")
    groups = (len(close), 1)
    count_slots = heads_dev * slots
    masks = tuple(pieces)

    pair_rows = 2 * heads_dev * cap
    attended = pl.pallas_call(
        functools.partial(bag_kernel, bags, cap, masks, groups),
        out_shape=jax.ShapeDtypeStruct((heads_dev * bags, cap, local_width), jnp.bfloat16),
        in_specs=[VMEM] * (len(masks) + 3),
        out_specs=VMEM,
        scratch_shapes=[
            pltpu.VMEM((3, count_slots, local_width), jnp.bfloat16),
            pltpu.VMEM((count_slots, LANES), jnp.bfloat16),
            pltpu.VMEM((local_width // LANES, 2 * pair_rows, LANES), jnp.float32),
            pltpu.VMEM((local_width // LANES, 2 * pair_rows, 2 * LANES), jnp.float32),
            pltpu.SMEM((2 * bags,), jnp.int32),
        ],
        compiler_params=limit(28),
        cost_estimate=pl.CostEstimate(flops=3000000000, bytes_accessed=5000000, transcendentals=1200000),
        name="bag",
    )(*pieces.values(), near_qkv, across_qkv, folded)
    received = lax.all_to_all(attended, ("head", "bag"), split_axis=0, concat_axis=0, tiled=True)
    return pl.pallas_call(
        functools.partial(collect_kernel, frames_dev, heads_dev),
        out_shape=jax.ShapeDtypeStruct((tok_dev, heads_dev * local_width), jnp.bfloat16),
        in_specs=[VMEM, VMEM, VMEM],
        out_specs=VMEM,
        compiler_params=limit(16),
        name="collect",
    )(count, onehot, received.reshape(count_slots, local_width))


def solution(mesh):
    placed = (
        P("bag", "head", None, None, None),
        P("bag"),
        P("bag", None),
        P("bag"),
        P(),
        P(),
        P(None, None, "head"),
    )
    return jax.shard_map(
        shards, mesh=mesh, in_specs=placed, out_specs=P(("bag", "head"), None), check_vma=False
    )
```
